256 devices in a mesh: rx: 32 (over z, x), tb: 8 (over y, core).
Axes of the slice: x: 4, y: 4, z: 8, core: 2. Of those that a mesh axis runs over, the one named last changes fastest.
Arguments:
- raw_samples: bfloat16 [32, 2, 8192], P('rx', None, 'tb'), may hold values from -3.5 to 3.5
- block_scales: float32 [32, 32], P('rx', 'tb'), may hold values from 0.5 to 2
- lag_window_start: int32 [512, 16], P('rx'), may hold values from 0 to 1008
- doppler_window_start: int32 [512, 16], P('rx'), may hold values from 0 to 31
- peak_owner: int32 [512, 16, 1], P(('rx', 'tb')), may hold values from 0 to 31; in each aligned block of 32 rows (0 to 31, 32 to 63, ..., all dimensions but the last counted through in order) at most 2 rows name the same one
- peak_emitter: int32 [512, 16], P(('rx', 'tb')), may hold values from 0 to 3
- gn_steps: int32 [128], P('rx'), may hold values from 3 to 6
- receiver_pos: float32 [3, 32], replicated, may hold values from -4 to 4
- emitter_start: float32 [3, 128], P(None, 'rx'), may hold values from -4 to 4
Outputs:
- ambiguity: float32 [32, 512, 2, 1024], P('tb', 'rx')
- emitter_pos: float32 [3, 128], P(None, 'rx')
- emitter_vel: float32 [3, 128], P(None, 'rx')
- receiver_clock_bias: float32 [32], replicated
The draws below stay inside these ranges and needn't reach their ends.
Inputs may be any that keep to these rules, and one draw needn't show every extreme that they name: `peak_owner`: within the aligned blocks of 32 peaks of one device (consecutive pair slots, peaks in order), no owner is named more than 2 times, and in some block an owner is named exactly 2 times.
All inputs are finite; a program needn't handle non-finite values.
Results may differ from the reference program's by a relative error of at most 0.0037.
Values may be sent and summed in bfloat16 or wider, within the bound.
A program may use at most 128 MiB of HBM per device.

```python
import math
import jax
import jax.numpy as jnp
import numpy as np
from jax import lax

SEG = 256
DOPPLER_BINS = 32
LAG_COUNT = 1024
BLK = 256
PKP = 16
WL = 16
WD = 4
EM_DEV = 4
GN_MAX = 6
RECEIVERS = 32
HALF = 16
PSLOTS = 512
TBLOCKS = 8
SEGB = 4
SAMPLES = 8192
PK_DEV = 32
CAP = 2
EMITTERS = 128
N_RX = 32


def set_ends(result, own_key, smallest, top_value):
    extent = result.shape
    place = [jax.random.randint(jax.random.fold_in(own_key, axis), (), 0, extent[axis]) for axis in range(len(extent))]
    result = result.at[tuple(place)].set(smallest)
    longest = extent.index(max(extent))
    place[longest] = (place[longest] + 1) % extent[longest]
    return result.at[tuple(place)].set(top_value)


def block_scale(stream_key, shape, pieces, smallest, largest):
    def one(dim, blocks):
        draws = jax.random.uniform(jax.random.fold_in(jax.random.fold_in(stream_key, 6), dim), (blocks,), jnp.float32, smallest / len(pieces), largest / len(pieces))
        return jnp.repeat(jnp.exp(draws), shape[dim] // blocks).reshape((-1,) + (1,) * (len(shape) - dim - 1))

    factor_of = one(*pieces[0])
    for cut in pieces[1:]:
        factor_of = factor_of * one(*cut)
    return factor_of


def deal_out(rng, own, number, rows, amount, top, bound, slope):
    sequence = jax.random.permutation(rng, amount)
    heavy_load, common = shares(amount, rows * top, bound, slope, True), shares(amount, rows * top, bound, slope, False)
    places = jnp.arange(amount)

    def named(sizes, turn):
        used = int((sizes > 0).sum())
        fixed = max(1, used // 4)
        shifted = fixed + (places - fixed + turn * (used - fixed)) % max(1, amount - fixed)
        return jnp.zeros((amount,), jnp.int32).at[sequence[jnp.where(places < fixed, places, shifted)]].set(jnp.asarray(sizes, jnp.int32))

    sizes = jnp.where(number % 4 == 0, named(heavy_load, number // 4), named(common, number - number // 4 - 1))
    mixed = jax.random.permutation(jax.random.fold_in(own, 3), amount)
    giver, receiver = mixed[0:amount // 2 * 2:2], mixed[1:amount // 2 * 2:2]
    slack = jnp.minimum(sizes[giver] - 1, bound - sizes[receiver]) // 2
    slack = jnp.where((giver == sequence[0]) | (receiver == sequence[0]) | (sizes[receiver] == 0), 0, jnp.maximum(slack, 0))
    shifted = jax.random.randint(jax.random.fold_in(own, 4), (amount // 2,), 0, 1 << 20) % (slack + 1)
    sizes = sizes.at[giver].add(-shifted).at[receiver].add(shifted)
    labels = jnp.searchsorted(jnp.cumsum(sizes), jnp.arange(rows * top), side="right").astype(jnp.int32)
    grid = labels.reshape(top, rows).T
    grid = grid[jax.random.permutation(jax.random.fold_in(own, 1), rows)]
    turn = jax.random.randint(jax.random.fold_in(own, 2), (rows, 1), 0, top)
    return jnp.take_along_axis(grid, (jnp.arange(top)[None, :] + turn) % top, axis=1)


def shares(count, total, bound, slope, full):
    portions = [(1 << 20) // math.isqrt(standing ** slope) + 1 for standing in range(1, count + 1)]
    largest = bound if full else min(bound, max(-(-total // count), total * portions[0] // sum(portions)))
    least = 1 if total - largest >= count - 1 else 0
    given, surplus = [largest] + [least] * (count - 1), total - largest - least * (count - 1)
    while surplus > 0:
        movable = [i for i in range(1, count) if given[i] < largest] or [i for i in range(1, count) if given[i] < bound]
        mass, left = sum([portions[i] for i in movable]), surplus
        for i in movable:
            addition = min(bound - given[i], max(1, left * portions[i] // mass), surplus)
            given[i] = given[i] + addition
            surplus = surplus - addition
    return np.array(given)


def bell_draw(rng, extent, deviation, bound, shards=(), kind=jnp.bfloat16):
    entries = jax.random.normal(rng, extent, jnp.float32) * deviation
    if len(shards) > 0:
        entries = block_scale(rng, extent, shards, -0.22, 0.18) * entries
    return jnp.clip(entries, min=-bound, max=bound).astype(kind)


def setup_inputs(seed: int = 0) -> dict:
    arg_keys = jax.random.split(jax.random.key(seed), 10)
    raw_samples = bell_draw(arg_keys[0], (RECEIVERS, 2, SAMPLES), 0.5, 3.5, ((0, 32), (2, 8)))
    block_scales = jnp.clip(jnp.exp(math.log(2.0) - 1.3862944 * jax.random.uniform(arg_keys[1], (RECEIVERS, SAMPLES // BLK), jnp.float32) ** block_scale(arg_keys[1], (RECEIVERS, SAMPLES // BLK), ((0, 32), (1, 8)), -0.2, 0.2)), 0.5, 2.0)
    lag_window_start = set_ends(jax.random.randint(arg_keys[2], (PSLOTS, PKP), 0, LAG_COUNT - WL + 1), jax.random.fold_in(arg_keys[2], 1), 0, LAG_COUNT - WL).astype(jnp.int32)
    doppler_window_start = set_ends(jax.random.randint(arg_keys[3], (PSLOTS, PKP), 0, DOPPLER_BINS), jax.random.fold_in(arg_keys[3], 1), 0, DOPPLER_BINS - 1).astype(jnp.int32)
    peak_owner_keys = jax.random.split(jax.random.fold_in(arg_keys[4], 1), PSLOTS * PKP // PK_DEV)
    peak_owner_turns = jax.random.permutation(jax.random.fold_in(arg_keys[4], 3), PSLOTS * PKP // PK_DEV)
    peak_owner = jax.vmap(lambda own, number: deal_out(jax.random.fold_in(arg_keys[4], 2), own, number, PK_DEV, N_RX, 1, CAP, 2))(peak_owner_keys, peak_owner_turns).reshape((PSLOTS, PKP, 1))
    peak_emitter = set_ends(jax.random.randint(arg_keys[5], (PSLOTS, PKP), 0, EM_DEV), jax.random.fold_in(arg_keys[5], 1), 0, EM_DEV - 1).astype(jnp.int32)
    gn_steps = set_ends(jax.random.randint(arg_keys[6], (EMITTERS,), GN_MAX // 2, GN_MAX + 1), jax.random.fold_in(arg_keys[6], 1), GN_MAX // 2, GN_MAX).astype(jnp.int32)
    receiver_pos = jnp.clip(jax.random.uniform(arg_keys[7], (3, RECEIVERS), jnp.float32, -4.0, 4.0), -4.0, 4.0)
    emitter_start = jnp.clip(jax.random.uniform(arg_keys[8], (3, EMITTERS), jnp.float32, -4.0, 4.0) * block_scale(arg_keys[8], (3, EMITTERS), ((1, 32),), -0.4, 0.0), -4.0, 4.0)
    return {"raw_samples": raw_samples, "block_scales": block_scales, "lag_window_start": lag_window_start, "doppler_window_start": doppler_window_start, "peak_owner": peak_owner, "peak_emitter": peak_emitter, "gn_steps": gn_steps, "receiver_pos": receiver_pos, "emitter_start": emitter_start}


highest = lax.Precision.HIGHEST
two_pi = 2.0 * math.pi
damping = 2.0
delay_extent = 16.0
doppler_extent = 4.0

def angle_table(row_count, col_count, length):
    index_grid = jnp.arange(row_count, dtype=jnp.int32)[:, None] * jnp.arange(col_count, dtype=jnp.int32)[None, :] % length
    phase_grid = index_grid.astype(jnp.float32) * (two_pi / length)
    return (jnp.cos(phase_grid), jnp.sin(phase_grid))

def pick_windows(surface, dop_start, lag_start):
    slot_count = surface.shape[1]
    dop_index = (dop_start[:, :, None, None] + jnp.arange(WD, dtype=jnp.int32)[:, None]) % surface.shape[0]
    lag_index = lag_start[:, :, None, None] + jnp.arange(WL, dtype=jnp.int32)[None, :]
    slot_index = jnp.arange(slot_count, dtype=jnp.int32)[:, None, None, None]
    picked = surface[dop_index, slot_index, :, lag_index]
    return picked.reshape(slot_count, dop_start.shape[1], WD * WL * 2)

def solve_three(normals, damp_term):
    entry_xx = normals[0] + damp_term
    entry_xy = normals[1]
    entry_xz = normals[2]
    entry_yy = normals[3] + damp_term
    entry_yz = normals[4]
    entry_zz = normals[5] + damp_term
    minor_xx = entry_yy * entry_zz - entry_yz * entry_yz
    minor_xy = entry_xz * entry_yz - entry_xy * entry_zz
    minor_xz = entry_xy * entry_yz - entry_xz * entry_yy
    minor_yy = entry_xx * entry_zz - entry_xz * entry_xz
    minor_yz = entry_xy * entry_xz - entry_xx * entry_yz
    minor_zz = entry_xx * entry_yy - entry_xy * entry_xy
    determinant = entry_xx * minor_xx + entry_xy * minor_xy + entry_xz * minor_xz
    step_x = minor_xx * normals[6] + minor_xy * normals[7] + minor_xz * normals[8]
    step_y = minor_xy * normals[6] + minor_yy * normals[7] + minor_yz * normals[8]
    step_z = minor_xz * normals[6] + minor_yz * normals[7] + minor_zz * normals[8]
    return jnp.stack([step_x, step_y, step_z]) / determinant

def normal_rows(sensitivity_matrix, misfit_vector):
    return [sensitivity_matrix[0] * sensitivity_matrix[0], sensitivity_matrix[0] * sensitivity_matrix[1], sensitivity_matrix[0] * sensitivity_matrix[2], sensitivity_matrix[1] * sensitivity_matrix[1], sensitivity_matrix[1] * sensitivity_matrix[2], sensitivity_matrix[2] * sensitivity_matrix[2], sensitivity_matrix[0] * misfit_vector, sensitivity_matrix[1] * misfit_vector, sensitivity_matrix[2] * misfit_vector]

def reference(raw_samples, block_scales, lag_window_start, doppler_window_start, peak_owner, peak_emitter, gn_steps, receiver_pos, emitter_start):
    length = SEG + LAG_COUNT
    signal = raw_samples.astype(jnp.float32) * jnp.repeat(block_scales, BLK, axis=1)[:, None, :]
    complex_sig = signal[:, 0] + 1j * signal[:, 1]
    padded = jnp.concatenate([complex_sig, jnp.zeros((RECEIVERS, LAG_COUNT), complex_sig.dtype)], axis=1)
    near_spec = jnp.fft.fft(complex_sig.reshape(RECEIVERS, DOPPLER_BINS, SEG), n=length, axis=-1)
    starts = jnp.arange(DOPPLER_BINS, dtype=jnp.int32)[:, None] * SEG + jnp.arange(length, dtype=jnp.int32)[None, :]
    far_spec = jnp.fft.fft(padded[:, starts], axis=-1)
    slot_ids = jnp.arange(PSLOTS, dtype=jnp.int32)
    first_recv = slot_ids // HALF
    second_recv = (first_recv + slot_ids % HALF + 1) % RECEIVERS
    near_pair = near_spec[first_recv]
    far_pair = jnp.conj(far_spec[second_recv])
    seg_ids = jnp.arange(DOPPLER_BINS, dtype=jnp.int32)
    mix_phase = (seg_ids[:, None] * seg_ids[None, :] % DOPPLER_BINS).astype(jnp.float32) * (two_pi / DOPPLER_BINS)
    mix_weight = jnp.cos(mix_phase) - 1j * jnp.sin(mix_phase)
    total_real = jnp.zeros((DOPPLER_BINS, PSLOTS, length), jnp.float32)
    total_imag = jnp.zeros((DOPPLER_BINS, PSLOTS, length), jnp.float32)
    for block_id in range(TBLOCKS):
        seg_lower = block_id * SEGB
        seg_upper = seg_lower + SEGB
        mixed_spec = jnp.einsum('dm,qmf->dqf', mix_weight[:, seg_lower:seg_upper], near_pair[:, seg_lower:seg_upper] * far_pair[:, seg_lower:seg_upper], precision=highest)
        part_real = lax.optimization_barrier(jnp.real(mixed_spec).astype(jnp.bfloat16))
        part_imag = lax.optimization_barrier(jnp.imag(mixed_spec).astype(jnp.bfloat16))
        total_real = total_real + part_real.astype(jnp.float32)
        total_imag = total_imag + part_imag.astype(jnp.float32)
    cosine, sine_part = angle_table(length, LAG_COUNT, length)
    coeff_bf = lax.optimization_barrier(jnp.concatenate([cosine, sine_part], axis=1).astype(jnp.bfloat16))
    lag_coeff = coeff_bf.astype(jnp.float32)
    stacked = jnp.stack([total_real, total_imag], axis=2).reshape(DOPPLER_BINS * PSLOTS * 2, length)
    product = jnp.dot(stacked, lag_coeff, precision=highest).reshape(DOPPLER_BINS, PSLOTS, 2, 2 * LAG_COUNT)
    surface = jnp.stack([product[:, :, 0, :LAG_COUNT] + product[:, :, 1, LAG_COUNT:], product[:, :, 1, :LAG_COUNT] - product[:, :, 0, LAG_COUNT:]], axis=2) * (1.0 / length)
    ambiguity = surface * (1.0 / math.sqrt(SAMPLES))
    windows = pick_windows(surface, doppler_window_start, lag_window_start)
    window_five = windows.reshape(PSLOTS, PKP, WD, WL, 2)
    window_power = lax.optimization_barrier(jnp.sum(window_five * window_five, axis=4)) * (1.0 / SAMPLES)
    total_power = lax.optimization_barrier(jnp.mean(window_power, axis=(2, 3))) + 1e-06
    lag_average = lax.optimization_barrier(jnp.mean(window_power * jnp.arange(WL, dtype=jnp.float32), axis=(2, 3))) / total_power
    doppler_average = lax.optimization_barrier(jnp.mean(window_power * jnp.arange(WD, dtype=jnp.float32)[:, None], axis=(2, 3))) / total_power
    measured_delay = ((lag_window_start.astype(jnp.float32) + lag_average) * (delay_extent / LAG_COUNT)).reshape(-1)
    measured_doppler = ((doppler_window_start.astype(jnp.float32) + doppler_average) * (doppler_extent / DOPPLER_BINS)).reshape(-1)
    emitter_index = (peak_owner[:, :, 0] * EM_DEV + peak_emitter).reshape(-1)
    leading_peak = jnp.broadcast_to(first_recv[:, None], (PSLOTS, PKP)).reshape(-1)
    trailing_peak = jnp.broadcast_to(second_recv[:, None], (PSLOTS, PKP)).reshape(-1)

    def ranges(position):
        at_peak = position[:, emitter_index]
        diff_first = at_peak - receiver_pos[:, leading_peak]
        diff_second = at_peak - receiver_pos[:, trailing_peak]
        range_first = jnp.sqrt(lax.optimization_barrier(jnp.sum(diff_first * diff_first, axis=0)) + 1.0)
        range_second = jnp.sqrt(lax.optimization_barrier(jnp.sum(diff_second * diff_second, axis=0)) + 1.0)
        return (range_second - range_first, diff_second / range_second - diff_first / range_first)
    position = emitter_start
    emitter_speed = jnp.zeros((3, EMITTERS), jnp.float32)
    receiver_clock_bias = jnp.zeros((RECEIVERS,), jnp.float32)
    for gn_step in range(GN_MAX):
        peak_dispersion, sensitivity_matrix = ranges(position)
        misfit_vector = measured_delay - peak_dispersion - receiver_clock_bias[trailing_peak] + receiver_clock_bias[leading_peak]
        stacked_rows = jnp.stack(normal_rows(sensitivity_matrix, misfit_vector) + [jnp.ones_like(misfit_vector)])
        pos_normals = jax.ops.segment_sum(stacked_rows.T, emitter_index, num_segments=EMITTERS).T
        damp_term = damping * (pos_normals[9] + 1.0)
        still_moving = (gn_step < gn_steps)[None, :]
        position = position + jnp.where(still_moving, solve_three(pos_normals, damp_term), 0.0)
        peak_dispersion, sensitivity_matrix = ranges(position)
        velocity_misfit = measured_doppler - lax.optimization_barrier(jnp.sum(emitter_speed[:, emitter_index] * sensitivity_matrix, axis=0))
        vel_normals = jax.ops.segment_sum(jnp.stack(normal_rows(sensitivity_matrix, velocity_misfit)).T, emitter_index, num_segments=EMITTERS).T
        clock_misfit = measured_delay - peak_dispersion - receiver_clock_bias[trailing_peak] + receiver_clock_bias[leading_peak]
        clock_total = jax.ops.segment_sum(clock_misfit, trailing_peak, num_segments=RECEIVERS) - jax.ops.segment_sum(clock_misfit, leading_peak, num_segments=RECEIVERS)
        emitter_speed = emitter_speed + jnp.where(still_moving, solve_three(vel_normals, damp_term), 0.0)
        receiver_clock_bias = receiver_clock_bias + clock_total / ((1.0 + damping) * PKP * RECEIVERS)
    return (ambiguity, position, emitter_speed, receiver_clock_bias)
```

```python
import functools
import math

import jax
import jax.numpy as jnp
import numpy as np
from jax import lax
from jax.experimental import pallas as pl
from jax.experimental.pallas import tpu as pltpu
from jax.sharding import PartitionSpec as P

SEG = 256
DOPPLER_BINS = 32
LAG_COUNT = 1024
WL = 16
WD = 4
GN_MAX = 6
RX = 32
TB = 8
FFT = 512
SAMPLES = SEG * DOPPLER_BINS

MESH = pl.DeviceIdType.MESH
f32 = jnp.float32
bf16 = jnp.bfloat16
highest = lax.Precision.HIGHEST


def split_pair(table):
    high = table.astype(bf16)
    low = (table - high.astype(np.float64)).astype(bf16)
    return high, low


def tables():
    turn = 2.0 * np.pi / FFT
    t_f = np.arange(SEG)[:, None] * np.arange(FFT)[None, :] % FFT * turn
    forward = np.concatenate([np.cos(t_f), np.sin(t_f)], axis=1)
    backward = np.concatenate([np.cos(t_f.T), np.sin(t_f.T)], axis=1)
    d_m = (
        np.arange(DOPPLER_BINS)[:, None] * np.arange(DOPPLER_BINS)[None, :] % DOPPLER_BINS
    ) * (2.0 * np.pi / DOPPLER_BINS)
    mix = np.block([[np.cos(d_m), np.sin(d_m)], [-np.sin(d_m), np.cos(d_m)]])
    mix = mix / (FFT * math.sqrt(SAMPLES))
    return split_pair(forward) + split_pair(backward) + (mix.astype(np.float32),)


def gather_kernel(raw, scl, raw_all, scl_all, send_a, recv_a, send_b, recv_b, own_sem):
    r = lax.axis_index("rx")
    b = lax.axis_index("tb")
    barrier = pltpu.get_barrier_semaphore()
    targets = []
    for d in range(1, TB):
        peer = lax.rem(b + d, TB)
        pl.semaphore_signal(barrier, inc=1, device_id={"rx": r, "tb": peer}, device_id_type=MESH)
        targets.append((r, peer, 0))
    for i in (1, 2):
        source = lax.rem(r + 2 * b + i, RX)
        for t in range(TB):
            pl.semaphore_signal(
                barrier, inc=1, device_id={"rx": source, "tb": t}, device_id_type=MESH
            )
            targets.append((lax.rem(r + RX - 2 * t - i, RX), t, i))
    pl.semaphore_wait(barrier, len(targets))
    own = [
        pltpu.make_async_copy(raw, raw_all.at[b], own_sem.at[0]),
        pltpu.make_async_copy(scl, scl_all.at[b], own_sem.at[1]),
    ]
    sends = []
    for n, (to_r, to_b, i) in enumerate(targets):
        slot = i * TB + b
        for src, dst, ss, rs in (
            (raw, raw_all, send_a, recv_a),
            (scl, scl_all, send_b, recv_b),
        ):
            copy = pltpu.make_async_remote_copy(
                src_ref=src,
                dst_ref=dst.at[slot],
                send_sem=ss.at[n],
                recv_sem=rs.at[slot],
                device_id={"rx": to_r, "tb": to_b},
                device_id_type=MESH,
            )
            copy.start()
            sends.append(copy)
    for copy in own:
        copy.start()
    for copy in own:
        copy.wait()
    arrivals = [lax.rem(b + d, TB) for d in range(1, TB)]
    arrivals += [i * TB + t for i in (1, 2) for t in range(TB)]
    for slot in arrivals:
        for src, dst, rs in ((raw, raw_all, recv_a), (scl, scl_all, recv_b)):
            pltpu.make_async_remote_copy(
                src_ref=src,
                dst_ref=dst.at[slot],
                send_sem=send_a.at[0],
                recv_sem=rs.at[slot],
                device_id={"rx": r, "tb": lax.rem(b + 1, TB)},
                device_id_type=MESH,
            ).wait_recv()
    for copy in sends:
        copy.wait_send()


def gather_samples(raw, scl):
    any_spec = pl.BlockSpec(memory_space=pl.ANY)
    n = 3 * TB - 1
    return pl.pallas_call(
        gather_kernel,
        out_shape=(
            jax.ShapeDtypeStruct((3 * TB,) + raw.shape, raw.dtype),
            jax.ShapeDtypeStruct((3 * TB,) + scl.shape, scl.dtype),
        ),
        in_specs=[any_spec, any_spec],
        out_specs=(any_spec, any_spec),
        scratch_shapes=[
            pltpu.SemaphoreType.DMA((n,)),
            pltpu.SemaphoreType.DMA((3 * TB,)),
            pltpu.SemaphoreType.DMA((n,)),
            pltpu.SemaphoreType.DMA((3 * TB,)),
            pltpu.SemaphoreType.DMA((2,)),
        ],
        compiler_params=pltpu.CompilerParams(collective_id=0, has_side_effects=True),
        name="gather_samples",
    )(raw, scl)


def iota(shape, dim):
    return lax.broadcasted_iota(jnp.int32, shape, dim)


def to_column(row, count):
    eye = iota((count, count), 0) == iota((count, count), 1)
    return jnp.sum(jnp.where(eye, row, 0.0), axis=1, keepdims=True)


def surface_kernel(
    raw_ref, scl_ref, fhi_ref, flo_ref, bhi_ref, blo_ref, mix_ref,
    lag_ref, dop_ref, own_ref, em_ref, start_ref, steps_ref,
    surf_ref, pay_ref, re_ref, im_ref, rr_ref,
):
    raw = raw_ref[...].astype(f32).reshape(3 * TB * 8, SEG).astype(bf16)
    spec = jnp.dot(raw, fhi_ref[...], preferred_element_type=f32)
    spec = spec + jnp.dot(raw, flo_ref[...], preferred_element_type=f32)
    cos_part = spec[:, :FFT].reshape(3 * TB, 8, FFT)
    sin_part = spec[:, FFT:].reshape(3 * TB, 8, FFT)
    sub = iota((1, 8, 1), 1)
    sign = jnp.where(sub < 4, 1.0, -1.0).astype(f32)
    sub_l = iota((1, 8, 128), 1)
    lane_l = iota((1, 8, 128), 2)
    pick = lane_l == lax.rem(sub_l, 4)
    scale = jnp.sum(jnp.where(pick, scl_ref[...], 0.0), axis=2, keepdims=True)
    pieces = (cos_part + sign * pltpu.roll(sin_part, 4, 1)) * scale
    for i in range(3):
        re_ref[i, 32:40, :] = jnp.zeros((8, FFT), f32)
        im_ref[i, 32:40, :] = jnp.zeros((8, FFT), f32)
        for t in range(TB):
            re_ref[i, 4 * t : 4 * t + 4, :] = pieces[i * TB + t, 0:4, :]
            im_ref[i, 4 * t : 4 * t + 4, :] = pieces[i * TB + t, 4:8, :]
    near_re = re_ref[0, 0:32, :]
    near_im = im_ref[0, 0:32, :]
    alt = jnp.where(lax.rem(iota((1, FFT), 1), 2) == 0, 1.0, -1.0).astype(f32)
    for c in range(2):
        for j in range(4):
            far_re = re_ref[c + 1, j : j + 32, :] + alt * re_ref[c + 1, j + 1 : j + 33, :]
            far_im = im_ref[c + 1, j : j + 32, :] + alt * im_ref[c + 1, j + 1 : j + 33, :]
            row = (c * 4 + j) * 32
            rr_ref[row : row + 32, :] = near_re * far_re + near_im * far_im
            rr_ref[256 + row : 288 + row, :] = near_im * far_re - near_re * far_im
    cross = rr_ref[...]
    high = cross.astype(bf16)
    low = (cross - high.astype(f32)).astype(bf16)
    lagged = jnp.dot(high, bhi_ref[...], preferred_element_type=f32)
    lagged = lagged + jnp.dot(low, bhi_ref[...], preferred_element_type=f32)
    lagged = lagged + jnp.dot(high, blo_ref[...], preferred_element_type=f32)
    lag_re = lagged[0:256, 0:256] + lagged[256:512, 256:512]
    lag_im = lagged[256:512, 0:256] - lagged[0:256, 256:512]

    b = lax.axis_index("tb")
    r = lax.axis_index("rx")
    lag_rows = lag_ref[pl.ds(2 * b, 2), :].astype(f32)
    dop_rows = dop_ref[pl.ds(2 * b, 2), :].astype(f32)
    tau_cols, nu_cols, own_cols, em_cols = [], [], [], []
    for c in range(2):
        top = jnp.concatenate(
            [lag_re[(c * 4 + j) * 32 : (c * 4 + j + 1) * 32] for j in range(4)], axis=1
        )
        low_half = jnp.concatenate(
            [lag_im[(c * 4 + j) * 32 : (c * 4 + j + 1) * 32] for j in range(4)], axis=1
        )
        stacked = jnp.concatenate([top, low_half], axis=0)
        surf = jnp.dot(mix_ref[...], stacked, precision=highest, preferred_element_type=f32)
        for comp in range(2):
            for lt in range(8):
                surf_ref[pl.ds(c * 16 + lt * 2 + comp, 32, stride=32), :] = surf[
                    comp * 32 : comp * 32 + 32, lt * 128 : lt * 128 + 128
                ]
        power = surf[0:32] * surf[0:32] + surf[32:64] * surf[32:64]
        lag0 = to_column(lag_rows[c : c + 1, :], 16)
        dop0 = to_column(dop_rows[c : c + 1, :], 16)
        d_id = iota((16, DOPPLER_BINS), 1).astype(f32)
        offset = d_id - dop0
        offset = jnp.where(offset < 0.0, offset + DOPPLER_BINS, offset)
        inside = jnp.where(offset < WD, 1.0, 0.0).astype(f32)
        weights = jnp.concatenate([inside, inside * offset], axis=0)
        rows = jnp.dot(weights, power, precision=highest, preferred_element_type=f32)
        step = iota((16, LAG_COUNT), 1).astype(f32) - lag0
        within = (step >= 0.0) & (step < WL)
        plain = jnp.where(within, rows[0:16], 0.0)
        norm = 1.0 / (WL * WD)
        total = jnp.sum(plain, axis=1, keepdims=True) * norm + 1e-06
        lag_mean = jnp.sum(plain * step, axis=1, keepdims=True) * norm / total
        dop_mean = jnp.sum(jnp.where(within, rows[16:32], 0.0), axis=1, keepdims=True) * norm / total
        tau_cols.append((lag0 + lag_mean) * (16.0 / LAG_COUNT))
        nu_cols.append((dop0 + dop_mean) * (4.0 / DOPPLER_BINS))
        own_cols.append(to_column(own_ref[c : c + 1, :].astype(f32), 16))
        em_cols.append(to_column(em_ref[c : c + 1, :].astype(f32), 16) + (1.0 + 4.0 * c))
    tau = jnp.concatenate(tau_cols, axis=0)
    nu = jnp.concatenate(nu_cols, axis=0)
    owner = jnp.concatenate(own_cols, axis=0)
    code = jnp.concatenate(em_cols, axis=0)
    p_row = iota((32, 32), 0)
    p_col = iota((32, 32), 1)
    owner_row = jnp.sum(jnp.where(p_row == p_col, owner, 0.0), axis=0, keepdims=True)
    same = (owner_row == owner) & (p_col < p_row)
    rank = jnp.sum(jnp.where(same, 1.0, 0.0), axis=1, keepdims=True)
    lane = iota((32, 128), 1)
    slot = lax.rem(lane, 64).astype(f32)
    placed = (rank * 32.0 + owner) == slot
    first = lane < 64
    pay_ref[0] = jnp.sum(
        jnp.where(placed, jnp.where(first, tau, nu), 0.0), axis=0, keepdims=True
    )
    codes = jnp.sum(jnp.where(placed & first, code, 0.0), axis=0, keepdims=True)
    lane1 = iota((1, 128), 1)
    for k in range(3):
        for e in range(4):
            codes = jnp.where(lane1 == 64 + 4 * k + e, start_ref[k : k + 1, e : e + 1], codes)
    for e in range(4):
        codes = jnp.where(lane1 == 76 + e, steps_ref[0:1, e : e + 1].astype(f32), codes)
    pay_ref[1] = codes


def surfaces(raw_all, scl_all, lag, dop, own, em, start, steps, consts):
    vmem = pl.BlockSpec(memory_space=pltpu.VMEM)
    return pl.pallas_call(
        surface_kernel,
        out_shape=(
            jax.ShapeDtypeStruct((1024, 128), f32),
            jax.ShapeDtypeStruct((2, 1, 128), f32),
        ),
        in_specs=[vmem] * 13,
        out_specs=(vmem, vmem),
        scratch_shapes=[
            pltpu.VMEM((3, 40, FFT), f32),
            pltpu.VMEM((3, 40, FFT), f32),
            pltpu.VMEM((512, FFT), f32),
        ],
        name="surfaces",
    )(raw_all, scl_all, *consts, lag, dop, own, em, start, steps)


def exchange_kernel(surf, pay, amb, table, send_p, recv_p, send_s, recv_s, send_t, recv_t, own_sem):
    r = lax.axis_index("rx")
    b = lax.axis_index("tb")
    barrier = pltpu.get_barrier_semaphore()
    for d in range(1, RX):
        pl.semaphore_signal(
            barrier,
            inc=1,
            device_id={"rx": lax.rem(r + d, RX), "tb": b},
            device_id_type=MESH,
        )
    for d in range(1, TB):
        pl.semaphore_signal(
            barrier,
            inc=1,
            device_id={"rx": r, "tb": lax.rem(b + d, TB)},
            device_id_type=MESH,
        )
    pl.semaphore_wait(barrier, RX + TB - 2)
    own = [
        pltpu.make_async_copy(pay, table.at[b, :, r], own_sem.at[0]),
        pltpu.make_async_copy(surf.at[b], amb.at[:, b], own_sem.at[1]),
    ]
    own[0].start()
    first, second, third = [], [], []
    for d in range(1, RX):
        copy = pltpu.make_async_remote_copy(
            src_ref=pay,
            dst_ref=table.at[b, :, r],
            send_sem=send_p.at[d - 1],
            recv_sem=recv_p.at[d - 1],
            device_id={"rx": lax.rem(r + d, RX), "tb": b},
            device_id_type=MESH,
        )
        copy.start()
        first.append(copy)
    for d in range(1, TB):
        peer = lax.rem(b + d, TB)
        copy = pltpu.make_async_remote_copy(
            src_ref=surf.at[peer],
            dst_ref=amb.at[:, b],
            send_sem=send_s.at[d - 1],
            recv_sem=recv_s.at[d - 1],
            device_id={"rx": r, "tb": peer},
            device_id_type=MESH,
        )
        copy.start()
        second.append(copy)
    own[1].start()
    own[0].wait()
    for d in range(1, RX):
        source = lax.rem(r + RX - d, RX)
        pltpu.make_async_remote_copy(
            src_ref=pay,
            dst_ref=table.at[b, :, source],
            send_sem=send_p.at[d - 1],
            recv_sem=recv_p.at[d - 1],
            device_id={"rx": source, "tb": b},
            device_id_type=MESH,
        ).wait_recv()
    for d in range(1, TB):
        copy = pltpu.make_async_remote_copy(
            src_ref=table.at[b],
            dst_ref=table.at[b],
            send_sem=send_t.at[d - 1],
            recv_sem=recv_t.at[d - 1],
            device_id={"rx": r, "tb": lax.rem(b + d, TB)},
            device_id_type=MESH,
        )
        copy.start()
        third.append(copy)
    for d in range(1, TB):
        source = lax.rem(b + TB - d, TB)
        pltpu.make_async_remote_copy(
            src_ref=surf.at[source],
            dst_ref=amb.at[:, source],
            send_sem=send_s.at[d - 1],
            recv_sem=recv_s.at[d - 1],
            device_id={"rx": r, "tb": source},
            device_id_type=MESH,
        ).wait_recv()
        pltpu.make_async_remote_copy(
            src_ref=table.at[source],
            dst_ref=table.at[source],
            send_sem=send_t.at[d - 1],
            recv_sem=recv_t.at[d - 1],
            device_id={"rx": r, "tb": source},
            device_id_type=MESH,
        ).wait_recv()
    for copy in first + second + third:
        copy.wait_send()
    own[1].wait()


def exchange(surf, pay):
    any_spec = pl.BlockSpec(memory_space=pl.ANY)
    vmem = pl.BlockSpec(memory_space=pltpu.VMEM)
    dma = pltpu.SemaphoreType.DMA
    return pl.pallas_call(
        exchange_kernel,
        out_shape=(
            jax.ShapeDtypeStruct((4, TB, 32, 128), f32),
            jax.ShapeDtypeStruct((TB, 2, RX, 1, 128), f32),
        ),
        in_specs=[vmem, vmem],
        out_specs=(any_spec, any_spec),
        scratch_shapes=[
            dma((RX - 1,)), dma((RX - 1,)), dma((TB - 1,)), dma((TB - 1,)),
            dma((TB - 1,)), dma((TB - 1,)), dma((2,)),
        ],
        compiler_params=pltpu.CompilerParams(collective_id=1, has_side_effects=True),
        name="exchange",
    )(surf, pay)


def solve_three(normals, rhs, damp_term):
    entry_xx = normals[0] + damp_term
    entry_xy = normals[1]
    entry_xz = normals[2]
    entry_yy = normals[3] + damp_term
    entry_yz = normals[4]
    entry_zz = normals[5] + damp_term
    minor_xx = entry_yy * entry_zz - entry_yz * entry_yz
    minor_xy = entry_xz * entry_yz - entry_xy * entry_zz
    minor_xz = entry_xy * entry_yz - entry_xz * entry_yy
    minor_yy = entry_xx * entry_zz - entry_xz * entry_xz
    minor_yz = entry_xy * entry_xz - entry_xx * entry_yz
    minor_zz = entry_xx * entry_yy - entry_xy * entry_xy
    inverse = 1.0 / (entry_xx * minor_xx + entry_xy * minor_xy + entry_xz * minor_xz)
    step_x = minor_xx * rhs[0] + minor_xy * rhs[1] + minor_xz * rhs[2]
    step_y = minor_xy * rhs[0] + minor_yy * rhs[1] + minor_yz * rhs[2]
    step_z = minor_xz * rhs[0] + minor_yz * rhs[1] + minor_zz * rhs[2]
    return [step_x * inverse, step_y * inverse, step_z * inverse]


def per_receiver(x, shift):
    return pltpu.roll(x, (RX - shift) % RX, 0)


def solve_kernel(
    table_ref, rpos_ref, pos_ref, vel_ref, bias_ref,
    tau_ref, nu_ref, mask_ref, late_ref, fst_ref, snd_ref, spread_ref, jac_ref,
):
    lane = iota((RX, 128), 1)
    low = lane < 64
    own_lane = iota((RX, 128), 0) == lax.rem(lane, RX)
    halves = []
    for k in range(4):
        a0, a1 = table_ref[k, 0], table_ref[k + 4, 0]
        tau_ref[k] = jnp.where(low, a0, pltpu.roll(a1, 64, 1))
        nu_ref[k] = jnp.where(low, pltpu.roll(a0, 64, 1), a1)
        code = jnp.where(low, table_ref[k, 1], pltpu.roll(table_ref[k + 4, 1], 64, 1))
        late = code > 4.5
        late_ref[k] = jnp.where(late, 1.0, 0.0)
        emitter = jnp.where(late, code - 4.0, code)
        for e in range(4):
            mask_ref[e, k] = jnp.where(emitter == e + 1.0, 1.0, 0.0)

    info = table_ref[0, 1]

    def owner_row(col):
        value = jnp.sum(jnp.where(lane == col, info, 0.0), axis=1, keepdims=True)
        return jnp.sum(jnp.where(own_lane, value, 0.0), axis=0, keepdims=True)

    def owner_rows(base):
        return jnp.concatenate([owner_row(base + e) for e in range(4)], axis=0)

    position = [owner_rows(64 + 4 * k) for k in range(3)]
    steps = owner_rows(76)

    def second_of(x, k):
        late = late_ref[k] > 0.5
        near_half = jnp.where(late, per_receiver(x, 2 * k + 2), per_receiver(x, 2 * k + 1))
        far_half = jnp.where(late, per_receiver(x, 2 * k + 10), per_receiver(x, 2 * k + 9))
        return jnp.where(low, near_half, far_half)

    eye = iota((RX, RX), 0) == iota((RX, RX), 1)
    for comp in range(3):
        column = jnp.sum(
            jnp.where(eye, rpos_ref[comp : comp + 1, :], 0.0), axis=1, keepdims=True
        )
        column = jnp.broadcast_to(column, (RX, 128))
        fst_ref[comp] = column
        for k in range(4):
            snd_ref[comp, k] = second_of(column, k)

    def sum_rows(parts):
        rows = jnp.concatenate([jnp.sum(p, axis=0, keepdims=True) for p in parts], axis=0)
        rows = rows + pltpu.roll(rows, 32, 1)
        return rows + pltpu.roll(rows, 64, 1)

    def add_to(acc, key, k, quantity):
        for e in range(4):
            term = mask_ref[e, k] * quantity
            term = term[0:8] + term[8:16] + term[16:24] + term[24:32]
            acc[key][e] = term if k == 0 else acc[key][e] + term

    def at_peaks(rows, k):
        value = mask_ref[0, k] * rows[0:1]
        for e in range(1, 4):
            value = value + mask_ref[e, k] * rows[e : e + 1]
        return value

    def ranges(position, k):
        sq_first = jnp.ones((RX, 128), f32)
        sq_second = sq_first
        firsts, seconds = [], []
        for comp in range(3):
            at = at_peaks(position[comp], k)
            d_first = at - fst_ref[comp]
            d_second = at - snd_ref[comp, k]
            sq_first = sq_first + d_first * d_first
            sq_second = sq_second + d_second * d_second
            firsts.append(d_first)
            seconds.append(d_second)
        inv_first = lax.rsqrt(sq_first)
        inv_second = lax.rsqrt(sq_second)
        spread = sq_second * inv_second - sq_first * inv_first
        spread_ref[k] = spread
        jac = [seconds[i] * inv_second - firsts[i] * inv_first for i in range(3)]
        for i in range(3):
            jac_ref[i, k] = jac[i]
        return spread, jac

    pairs = ((0, 0), (0, 1), (0, 2), (1, 1), (1, 2), (2, 2))
    acc = {key: [None] * 4 for key in range(7)}
    for k in range(4):
        _, jac = ranges(position, k)
        for key, (x, y) in enumerate(pairs):
            add_to(acc, key, k, jac[x] * jac[y])
        add_to(acc, 6, k, jnp.ones((RX, 128), f32))
    normals = [sum_rows(acc[key]) for key in range(6)]
    damp = 2.0 * (sum_rows(acc[6]) + 1.0)
    zero = jnp.zeros((4, 128), f32)

    def gn_step(step, carry):
        position, speed, bias, normals = carry
        moving = step.astype(f32) < steps
        acc = {key: [None] * 4 for key in range(3)}
        for k in range(4):
            delta = second_of(bias, k) - bias
            resid = tau_ref[k] - spread_ref[k] - delta
            for i in range(3):
                add_to(acc, i, k, jac_ref[i, k] * resid)
        moved = solve_three(normals, [sum_rows(acc[i]) for i in range(3)], damp)
        position = [position[i] + jnp.where(moving, moved[i], 0.0) for i in range(3)]
        acc = {key: [None] * 4 for key in range(9)}
        clock = None
        for k in range(4):
            spread, jac = ranges(position, k)
            for key, (x, y) in enumerate(pairs):
                add_to(acc, key, k, jac[x] * jac[y])
            rate = nu_ref[k]
            for i in range(3):
                rate = rate - at_peaks(speed[i], k) * jac[i]
            for i in range(3):
                add_to(acc, 6 + i, k, jac[i] * rate)
            live = mask_ref[0, k] + mask_ref[1, k] + mask_ref[2, k] + mask_ref[3, k]
            delta = second_of(bias, k) - bias
            cres = live * (tau_ref[k] - spread - delta)
            late = late_ref[k] * cres
            early = cres - late
            part = -cres
            for term, keep, shift in (
                (early, low, 2 * k + 1),
                (late, low, 2 * k + 2),
                (early, jnp.logical_not(low), 2 * k + 9),
                (late, jnp.logical_not(low), 2 * k + 10),
            ):
                part = part + pltpu.roll(jnp.where(keep, term, 0.0), shift, 0)
            clock = part if clock is None else clock + part
        normals = [sum_rows(acc[key]) for key in range(6)]
        turned = solve_three(normals, [sum_rows(acc[6 + i]) for i in range(3)], damp)
        speed = [speed[i] + jnp.where(moving, turned[i], 0.0) for i in range(3)]
        total = jnp.sum(clock, axis=1, keepdims=True)
        bias = bias + jnp.broadcast_to(total, (RX, 128)) / (3.0 * 16 * RX)
        return position, speed, bias, normals

    carry = (position, [zero, zero, zero], jnp.zeros((RX, 128), f32), normals)
    position, speed, bias, _ = lax.fori_loop(0, GN_MAX, gn_step, carry)
    r = lax.axis_index("rx")
    lane4 = iota((4, 128), 1)
    sub4 = iota((4, 128), 0)
    for out, value in ((pos_ref, position), (vel_ref, speed)):
        for i in range(3):
            column = jnp.sum(jnp.where(lane4 == r, value[i], 0.0), axis=1, keepdims=True)
            row = jnp.sum(jnp.where(lane4 == sub4, column, 0.0), axis=0, keepdims=True)
            out[i : i + 1, :] = row[:, 0:4]
    bias_row = jnp.sum(jnp.where(iota((RX, 128), 0) == lane, bias, 0.0), axis=0, keepdims=True)
    bias_ref[...] = bias_row[:, 0:RX]


def solve(table, receiver_pos):
    vmem = pl.BlockSpec(memory_space=pltpu.VMEM)
    block = (4, RX, 128)
    return pl.pallas_call(
        solve_kernel,
        out_shape=(
            jax.ShapeDtypeStruct((3, 4), f32),
            jax.ShapeDtypeStruct((3, 4), f32),
            jax.ShapeDtypeStruct((1, RX), f32),
        ),
        in_specs=[vmem, vmem],
        out_specs=(vmem, vmem, vmem),
        scratch_shapes=[
            pltpu.VMEM(block, f32),
            pltpu.VMEM(block, f32),
            pltpu.VMEM((4,) + block, f32),
            pltpu.VMEM(block, f32),
            pltpu.VMEM((3, RX, 128), f32),
            pltpu.VMEM((3,) + block, f32),
            pltpu.VMEM(block, f32),
            pltpu.VMEM((3,) + block, f32),
        ],
        name="solve",
    )(table, receiver_pos)


def local(
    consts, raw_samples, block_scales, lag_window_start, doppler_window_start,
    peak_owner, peak_emitter, gn_steps, receiver_pos, emitter_start,
):
    raw = raw_samples.reshape(8, SEG)
    scl = jnp.pad(block_scales, ((0, 0), (0, 124)))
    raw_all, scl_all = gather_samples(raw, scl)
    surf, pay = surfaces(
        raw_all, scl_all, lag_window_start, doppler_window_start,
        peak_owner.reshape(2, 16), peak_emitter, emitter_start, gn_steps.reshape(1, 4), consts,
    )
    amb, table = exchange(surf.reshape(TB, 4, 32, 128), pay)
    position, speed, bias = solve(table.reshape(TB, 2, RX, 128), receiver_pos)
    amb = amb.reshape(4, 16, 8, 2, 128).transpose(0, 1, 3, 2, 4).reshape(4, 16, 2, LAG_COUNT)
    return amb, position, speed, bias.reshape(RX)


def solution(mesh):
    placed = (
        P("rx", None, "tb"),
        P("rx", "tb"),
        P("rx", None),
        P("rx", None),
        P(("rx", "tb"), None, None),
        P(("rx", "tb"), None),
        P("rx"),
        P(),
        P(None, "rx"),
    )
    return jax.shard_map(
        functools.partial(local, tables()),
        mesh=mesh,
        in_specs=placed,
        out_specs=(P("tb", "rx", None, None), P(None, "rx"), P(None, "rx"), P()),
        check_vma=False,
    )
```

```python
import functools
import math

import jax
import jax.numpy as jnp
import numpy as np
from jax import lax
from jax.experimental import pallas as pl
from jax.experimental.pallas import tpu as pltpu
from jax.sharding import PartitionSpec as P

SEG = 256
DOPPLER_BINS = 32
LAG_COUNT = 1024
WL = 16
WD = 4
GN_MAX = 6
RX = 32
TB = 8
FFT = 512
SAMPLES = SEG * DOPPLER_BINS

MESH = pl.DeviceIdType.MESH
f32 = jnp.float32
bf16 = jnp.bfloat16
highest = lax.Precision.HIGHEST


def split_pair(table):
    high = table.astype(bf16)
    low = (table - high.astype(np.float64)).astype(bf16)
    return high, low


def tables():
    turn = 2.0 * np.pi / FFT
    t_f = np.arange(SEG)[:, None] * np.arange(FFT)[None, :] % FFT * turn
    forward = np.concatenate([np.cos(t_f), np.sin(t_f)], axis=1)
    backward = np.concatenate([np.cos(t_f.T), np.sin(t_f.T)], axis=1)
    d_m = (
        np.arange(DOPPLER_BINS)[:, None] * np.arange(DOPPLER_BINS)[None, :] % DOPPLER_BINS
    ) * (2.0 * np.pi / DOPPLER_BINS)
    mix = np.block([[np.cos(d_m), np.sin(d_m)], [-np.sin(d_m), np.cos(d_m)]])
    mix = mix / (FFT * math.sqrt(SAMPLES))
    return split_pair(forward) + split_pair(backward) + (mix.astype(np.float32),)


def iota(shape, dim):
    return lax.broadcasted_iota(jnp.int32, shape, dim)


def to_column(row, count):
    eye = iota((count, count), 0) == iota((count, count), 1)
    return jnp.sum(jnp.where(eye, row, 0.0), axis=1, keepdims=True)


def peer_lists(r, b):
    rows = [(lax.rem(r + d, RX), b) for d in range(1, RX)]
    blocks = [(r, lax.rem(b + d, TB)) for d in range(1, TB)]
    return rows, blocks


def remote(src, dst, send_sem, recv_sem, peer):
    return pltpu.make_async_remote_copy(
        src_ref=src,
        dst_ref=dst,
        send_sem=send_sem,
        recv_sem=recv_sem,
        device_id={"rx": peer[0], "tb": peer[1]},
        device_id_type=MESH,
    )


def front_kernel(
    raw_in, scl_in, lag_in, dop_in, own_in, em_in, start_in, steps_in,
    fhi_in, flo_in, bhi_in, blo_in, mix_in,
    amb, table,
    raw_ref, scl_ref, lag_ref, dop_ref, own_ref, em_ref, start_ref, steps_ref,
    fhi_ref, flo_ref, bhi_ref, blo_ref, mix_ref,
    block_ref, raw_all, scl_all, re_ref, im_ref, rr_ref, surf_ref, pay_ref,
    load_sem, raw_send, raw_recv, scl_send, scl_recv, code_send, code_recv,
    cfwd_send, cfwd_recv, pay_send, pay_recv, fwd_send, fwd_recv, surf_send, surf_recv, own_sem,
):
    r = lax.axis_index("rx")
    b = lax.axis_index("tb")
    barrier = pltpu.get_barrier_semaphore()
    rows, blocks = peer_lists(r, b)

    def signal(peer):
        pl.semaphore_signal(
            barrier, inc=1, device_id={"rx": peer[0], "tb": peer[1]}, device_id_type=MESH
        )

    sources = [
        (lax.rem(r + 2 * b + i, RX), lax.rem(b + d, TB)) for d in range(1, TB) for i in (1, 2)
    ]
    for peer in sources + rows + blocks:
        signal(peer)

    loads = [
        pltpu.make_async_copy(src, dst, load_sem.at[n])
        for n, (src, dst) in enumerate(
            (
                (raw_in, raw_ref), (scl_in, scl_ref), (own_in, own_ref), (em_in, em_ref),
                (start_in, start_ref), (steps_in, steps_ref), (lag_in, lag_ref),
                (dop_in, dop_ref), (fhi_in, fhi_ref), (flo_in, flo_ref), (bhi_in, bhi_ref),
                (blo_in, blo_ref), (mix_in, mix_ref),
            )
        )
    ]
    for copy in loads:
        copy.start()
    for copy in loads[:8]:
        copy.wait()
    own_raw = raw_ref[0].astype(f32)
    block_ref[...] = jnp.concatenate(
        [own_raw[k : k + 1, SEG * s : SEG * s + SEG] for k in range(2) for s in range(4)], axis=0
    ).astype(bf16)

    owner = jnp.concatenate(
        [to_column(own_ref[c : c + 1, :].astype(f32), 16) for c in range(2)], axis=0
    )
    code = jnp.concatenate(
        [to_column(em_ref[c : c + 1, :].astype(f32), 16) + (1.0 + 4.0 * c) for c in range(2)],
        axis=0,
    )
    p_row = iota((32, 32), 0)
    p_col = iota((32, 32), 1)
    owner_row = jnp.sum(jnp.where(p_row == p_col, owner, 0.0), axis=0, keepdims=True)
    same = (owner_row == owner) & (p_col < p_row)
    rank = jnp.sum(jnp.where(same, 1.0, 0.0), axis=1, keepdims=True)
    lane = iota((32, 128), 1)
    slot = lax.rem(lane, 64).astype(f32)
    placed = (rank * 32.0 + owner) == slot
    first = lane < 64
    codes = jnp.sum(jnp.where(placed & first, code, 0.0), axis=0, keepdims=True)
    lane1 = iota((1, 128), 1)
    for k in range(3):
        for e in range(4):
            codes = jnp.where(lane1 == 64 + 4 * k + e, start_ref[k : k + 1, e : e + 1], codes)
    for e in range(4):
        codes = jnp.where(lane1 == 76 + e, steps_ref[0:1, e : e + 1].astype(f32), codes)
    pay_ref[1] = codes
    raw_all[b] = block_ref[...]
    scl_all[b] = scl_ref[...]

    pl.semaphore_wait(barrier, len(sources) + len(rows) + len(blocks))

    targets = [(r, p, 0) for _, p in blocks]
    targets += [(lax.rem(r + RX - 2 * t - i, RX), t, i) for t in range(TB) for i in (1, 2)]
    sends = []
    for n, (to_r, to_b, i) in enumerate(targets):
        place = i * TB + b
        for src, dst, ss, rs in (
            (block_ref, raw_all, raw_send, raw_recv),
            (scl_ref, scl_all, scl_send, scl_recv),
        ):
            sends.append(remote(src, dst.at[place], ss.at[n], rs.at[place], (to_r, to_b)))
            sends[-1].start()
    own_code = pltpu.make_async_copy(pay_ref.at[1], table.at[b, 1, r], own_sem.at[0])
    own_code.start()
    for n, peer in enumerate(rows):
        sends.append(
            remote(pay_ref.at[1], table.at[b, 1, r], code_send.at[n], code_recv.at[r], peer)
        )
        sends[-1].start()

    places = [p for _, p in blocks] + [i * TB + t for i in (1, 2) for t in range(TB)]
    for place in places:
        remote(
            block_ref, raw_all.at[place], raw_send.at[0], raw_recv.at[place], blocks[0]
        ).wait_recv()
        remote(
            scl_ref, scl_all.at[place], scl_send.at[0], scl_recv.at[place], blocks[0]
        ).wait_recv()
    own_code.wait()
    for q, _ in rows:
        remote(
            pay_ref.at[1], table.at[b, 1, q], code_send.at[0], code_recv.at[q], rows[0]
        ).wait_recv()
    for n, peer in enumerate(blocks):
        sends.append(
            remote(table.at[b, 1], table.at[b, 1], cfwd_send.at[n], cfwd_recv.at[b], peer)
        )
        sends[-1].start()
    for copy in loads[8:]:
        copy.wait()

    raw = raw_all[...].astype(f32).reshape(3 * TB * 8, SEG).astype(bf16)
    spec = jnp.dot(raw, fhi_ref[...], preferred_element_type=f32)
    spec = spec + jnp.dot(raw, flo_ref[...], preferred_element_type=f32)
    cos_part = spec[:, :FFT].reshape(3 * TB, 8, FFT)
    sin_part = spec[:, FFT:].reshape(3 * TB, 8, FFT)
    sub = iota((1, 8, 1), 1)
    sign = jnp.where(sub < 4, 1.0, -1.0).astype(f32)
    pick = iota((1, 8, 4), 2) == lax.rem(iota((1, 8, 4), 1), 4)
    scale = jnp.sum(jnp.where(pick, scl_all[...], 0.0), axis=2, keepdims=True)
    pieces = (cos_part + sign * pltpu.roll(sin_part, 4, 1)) * scale
    for i in range(3):
        re_ref[i, 32:40, :] = jnp.zeros((8, FFT), f32)
        im_ref[i, 32:40, :] = jnp.zeros((8, FFT), f32)
        for t in range(TB):
            re_ref[i, 4 * t : 4 * t + 4, :] = pieces[i * TB + t, 0:4, :]
            im_ref[i, 4 * t : 4 * t + 4, :] = pieces[i * TB + t, 4:8, :]
    near_re = re_ref[0, 0:32, :]
    near_im = im_ref[0, 0:32, :]
    alt = jnp.where(lax.rem(iota((1, FFT), 1), 2) == 0, 1.0, -1.0).astype(f32)
    for c in range(2):
        for j in range(4):
            far_re = re_ref[c + 1, j : j + 32, :] + alt * re_ref[c + 1, j + 1 : j + 33, :]
            far_im = im_ref[c + 1, j : j + 32, :] + alt * im_ref[c + 1, j + 1 : j + 33, :]
            row = (c * 4 + j) * 32
            rr_ref[row : row + 32, :] = near_re * far_re + near_im * far_im
            rr_ref[256 + row : 288 + row, :] = near_im * far_re - near_re * far_im
    cross = rr_ref[...]
    high = cross.astype(bf16)
    low = (cross - high.astype(f32)).astype(bf16)
    lagged = jnp.dot(high, bhi_ref[...], preferred_element_type=f32)
    lagged = lagged + jnp.dot(low, bhi_ref[...], preferred_element_type=f32)
    lagged = lagged + jnp.dot(high, blo_ref[...], preferred_element_type=f32)
    lag_re = lagged[0:256, 0:256] + lagged[256:512, 256:512]
    lag_im = lagged[256:512, 0:256] - lagged[0:256, 256:512]

    lag_rows = lag_ref[pl.ds(2 * b, 2), :].astype(f32)
    dop_rows = dop_ref[pl.ds(2 * b, 2), :].astype(f32)
    tau_cols, nu_cols = [], []
    for c in range(2):
        top = jnp.concatenate(
            [lag_re[(c * 4 + j) * 32 : (c * 4 + j + 1) * 32] for j in range(4)], axis=1
        )
        low_half = jnp.concatenate(
            [lag_im[(c * 4 + j) * 32 : (c * 4 + j + 1) * 32] for j in range(4)], axis=1
        )
        stacked = jnp.concatenate([top, low_half], axis=0)
        surf = jnp.dot(mix_ref[...], stacked, precision=highest, preferred_element_type=f32)
        for comp in range(2):
            for lt in range(8):
                surf_ref[pl.ds(c * 16 + lt * 2 + comp, 32, stride=32), :] = surf[
                    comp * 32 : comp * 32 + 32, lt * 128 : lt * 128 + 128
                ]
        power = surf[0:32] * surf[0:32] + surf[32:64] * surf[32:64]
        lag0 = to_column(lag_rows[c : c + 1, :], 16)
        dop0 = to_column(dop_rows[c : c + 1, :], 16)
        offset = iota((16, DOPPLER_BINS), 1).astype(f32) - dop0
        offset = jnp.where(offset < 0.0, offset + DOPPLER_BINS, offset)
        inside = jnp.where(offset < WD, 1.0, 0.0).astype(f32)
        weights = jnp.concatenate([inside, inside * offset], axis=0)
        sums = jnp.dot(weights, power, precision=highest, preferred_element_type=f32)
        step = iota((16, LAG_COUNT), 1).astype(f32) - lag0
        within = (step >= 0.0) & (step < WL)
        plain = jnp.where(within, sums[0:16], 0.0)
        norm = 1.0 / (WL * WD)
        total = jnp.sum(plain, axis=1, keepdims=True) * norm + 1e-06
        lag_mean = jnp.sum(plain * step, axis=1, keepdims=True) * norm / total
        dop_mean = (
            jnp.sum(jnp.where(within, sums[16:32], 0.0), axis=1, keepdims=True) * norm / total
        )
        tau_cols.append((lag0 + lag_mean) * (16.0 / LAG_COUNT))
        nu_cols.append((dop0 + dop_mean) * (4.0 / DOPPLER_BINS))
    tau = jnp.concatenate(tau_cols, axis=0)
    nu = jnp.concatenate(nu_cols, axis=0)
    pay_ref[0] = jnp.sum(
        jnp.where(placed, jnp.where(first, tau, nu), 0.0), axis=0, keepdims=True
    )

    own_pay = pltpu.make_async_copy(pay_ref.at[0], table.at[b, 0, r], own_sem.at[0])
    own_pay.start()
    for n, peer in enumerate(rows):
        sends.append(
            remote(pay_ref.at[0], table.at[b, 0, r], pay_send.at[n], pay_recv.at[r], peer)
        )
        sends[-1].start()
    locals_ = []
    for d in range(4):
        locals_.append(
            pltpu.make_async_copy(
                surf_ref.at[pl.ds(pl.multiple_of(128 * b + 32 * d, 32), 32), :],
                amb.at[d, b],
                own_sem.at[1 + d],
            )
        )
        locals_[-1].start()
    for n, peer in enumerate(blocks):
        for d in range(4):
            sends.append(
                remote(
                    surf_ref.at[pl.ds(pl.multiple_of(128 * peer[1] + 32 * d, 32), 32), :],
                    amb.at[d, b],
                    surf_send.at[n, d],
                    surf_recv.at[b, d],
                    peer,
                )
            )
            sends[-1].start()
    own_pay.wait()
    plane = r // 4
    spot = lax.rem(r, 4)
    for count, dz in enumerate((0, 1, 7, 2, 6, 3, 5, 4)):
        there = lax.rem(plane + dz, 8)
        for dx in range(4):
            if dz == 0 and dx == 0:
                continue
            q = there * 4 + lax.rem(spot + dx, 4)
            remote(
                pay_ref.at[0], table.at[b, 0, q], pay_send.at[0], pay_recv.at[q], rows[0]
            ).wait_recv()
        chunk = table.at[b, 0, pl.ds(there * 4, 4)]
        for n, peer in enumerate(blocks):
            sends.append(
                remote(chunk, chunk, fwd_send.at[n, count], fwd_recv.at[b, there], peer)
            )
            sends[-1].start()
    for _, t in blocks:
        remote(
            table.at[t, 1], table.at[t, 1], cfwd_send.at[0], cfwd_recv.at[t], blocks[0]
        ).wait_recv()
        for z in range(8):
            chunk = table.at[t, 0, pl.ds(z * 4, 4)]
            remote(chunk, chunk, fwd_send.at[0, 0], fwd_recv.at[t, z], blocks[0]).wait_recv()
        for d in range(4):
            remote(
                surf_ref.at[pl.ds(0, 32), :],
                amb.at[d, t],
                surf_send.at[0, 0],
                surf_recv.at[t, d],
                blocks[0],
            ).wait_recv()
    for copy in locals_:
        copy.wait()
    for copy in sends:
        copy.wait_send()


def front(raw, scl, lag, dop, own, em, start, steps, consts):
    any_spec = pl.BlockSpec(memory_space=pl.ANY)
    dma = pltpu.SemaphoreType.DMA
    operands = (raw, scl, lag, dop, own, em, start, steps, *consts)
    n = 3 * TB - 1
    return pl.pallas_call(
        front_kernel,
        out_shape=(
            jax.ShapeDtypeStruct((4, TB, 32, 128), f32),
            jax.ShapeDtypeStruct((TB, 2, RX, 1, 128), f32),
        ),
        in_specs=[any_spec] * len(operands),
        out_specs=(any_spec, any_spec),
        scratch_shapes=[pltpu.VMEM(x.shape, x.dtype) for x in operands]
        + [
            pltpu.VMEM((8, SEG), bf16),
            pltpu.VMEM((3 * TB, 8, SEG), bf16),
            pltpu.VMEM((3 * TB,) + scl.shape, f32),
            pltpu.VMEM((3, 40, FFT), f32),
            pltpu.VMEM((3, 40, FFT), f32),
            pltpu.VMEM((512, FFT), f32),
            pltpu.VMEM((1024, 128), f32),
            pltpu.VMEM((2, 1, 128), f32),
            dma((len(operands),)),
            dma((n,)), dma((3 * TB,)), dma((n,)), dma((3 * TB,)),
            dma((RX - 1,)), dma((RX,)), dma((TB - 1,)), dma((TB,)),
            dma((RX - 1,)), dma((RX,)), dma((TB - 1, 8)), dma((TB, 8)),
            dma((TB - 1, 4)), dma((TB, 4)), dma((5,)),
        ],
        compiler_params=pltpu.CompilerParams(collective_id=0, has_side_effects=True),
        name="front",
    )(*operands)


def solve_three(normals, rhs, damp_term):
    entry_xx = normals[0] + damp_term
    entry_xy = normals[1]
    entry_xz = normals[2]
    entry_yy = normals[3] + damp_term
    entry_yz = normals[4]
    entry_zz = normals[5] + damp_term
    minor_xx = entry_yy * entry_zz - entry_yz * entry_yz
    minor_xy = entry_xz * entry_yz - entry_xy * entry_zz
    minor_xz = entry_xy * entry_yz - entry_xz * entry_yy
    minor_yy = entry_xx * entry_zz - entry_xz * entry_xz
    minor_yz = entry_xy * entry_xz - entry_xx * entry_yz
    minor_zz = entry_xx * entry_yy - entry_xy * entry_xy
    inverse = 1.0 / (entry_xx * minor_xx + entry_xy * minor_xy + entry_xz * minor_xz)
    step_x = minor_xx * rhs[0] + minor_xy * rhs[1] + minor_xz * rhs[2]
    step_y = minor_xy * rhs[0] + minor_yy * rhs[1] + minor_yz * rhs[2]
    step_z = minor_xz * rhs[0] + minor_yz * rhs[1] + minor_zz * rhs[2]
    return [step_x * inverse, step_y * inverse, step_z * inverse]


def per_receiver(x, shift):
    return pltpu.roll(x, (RX - shift) % RX, 0)


def solve_kernel(
    table_ref, rpos_ref, amb_in, pos_ref, vel_ref, bias_ref, amb_out,
    stage_ref, stage_sem, tau_ref, nu_ref, mask_ref, late_ref, fst_ref, snd_ref, spread_ref, jac_ref,
):
    stage_in = pltpu.make_async_copy(amb_in, stage_ref, stage_sem.at[0])
    stage_in.start()
    lane = iota((RX, 128), 1)
    low = lane < 64
    own_lane = iota((RX, 128), 0) == lax.rem(lane, RX)
    halves = []
    for k in range(4):
        a0, a1 = table_ref[k, 0], table_ref[k + 4, 0]
        tau_ref[k] = jnp.where(low, a0, pltpu.roll(a1, 64, 1))
        nu_ref[k] = jnp.where(low, pltpu.roll(a0, 64, 1), a1)
        code = jnp.where(low, table_ref[k, 1], pltpu.roll(table_ref[k + 4, 1], 64, 1))
        late = code > 4.5
        late_ref[k] = jnp.where(late, 1.0, 0.0)
        emitter = jnp.where(late, code - 4.0, code)
        for e in range(4):
            mask_ref[e, k] = jnp.where(emitter == e + 1.0, 1.0, 0.0)

    info = table_ref[0, 1]

    def owner_row(col):
        value = jnp.sum(jnp.where(lane == col, info, 0.0), axis=1, keepdims=True)
        return jnp.sum(jnp.where(own_lane, value, 0.0), axis=0, keepdims=True)

    def owner_rows(base):
        return jnp.concatenate([owner_row(base + e) for e in range(4)], axis=0)

    position = [owner_rows(64 + 4 * k) for k in range(3)]
    steps = owner_rows(76)

    def second_of(x, k):
        late = late_ref[k] > 0.5
        near_half = jnp.where(late, per_receiver(x, 2 * k + 2), per_receiver(x, 2 * k + 1))
        far_half = jnp.where(late, per_receiver(x, 2 * k + 10), per_receiver(x, 2 * k + 9))
        return jnp.where(low, near_half, far_half)

    eye = iota((RX, RX), 0) == iota((RX, RX), 1)
    for comp in range(3):
        column = jnp.sum(
            jnp.where(eye, rpos_ref[comp : comp + 1, :], 0.0), axis=1, keepdims=True
        )
        column = jnp.broadcast_to(column, (RX, 128))
        fst_ref[comp] = column
        for k in range(4):
            snd_ref[comp, k] = second_of(column, k)

    def sum_rows(parts):
        rows = jnp.concatenate([jnp.sum(p, axis=0, keepdims=True) for p in parts], axis=0)
        rows = rows + pltpu.roll(rows, 32, 1)
        return rows + pltpu.roll(rows, 64, 1)

    def add_to(acc, key, k, quantity):
        for e in range(4):
            term = mask_ref[e, k] * quantity
            term = term[0:8] + term[8:16] + term[16:24] + term[24:32]
            acc[key][e] = term if k == 0 else acc[key][e] + term

    def at_peaks(rows, k):
        value = mask_ref[0, k] * rows[0:1]
        for e in range(1, 4):
            value = value + mask_ref[e, k] * rows[e : e + 1]
        return value

    def ranges(position, k):
        sq_first = jnp.ones((RX, 128), f32)
        sq_second = sq_first
        firsts, seconds = [], []
        for comp in range(3):
            at = at_peaks(position[comp], k)
            d_first = at - fst_ref[comp]
            d_second = at - snd_ref[comp, k]
            sq_first = sq_first + d_first * d_first
            sq_second = sq_second + d_second * d_second
            firsts.append(d_first)
            seconds.append(d_second)
        inv_first = lax.rsqrt(sq_first)
        inv_second = lax.rsqrt(sq_second)
        spread = sq_second * inv_second - sq_first * inv_first
        spread_ref[k] = spread
        jac = [seconds[i] * inv_second - firsts[i] * inv_first for i in range(3)]
        for i in range(3):
            jac_ref[i, k] = jac[i]
        return spread, jac

    pairs = ((0, 0), (0, 1), (0, 2), (1, 1), (1, 2), (2, 2))
    acc = {key: [None] * 4 for key in range(7)}
    for k in range(4):
        _, jac = ranges(position, k)
        for key, (x, y) in enumerate(pairs):
            add_to(acc, key, k, jac[x] * jac[y])
        add_to(acc, 6, k, jnp.ones((RX, 128), f32))
    normals = [sum_rows(acc[key]) for key in range(6)]
    damp = 2.0 * (sum_rows(acc[6]) + 1.0)
    zero = jnp.zeros((4, 128), f32)

    def gn_step(step, carry):
        position, speed, bias, normals = carry
        moving = step.astype(f32) < steps
        acc = {key: [None] * 4 for key in range(3)}
        for k in range(4):
            delta = second_of(bias, k) - bias
            resid = tau_ref[k] - spread_ref[k] - delta
            for i in range(3):
                add_to(acc, i, k, jac_ref[i, k] * resid)
        moved = solve_three(normals, [sum_rows(acc[i]) for i in range(3)], damp)
        position = [position[i] + jnp.where(moving, moved[i], 0.0) for i in range(3)]
        acc = {key: [None] * 4 for key in range(9)}
        clock = None
        for k in range(4):
            spread, jac = ranges(position, k)
            for key, (x, y) in enumerate(pairs):
                add_to(acc, key, k, jac[x] * jac[y])
            rate = nu_ref[k]
            for i in range(3):
                rate = rate - at_peaks(speed[i], k) * jac[i]
            for i in range(3):
                add_to(acc, 6 + i, k, jac[i] * rate)
            live = mask_ref[0, k] + mask_ref[1, k] + mask_ref[2, k] + mask_ref[3, k]
            delta = second_of(bias, k) - bias
            cres = live * (tau_ref[k] - spread - delta)
            late = late_ref[k] * cres
            early = cres - late
            part = -cres
            for term, keep, shift in (
                (early, low, 2 * k + 1),
                (late, low, 2 * k + 2),
                (early, jnp.logical_not(low), 2 * k + 9),
                (late, jnp.logical_not(low), 2 * k + 10),
            ):
                part = part + pltpu.roll(jnp.where(keep, term, 0.0), shift, 0)
            clock = part if clock is None else clock + part
        normals = [sum_rows(acc[key]) for key in range(6)]
        turned = solve_three(normals, [sum_rows(acc[6 + i]) for i in range(3)], damp)
        speed = [speed[i] + jnp.where(moving, turned[i], 0.0) for i in range(3)]
        total = jnp.sum(clock, axis=1, keepdims=True)
        bias = bias + jnp.broadcast_to(total, (RX, 128)) / (3.0 * 16 * RX)
        return position, speed, bias, normals

    stage_in.wait()
    stage_out = [
        pltpu.make_async_copy(
            stage_ref.at[:, :, lt],
            amb_out.at[:, :, :, lt * 128 : lt * 128 + 128],
            stage_sem.at[1 + lt],
        )
        for lt in range(8)
    ]
    for copy in stage_out:
        copy.start()
    carry = (position, [zero, zero, zero], jnp.zeros((RX, 128), f32), normals)
    position, speed, bias, _ = lax.fori_loop(0, GN_MAX, gn_step, carry)
    r = lax.axis_index("rx")
    lane4 = iota((4, 128), 1)
    sub4 = iota((4, 128), 0)
    for out, value in ((pos_ref, position), (vel_ref, speed)):
        for i in range(3):
            column = jnp.sum(jnp.where(lane4 == r, value[i], 0.0), axis=1, keepdims=True)
            row = jnp.sum(jnp.where(lane4 == sub4, column, 0.0), axis=0, keepdims=True)
            out[i : i + 1, :] = row[:, 0:4]
    bias_row = jnp.sum(jnp.where(iota((RX, 128), 0) == lane, bias, 0.0), axis=0, keepdims=True)
    bias_ref[...] = bias_row[:, 0:RX]
    for copy in stage_out:
        copy.wait()


def solve(table, receiver_pos, amb):
    any_spec = pl.BlockSpec(memory_space=pl.ANY)
    vmem = pl.BlockSpec(memory_space=pltpu.VMEM)
    block = (4, RX, 128)
    return pl.pallas_call(
        solve_kernel,
        out_shape=(
            jax.ShapeDtypeStruct((3, 4), f32),
            jax.ShapeDtypeStruct((3, 4), f32),
            jax.ShapeDtypeStruct((1, RX), f32),
            jax.ShapeDtypeStruct((4, 16, 2, LAG_COUNT), f32),
        ),
        in_specs=[vmem, vmem, any_spec],
        out_specs=(vmem, vmem, vmem, any_spec),
        scratch_shapes=[
            pltpu.VMEM((4, 16, 8, 2, 128), f32),
            pltpu.SemaphoreType.DMA((9,)),
            pltpu.VMEM(block, f32),
            pltpu.VMEM(block, f32),
            pltpu.VMEM((4,) + block, f32),
            pltpu.VMEM(block, f32),
            pltpu.VMEM((3, RX, 128), f32),
            pltpu.VMEM((3,) + block, f32),
            pltpu.VMEM(block, f32),
            pltpu.VMEM((3,) + block, f32),
        ],
        name="solve",
    )(table, receiver_pos, amb)


def local(
    consts, raw_samples, block_scales, lag_window_start, doppler_window_start,
    peak_owner, peak_emitter, gn_steps, receiver_pos, emitter_start,
):
    amb, table = front(
        raw_samples, block_scales, lag_window_start, doppler_window_start,
        peak_owner.reshape(2, 16), peak_emitter, emitter_start, gn_steps.reshape(1, 4), consts,
    )
    position, speed, bias, amb = solve(
        table.reshape(TB, 2, RX, 128), receiver_pos, amb.reshape(4, 16, 8, 2, 128)
    )
    return amb, position, speed, bias.reshape(RX)


def solution(mesh):
    placed = (
        P("rx", None, "tb"),
        P("rx", "tb"),
        P("rx", None),
        P("rx", None),
        P(("rx", "tb"), None, None),
        P(("rx", "tb"), None),
        P("rx"),
        P(),
        P(None, "rx"),
    )
    return jax.shard_map(
        functools.partial(local, tables()),
        mesh=mesh,
        in_specs=placed,
        out_specs=(P("tb", "rx", None, None), P(None, "rx"), P(None, "rx"), P()),
        check_vma=False,
    )
```

```python
import functools
import math

import jax
import jax.numpy as jnp
import numpy as np
from jax import lax
from jax.experimental import pallas as pl
from jax.experimental.pallas import tpu as pltpu
from jax.sharding import PartitionSpec as P

SEG = 256
DOPPLER_BINS = 32
LAG_COUNT = 1024
WL = 16
WD = 4
GN_MAX = 6
RX = 32
TB = 8
FFT = 512
SAMPLES = SEG * DOPPLER_BINS

MESH = pl.DeviceIdType.MESH
f32 = jnp.float32
bf16 = jnp.bfloat16
highest = lax.Precision.HIGHEST


def split_pair(table):
    high = table.astype(bf16)
    low = (table - high.astype(np.float64)).astype(bf16)
    return high, low


def tables():
    turn = 2.0 * np.pi / FFT
    t_f = np.arange(SEG)[:, None] * np.arange(FFT)[None, :] % FFT * turn
    forward = np.concatenate([np.cos(t_f), np.sin(t_f)], axis=1)
    backward = np.concatenate([np.cos(t_f.T), np.sin(t_f.T)], axis=1)
    d_m = (
        np.arange(DOPPLER_BINS)[:, None] * np.arange(DOPPLER_BINS)[None, :] % DOPPLER_BINS
    ) * (2.0 * np.pi / DOPPLER_BINS)
    mix = np.block([[np.cos(d_m), np.sin(d_m)], [-np.sin(d_m), np.cos(d_m)]])
    mix = mix / (FFT * math.sqrt(SAMPLES))
    return split_pair(forward) + split_pair(backward) + (mix.astype(np.float32),)


def iota(shape, dim):
    return lax.broadcasted_iota(jnp.int32, shape, dim)


def to_column(row, count):
    eye = iota((count, count), 0) == iota((count, count), 1)
    return jnp.sum(jnp.where(eye, row, 0.0), axis=1, keepdims=True)


def peer_lists(r, b):
    rows = [(lax.rem(r + d, RX), b) for d in range(1, RX)]
    blocks = [(r, lax.rem(b + d, TB)) for d in range(1, TB)]
    return rows, blocks


def remote(src, dst, send_sem, recv_sem, peer):
    return pltpu.make_async_remote_copy(
        src_ref=src,
        dst_ref=dst,
        send_sem=send_sem,
        recv_sem=recv_sem,
        device_id={"rx": peer[0], "tb": peer[1]},
        device_id_type=MESH,
    )


def front_kernel(
    raw_in, scl_in, lag_in, dop_in, own_in, em_in, start_in, steps_in,
    fhi_in, flo_in, bhi_in, blo_in, mix_in,
    amb, table,
    raw_ref, scl_ref, lag_ref, dop_ref, own_ref, em_ref, start_ref, steps_ref,
    fhi_ref, flo_ref, bhi_ref, blo_ref, mix_ref,
    block_ref, raw_all, scl_all, re_ref, im_ref, rr_ref, surf_ref, pay_ref,
    load_sem, raw_send, raw_recv, scl_send, scl_recv, code_send, code_recv,
    cfwd_send, cfwd_recv, pay_send, pay_recv, fwd_send, fwd_recv, surf_send, surf_recv, own_sem,
):
    r = lax.axis_index("rx")
    b = lax.axis_index("tb")
    barrier = pltpu.get_barrier_semaphore()
    rows, blocks = peer_lists(r, b)

    def signal(peer):
        pl.semaphore_signal(
            barrier, inc=1, device_id={"rx": peer[0], "tb": peer[1]}, device_id_type=MESH
        )

    sources = [
        (lax.rem(r + 2 * b + i, RX), lax.rem(b + d, TB)) for d in range(1, TB) for i in (1, 2)
    ]
    for peer in sources + rows + blocks:
        signal(peer)

    loads = [
        pltpu.make_async_copy(src, dst, load_sem.at[n])
        for n, (src, dst) in enumerate(
            (
                (raw_in, raw_ref), (scl_in, scl_ref), (own_in, own_ref), (em_in, em_ref),
                (start_in, start_ref), (steps_in, steps_ref), (lag_in, lag_ref),
                (dop_in, dop_ref), (fhi_in, fhi_ref), (flo_in, flo_ref), (bhi_in, bhi_ref),
                (blo_in, blo_ref), (mix_in, mix_ref),
            )
        )
    ]
    for copy in loads:
        copy.start()
    for copy in loads[:2]:
        copy.wait()
    own_raw = raw_ref[0].astype(f32)
    block_ref[...] = jnp.concatenate(
        [own_raw[k : k + 1, SEG * s : SEG * s + SEG] for k in range(2) for s in range(4)], axis=0
    ).astype(bf16)

    raw_all[b] = block_ref[...]
    scl_all[b] = scl_ref[...]

    pl.semaphore_wait(barrier, len(sources) + len(rows) + len(blocks))

    targets = [(r, p, 0) for _, p in blocks]
    targets += [(lax.rem(r + RX - 2 * t - i, RX), t, i) for t in range(TB) for i in (1, 2)]
    sends = []
    for n, (to_r, to_b, i) in enumerate(targets):
        place = i * TB + b
        for src, dst, ss, rs in (
            (block_ref, raw_all, raw_send, raw_recv),
            (scl_ref, scl_all, scl_send, scl_recv),
        ):
            sends.append(remote(src, dst.at[place], ss.at[n], rs.at[place], (to_r, to_b)))
            sends[-1].start()
    for copy in loads[2:8]:
        copy.wait()
    owner = jnp.concatenate(
        [to_column(own_ref[c : c + 1, :].astype(f32), 16) for c in range(2)], axis=0
    )
    code = jnp.concatenate(
        [to_column(em_ref[c : c + 1, :].astype(f32), 16) + (1.0 + 4.0 * c) for c in range(2)],
        axis=0,
    )
    p_row = iota((32, 32), 0)
    p_col = iota((32, 32), 1)
    owner_row = jnp.sum(jnp.where(p_row == p_col, owner, 0.0), axis=0, keepdims=True)
    same = (owner_row == owner) & (p_col < p_row)
    rank = jnp.sum(jnp.where(same, 1.0, 0.0), axis=1, keepdims=True)
    lane = iota((32, 128), 1)
    slot = lax.rem(lane, 64).astype(f32)
    placed = (rank * 32.0 + owner) == slot
    first = lane < 64
    codes = jnp.sum(jnp.where(placed & first, code, 0.0), axis=0, keepdims=True)
    lane1 = iota((1, 128), 1)
    for k in range(3):
        for e in range(4):
            codes = jnp.where(lane1 == 64 + 4 * k + e, start_ref[k : k + 1, e : e + 1], codes)
    for e in range(4):
        codes = jnp.where(lane1 == 76 + e, steps_ref[0:1, e : e + 1].astype(f32), codes)
    pay_ref[1] = codes
    own_code = pltpu.make_async_copy(pay_ref.at[1], table.at[b, 1, r], own_sem.at[5])
    own_code.start()
    for n, peer in enumerate(rows):
        sends.append(
            remote(pay_ref.at[1], table.at[b, 1, r], code_send.at[n], code_recv.at[r], peer)
        )
        sends[-1].start()


    places = [p for _, p in blocks] + [i * TB + t for i in (1, 2) for t in range(TB)]
    for place in places:
        remote(
            block_ref, raw_all.at[place], raw_send.at[0], raw_recv.at[place], blocks[0]
        ).wait_recv()
        remote(
            scl_ref, scl_all.at[place], scl_send.at[0], scl_recv.at[place], blocks[0]
        ).wait_recv()
    for copy in loads[8:]:
        copy.wait()

    raw = raw_all[...].astype(f32).reshape(3 * TB * 8, SEG).astype(bf16)
    spec = jnp.dot(raw, fhi_ref[...], preferred_element_type=f32)
    spec = spec + jnp.dot(raw, flo_ref[...], preferred_element_type=f32)
    cos_part = spec[:, :FFT].reshape(3 * TB, 8, FFT)
    sin_part = spec[:, FFT:].reshape(3 * TB, 8, FFT)
    sub = iota((1, 8, 1), 1)
    sign = jnp.where(sub < 4, 1.0, -1.0).astype(f32)
    pick = iota((1, 8, 4), 2) == lax.rem(iota((1, 8, 4), 1), 4)
    scale = jnp.sum(jnp.where(pick, scl_all[...], 0.0), axis=2, keepdims=True)
    pieces = (cos_part + sign * pltpu.roll(sin_part, 4, 1)) * scale
    for i in range(3):
        re_ref[i, 32:40, :] = jnp.zeros((8, FFT), f32)
        im_ref[i, 32:40, :] = jnp.zeros((8, FFT), f32)
        for t in range(TB):
            re_ref[i, 4 * t : 4 * t + 4, :] = pieces[i * TB + t, 0:4, :]
            im_ref[i, 4 * t : 4 * t + 4, :] = pieces[i * TB + t, 4:8, :]
    near_re = re_ref[0, 0:32, :]
    near_im = im_ref[0, 0:32, :]
    alt = jnp.where(lax.rem(iota((1, FFT), 1), 2) == 0, 1.0, -1.0).astype(f32)
    for c in range(2):
        for j in range(4):
            far_re = re_ref[c + 1, j : j + 32, :] + alt * re_ref[c + 1, j + 1 : j + 33, :]
            far_im = im_ref[c + 1, j : j + 32, :] + alt * im_ref[c + 1, j + 1 : j + 33, :]
            row = (c * 4 + j) * 32
            rr_ref[row : row + 32, :] = near_re * far_re + near_im * far_im
            rr_ref[256 + row : 288 + row, :] = near_im * far_re - near_re * far_im
    cross = rr_ref[...]
    high = cross.astype(bf16)
    low = (cross - high.astype(f32)).astype(bf16)
    lagged = jnp.dot(high, bhi_ref[...], preferred_element_type=f32)
    lagged = lagged + jnp.dot(low, bhi_ref[...], preferred_element_type=f32)
    lagged = lagged + jnp.dot(high, blo_ref[...], preferred_element_type=f32)
    lag_re = lagged[0:256, 0:256] + lagged[256:512, 256:512]
    lag_im = lagged[256:512, 0:256] - lagged[0:256, 256:512]

    lag_rows = lag_ref[pl.ds(2 * b, 2), :].astype(f32)
    dop_rows = dop_ref[pl.ds(2 * b, 2), :].astype(f32)
    tau_cols, nu_cols, surfs = [], [], []
    for c in range(2):
        top = jnp.concatenate(
            [lag_re[(c * 4 + j) * 32 : (c * 4 + j + 1) * 32] for j in range(4)], axis=1
        )
        low_half = jnp.concatenate(
            [lag_im[(c * 4 + j) * 32 : (c * 4 + j + 1) * 32] for j in range(4)], axis=1
        )
        stacked = jnp.concatenate([top, low_half], axis=0)
        surf = jnp.dot(mix_ref[...], stacked, precision=highest, preferred_element_type=f32)
        surfs.append(surf)
        power = surf[0:32] * surf[0:32] + surf[32:64] * surf[32:64]
        lag0 = to_column(lag_rows[c : c + 1, :], 16)
        dop0 = to_column(dop_rows[c : c + 1, :], 16)
        offset = iota((16, DOPPLER_BINS), 1).astype(f32) - dop0
        offset = jnp.where(offset < 0.0, offset + DOPPLER_BINS, offset)
        inside = jnp.where(offset < WD, 1.0, 0.0).astype(f32)
        weights = jnp.concatenate([inside, inside * offset], axis=0)
        sums = jnp.dot(weights, power, precision=highest, preferred_element_type=f32)
        step = iota((16, LAG_COUNT), 1).astype(f32) - lag0
        within = (step >= 0.0) & (step < WL)
        plain = jnp.where(within, sums[0:16], 0.0)
        norm = 1.0 / (WL * WD)
        total = jnp.sum(plain, axis=1, keepdims=True) * norm + 1e-06
        lag_mean = jnp.sum(plain * step, axis=1, keepdims=True) * norm / total
        dop_mean = (
            jnp.sum(jnp.where(within, sums[16:32], 0.0), axis=1, keepdims=True) * norm / total
        )
        tau_cols.append((lag0 + lag_mean) * (16.0 / LAG_COUNT))
        nu_cols.append((dop0 + dop_mean) * (4.0 / DOPPLER_BINS))
    tau = jnp.concatenate(tau_cols, axis=0)
    nu = jnp.concatenate(nu_cols, axis=0)
    pay_ref[0] = jnp.sum(
        jnp.where(placed, jnp.where(first, tau, nu), 0.0), axis=0, keepdims=True
    )

    own_pay = pltpu.make_async_copy(pay_ref.at[0], table.at[b, 0, r], own_sem.at[0])
    own_pay.start()
    for n, peer in enumerate(rows):
        sends.append(
            remote(pay_ref.at[0], table.at[b, 0, r], pay_send.at[n], pay_recv.at[r], peer)
        )
        sends[-1].start()
    own_code.wait()
    for q, _ in rows:
        remote(
            pay_ref.at[1], table.at[b, 1, q], code_send.at[0], code_recv.at[q], rows[0]
        ).wait_recv()
    for n, peer in enumerate(blocks):
        sends.append(
            remote(table.at[b, 1], table.at[b, 1], cfwd_send.at[n], cfwd_recv.at[b], peer)
        )
        sends[-1].start()
    for c in range(2):
        for comp in range(2):
            for lt in range(8):
                surf_ref[pl.ds(c * 16 + lt * 2 + comp, 32, stride=32), :] = surfs[c][
                    comp * 32 : comp * 32 + 32, lt * 128 : lt * 128 + 128
                ]
    locals_ = []
    for d in range(4):
        locals_.append(
            pltpu.make_async_copy(
                surf_ref.at[pl.ds(pl.multiple_of(128 * b + 32 * d, 32), 32), :],
                amb.at[d, b],
                own_sem.at[1 + d],
            )
        )
        locals_[-1].start()
    for n, peer in enumerate(blocks):
        for d in range(4):
            sends.append(
                remote(
                    surf_ref.at[pl.ds(pl.multiple_of(128 * peer[1] + 32 * d, 32), 32), :],
                    amb.at[d, b],
                    surf_send.at[n, d],
                    surf_recv.at[b, d],
                    peer,
                )
            )
            sends[-1].start()
    own_pay.wait()
    plane = r // 4
    spot = lax.rem(r, 4)
    for count, dz in enumerate((0, 1, 7, 2, 6, 3, 5, 4)):
        there = lax.rem(plane + dz, 8)
        for dx in range(4):
            if dz == 0 and dx == 0:
                continue
            q = there * 4 + lax.rem(spot + dx, 4)
            remote(
                pay_ref.at[0], table.at[b, 0, q], pay_send.at[0], pay_recv.at[q], rows[0]
            ).wait_recv()
        chunk = table.at[b, 0, pl.ds(there * 4, 4)]
        for n, peer in enumerate(blocks):
            sends.append(
                remote(chunk, chunk, fwd_send.at[n, count], fwd_recv.at[b, there], peer)
            )
            sends[-1].start()
    for _, t in blocks:
        remote(
            table.at[t, 1], table.at[t, 1], cfwd_send.at[0], cfwd_recv.at[t], blocks[0]
        ).wait_recv()
        for z in range(8):
            chunk = table.at[t, 0, pl.ds(z * 4, 4)]
            remote(chunk, chunk, fwd_send.at[0, 0], fwd_recv.at[t, z], blocks[0]).wait_recv()
        for d in range(4):
            remote(
                surf_ref.at[pl.ds(0, 32), :],
                amb.at[d, t],
                surf_send.at[0, 0],
                surf_recv.at[t, d],
                blocks[0],
            ).wait_recv()
    for copy in locals_:
        copy.wait()
    for copy in sends:
        copy.wait_send()


def front(raw, scl, lag, dop, own, em, start, steps, consts):
    any_spec = pl.BlockSpec(memory_space=pl.ANY)
    dma = pltpu.SemaphoreType.DMA
    operands = (raw, scl, lag, dop, own, em, start, steps, *consts)
    n = 3 * TB - 1
    return pl.pallas_call(
        front_kernel,
        out_shape=(
            pltpu.VMEM((4, TB, 32, 128), f32),
            pltpu.VMEM((TB, 2, RX, 1, 128), f32),
        ),
        in_specs=[any_spec] * len(operands),
        out_specs=(any_spec, any_spec),
        scratch_shapes=[pltpu.VMEM(x.shape, x.dtype) for x in operands]
        + [
            pltpu.VMEM((8, SEG), bf16),
            pltpu.VMEM((3 * TB, 8, SEG), bf16),
            pltpu.VMEM((3 * TB,) + scl.shape, f32),
            pltpu.VMEM((3, 40, FFT), f32),
            pltpu.VMEM((3, 40, FFT), f32),
            pltpu.VMEM((512, FFT), f32),
            pltpu.VMEM((1024, 128), f32),
            pltpu.VMEM((2, 1, 128), f32),
            dma((len(operands),)),
            dma((n,)), dma((3 * TB,)), dma((n,)), dma((3 * TB,)),
            dma((RX - 1,)), dma((RX,)), dma((TB - 1,)), dma((TB,)),
            dma((RX - 1,)), dma((RX,)), dma((TB - 1, 8)), dma((TB, 8)),
            dma((TB - 1, 4)), dma((TB, 4)), dma((6,)),
        ],
        compiler_params=pltpu.CompilerParams(collective_id=0, has_side_effects=True),
        name="front",
    )(*operands)


def solve_three(normals, rhs, damp_term):
    entry_xx = normals[0] + damp_term
    entry_xy = normals[1]
    entry_xz = normals[2]
    entry_yy = normals[3] + damp_term
    entry_yz = normals[4]
    entry_zz = normals[5] + damp_term
    minor_xx = entry_yy * entry_zz - entry_yz * entry_yz
    minor_xy = entry_xz * entry_yz - entry_xy * entry_zz
    minor_xz = entry_xy * entry_yz - entry_xz * entry_yy
    minor_yy = entry_xx * entry_zz - entry_xz * entry_xz
    minor_yz = entry_xy * entry_xz - entry_xx * entry_yz
    minor_zz = entry_xx * entry_yy - entry_xy * entry_xy
    inverse = 1.0 / (entry_xx * minor_xx + entry_xy * minor_xy + entry_xz * minor_xz)
    step_x = minor_xx * rhs[0] + minor_xy * rhs[1] + minor_xz * rhs[2]
    step_y = minor_xy * rhs[0] + minor_yy * rhs[1] + minor_yz * rhs[2]
    step_z = minor_xz * rhs[0] + minor_yz * rhs[1] + minor_zz * rhs[2]
    return [step_x * inverse, step_y * inverse, step_z * inverse]


def per_receiver(x, shift):
    return pltpu.roll(x, (RX - shift) % RX, 0)


def solve_kernel(
    table_ref, rpos_in, amb_in, pos_ref, vel_ref, bias_ref, amb_out,
    rpos_ref, stage_sem, tau_ref, nu_ref, mask_ref, late_ref, fst_ref, snd_ref, spread_ref, jac_ref,
):
    stage_out = [
        pltpu.make_async_copy(
            amb_in.at[:, :, lt],
            amb_out.at[:, :, :, lt * 128 : lt * 128 + 128],
            stage_sem.at[lt],
        )
        for lt in range(8)
    ]
    rpos_copy = pltpu.make_async_copy(rpos_in, rpos_ref, stage_sem.at[8])
    rpos_copy.start()
    for copy in stage_out:
        copy.start()
    lane = iota((RX, 128), 1)
    low = lane < 64
    own_lane = iota((RX, 128), 0) == lax.rem(lane, RX)
    halves = []
    for k in range(4):
        a0, a1 = table_ref[k, 0], table_ref[k + 4, 0]
        tau_ref[k] = jnp.where(low, a0, pltpu.roll(a1, 64, 1))
        nu_ref[k] = jnp.where(low, pltpu.roll(a0, 64, 1), a1)
        code = jnp.where(low, table_ref[k, 1], pltpu.roll(table_ref[k + 4, 1], 64, 1))
        late = code > 4.5
        late_ref[k] = jnp.where(late, 1.0, 0.0)
        emitter = jnp.where(late, code - 4.0, code)
        for e in range(4):
            mask_ref[e, k] = jnp.where(emitter == e + 1.0, 1.0, 0.0)

    info = table_ref[0, 1]

    def owner_row(col):
        value = jnp.sum(jnp.where(lane == col, info, 0.0), axis=1, keepdims=True)
        return jnp.sum(jnp.where(own_lane, value, 0.0), axis=0, keepdims=True)

    def owner_rows(base):
        return jnp.concatenate([owner_row(base + e) for e in range(4)], axis=0)

    position = [owner_rows(64 + 4 * k) for k in range(3)]
    steps = owner_rows(76)

    def second_of(x, k):
        late = late_ref[k] > 0.5
        near_half = jnp.where(late, per_receiver(x, 2 * k + 2), per_receiver(x, 2 * k + 1))
        far_half = jnp.where(late, per_receiver(x, 2 * k + 10), per_receiver(x, 2 * k + 9))
        return jnp.where(low, near_half, far_half)

    rpos_copy.wait()
    eye = iota((RX, RX), 0) == iota((RX, RX), 1)
    for comp in range(3):
        column = jnp.sum(
            jnp.where(eye, rpos_ref[comp : comp + 1, :], 0.0), axis=1, keepdims=True
        )
        column = jnp.broadcast_to(column, (RX, 128))
        fst_ref[comp] = column
        for k in range(4):
            snd_ref[comp, k] = second_of(column, k)

    def sum_rows(parts):
        rows = jnp.concatenate([jnp.sum(p, axis=0, keepdims=True) for p in parts], axis=0)
        rows = rows + pltpu.roll(rows, 32, 1)
        return rows + pltpu.roll(rows, 64, 1)

    def add_to(acc, key, k, quantity):
        for e in range(4):
            term = mask_ref[e, k] * quantity
            term = term[0:8] + term[8:16] + term[16:24] + term[24:32]
            acc[key][e] = term if k == 0 else acc[key][e] + term

    def at_peaks(rows, k):
        value = mask_ref[0, k] * rows[0:1]
        for e in range(1, 4):
            value = value + mask_ref[e, k] * rows[e : e + 1]
        return value

    def ranges(position, k):
        sq_first = jnp.ones((RX, 128), f32)
        sq_second = sq_first
        firsts, seconds = [], []
        for comp in range(3):
            at = at_peaks(position[comp], k)
            d_first = at - fst_ref[comp]
            d_second = at - snd_ref[comp, k]
            sq_first = sq_first + d_first * d_first
            sq_second = sq_second + d_second * d_second
            firsts.append(d_first)
            seconds.append(d_second)
        inv_first = lax.rsqrt(sq_first)
        inv_second = lax.rsqrt(sq_second)
        spread = sq_second * inv_second - sq_first * inv_first
        spread_ref[k] = spread
        jac = [seconds[i] * inv_second - firsts[i] * inv_first for i in range(3)]
        for i in range(3):
            jac_ref[i, k] = jac[i]
        return spread, jac

    pairs = ((0, 0), (0, 1), (0, 2), (1, 1), (1, 2), (2, 2))
    acc = {key: [None] * 4 for key in range(7)}
    for k in range(4):
        _, jac = ranges(position, k)
        for key, (x, y) in enumerate(pairs):
            add_to(acc, key, k, jac[x] * jac[y])
        add_to(acc, 6, k, jnp.ones((RX, 128), f32))
    normals = [sum_rows(acc[key]) for key in range(6)]
    damp = 2.0 * (sum_rows(acc[6]) + 1.0)
    zero = jnp.zeros((4, 128), f32)

    def gn_step(step, carry):
        position, speed, bias, normals = carry
        moving = step.astype(f32) < steps
        acc = {key: [None] * 4 for key in range(3)}
        for k in range(4):
            delta = second_of(bias, k) - bias
            resid = tau_ref[k] - spread_ref[k] - delta
            for i in range(3):
                add_to(acc, i, k, jac_ref[i, k] * resid)
        moved = solve_three(normals, [sum_rows(acc[i]) for i in range(3)], damp)
        position = [position[i] + jnp.where(moving, moved[i], 0.0) for i in range(3)]
        acc = {key: [None] * 4 for key in range(9)}
        clock = None
        for k in range(4):
            spread, jac = ranges(position, k)
            for key, (x, y) in enumerate(pairs):
                add_to(acc, key, k, jac[x] * jac[y])
            rate = nu_ref[k]
            for i in range(3):
                rate = rate - at_peaks(speed[i], k) * jac[i]
            for i in range(3):
                add_to(acc, 6 + i, k, jac[i] * rate)
            live = mask_ref[0, k] + mask_ref[1, k] + mask_ref[2, k] + mask_ref[3, k]
            delta = second_of(bias, k) - bias
            cres = live * (tau_ref[k] - spread - delta)
            late = late_ref[k] * cres
            early = cres - late
            part = -cres
            for term, keep, shift in (
                (early, low, 2 * k + 1),
                (late, low, 2 * k + 2),
                (early, jnp.logical_not(low), 2 * k + 9),
                (late, jnp.logical_not(low), 2 * k + 10),
            ):
                part = part + pltpu.roll(jnp.where(keep, term, 0.0), shift, 0)
            clock = part if clock is None else clock + part
        normals = [sum_rows(acc[key]) for key in range(6)]
        turned = solve_three(normals, [sum_rows(acc[6 + i]) for i in range(3)], damp)
        speed = [speed[i] + jnp.where(moving, turned[i], 0.0) for i in range(3)]
        total = jnp.sum(clock, axis=1, keepdims=True)
        bias = bias + jnp.broadcast_to(total, (RX, 128)) / (3.0 * 16 * RX)
        return position, speed, bias, normals

    carry = (position, [zero, zero, zero], jnp.zeros((RX, 128), f32), normals)
    position, speed, bias, _ = lax.fori_loop(0, GN_MAX, gn_step, carry)
    r = lax.axis_index("rx")
    lane4 = iota((4, 128), 1)
    sub4 = iota((4, 128), 0)
    for out, value in ((pos_ref, position), (vel_ref, speed)):
        for i in range(3):
            column = jnp.sum(jnp.where(lane4 == r, value[i], 0.0), axis=1, keepdims=True)
            row = jnp.sum(jnp.where(lane4 == sub4, column, 0.0), axis=0, keepdims=True)
            out[i : i + 1, :] = row[:, 0:4]
    bias_row = jnp.sum(jnp.where(iota((RX, 128), 0) == lane, bias, 0.0), axis=0, keepdims=True)
    bias_ref[...] = bias_row[:, 0:RX]
    for copy in stage_out:
        copy.wait()


def solve(table, receiver_pos, amb):
    any_spec = pl.BlockSpec(memory_space=pl.ANY)
    vmem = pl.BlockSpec(memory_space=pltpu.VMEM)
    block = (4, RX, 128)
    return pl.pallas_call(
        solve_kernel,
        out_shape=(
            jax.ShapeDtypeStruct((3, 4), f32),
            jax.ShapeDtypeStruct((3, 4), f32),
            jax.ShapeDtypeStruct((1, RX), f32),
            jax.ShapeDtypeStruct((4, 16, 2, LAG_COUNT), f32),
        ),
        in_specs=[vmem, pl.BlockSpec(memory_space=pltpu.HBM), any_spec],
        out_specs=(vmem, vmem, vmem, any_spec),
        scratch_shapes=[
            pltpu.VMEM((3, RX), f32),
            pltpu.SemaphoreType.DMA((9,)),
            pltpu.VMEM(block, f32),
            pltpu.VMEM(block, f32),
            pltpu.VMEM((4,) + block, f32),
            pltpu.VMEM(block, f32),
            pltpu.VMEM((3, RX, 128), f32),
            pltpu.VMEM((3,) + block, f32),
            pltpu.VMEM(block, f32),
            pltpu.VMEM((3,) + block, f32),
        ],
        compiler_params=pltpu.CompilerParams(vmem_limit_bytes=12 << 20),
        name="solve",
    )(table, receiver_pos, amb)


def local(
    consts, raw_samples, block_scales, lag_window_start, doppler_window_start,
    peak_owner, peak_emitter, gn_steps, receiver_pos, emitter_start,
):
    amb, table = front(
        raw_samples, block_scales, lag_window_start, doppler_window_start,
        peak_owner.reshape(2, 16), peak_emitter, emitter_start, gn_steps.reshape(1, 4), consts,
    )
    position, speed, bias, amb = solve(
        table.reshape(TB, 2, RX, 128), receiver_pos, amb.reshape(4, 16, 8, 2, 128)
    )
    return amb, position, speed, bias.reshape(RX)


def solution(mesh):
    placed = (
        P("rx", None, "tb"),
        P("rx", "tb"),
        P("rx", None),
        P("rx", None),
        P(("rx", "tb"), None, None),
        P(("rx", "tb"), None),
        P("rx"),
        P(),
        P(None, "rx"),
    )
    return jax.shard_map(
        functools.partial(local, tables()),
        mesh=mesh,
        in_specs=placed,
        out_specs=(P("tb", "rx", None, None), P(None, "rx"), P(None, "rx"), P()),
        check_vma=False,
    )
```

```python
import functools
import math

import jax
import jax.numpy as jnp
import numpy as np
from jax import lax
from jax.experimental import pallas as pl
from jax.experimental.pallas import tpu as pltpu
from jax.sharding import PartitionSpec as P

SEG = 256
DOPPLER_BINS = 32
LAG_COUNT = 1024
WL = 16
WD = 4
GN_MAX = 6
RX = 32
TB = 8
FFT = 512
SAMPLES = SEG * DOPPLER_BINS

MESH = pl.DeviceIdType.MESH
f32 = jnp.float32
bf16 = jnp.bfloat16
highest = lax.Precision.HIGHEST


def split_pair(table):
    high = table.astype(bf16)
    low = (table - high.astype(np.float64)).astype(bf16)
    return high, low


def tables():
    turn = 2.0 * np.pi / FFT
    t_f = np.arange(SEG)[:, None] * np.arange(FFT)[None, :] % FFT * turn
    forward = np.concatenate([np.cos(t_f), np.sin(t_f)], axis=1)
    backward = np.concatenate([np.cos(t_f.T), np.sin(t_f.T)], axis=1)
    d_m = (
        np.arange(DOPPLER_BINS)[:, None] * np.arange(DOPPLER_BINS)[None, :] % DOPPLER_BINS
    ) * (2.0 * np.pi / DOPPLER_BINS)
    mix = np.block([[np.cos(d_m), np.sin(d_m)], [-np.sin(d_m), np.cos(d_m)]])
    mix = mix.reshape(2, DOPPLER_BINS, -1).transpose(1, 0, 2).reshape(2 * DOPPLER_BINS, -1)
    mix = mix / (FFT * math.sqrt(SAMPLES))
    return split_pair(forward) + split_pair(backward) + (mix.astype(np.float32),)


def iota(shape, dim):
    return lax.broadcasted_iota(jnp.int32, shape, dim)


def to_column(row, count):
    eye = iota((count, count), 0) == iota((count, count), 1)
    return jnp.sum(jnp.where(eye, row, 0.0), axis=1, keepdims=True)


def peer_lists(r, b):
    rows = [(lax.rem(r + d, RX), b) for d in range(1, RX)]
    blocks = [(r, lax.rem(b + d, TB)) for d in range(1, TB)]
    return rows, blocks


def remote(src, dst, send_sem, recv_sem, peer):
    return pltpu.make_async_remote_copy(
        src_ref=src,
        dst_ref=dst,
        send_sem=send_sem,
        recv_sem=recv_sem,
        device_id={"rx": peer[0], "tb": peer[1]},
        device_id_type=MESH,
    )


def front_kernel(
    raw_in, scl_in, lag_in, dop_in, own_in, em_in, start_in, steps_in,
    fhi_in, flo_in, bhi_in, blo_in, mix_in, rpos_in,
    amb, table, rpos_out,
    raw_ref, scl_ref, lag_ref, dop_ref, own_ref, em_ref, start_ref, steps_ref,
    fhi_ref, flo_ref, bhi_ref, blo_ref, mix_ref,
    block_ref, raw_all, scl_all, re_ref, im_ref, rr_ref, surf_ref, pay_ref,
    load_sem, raw_send, raw_recv, scl_send, scl_recv, code_send, code_recv,
    cfwd_send, cfwd_recv, pay_send, pay_recv, fwd_send, fwd_recv, surf_send, surf_recv, own_sem,
):
    r = lax.axis_index("rx")
    b = lax.axis_index("tb")
    barrier = pltpu.get_barrier_semaphore()
    rows, blocks = peer_lists(r, b)

    def signal(peer):
        pl.semaphore_signal(
            barrier, inc=1, device_id={"rx": peer[0], "tb": peer[1]}, device_id_type=MESH
        )

    sources = [
        (lax.rem(r + 2 * b + i, RX), lax.rem(b + d, TB)) for d in range(1, TB) for i in (1, 2)
    ]
    for peer in sources + rows + blocks:
        signal(peer)

    loads = [
        pltpu.make_async_copy(src, dst, load_sem.at[n])
        for n, (src, dst) in enumerate(
            (
                (raw_in, raw_ref), (scl_in, scl_ref), (own_in, own_ref), (em_in, em_ref),
                (start_in, start_ref), (steps_in, steps_ref), (lag_in, lag_ref),
                (dop_in, dop_ref), (fhi_in, fhi_ref), (flo_in, flo_ref), (bhi_in, bhi_ref),
                (blo_in, blo_ref), (mix_in, mix_ref),
            )
        )
    ]
    for copy in loads:
        copy.start()
    rpos_copy = pltpu.make_async_copy(rpos_in, rpos_out, own_sem.at[2])
    rpos_copy.start()
    for copy in loads[:2]:
        copy.wait()
    own_raw = raw_ref[0].astype(f32)
    block_ref[...] = jnp.concatenate(
        [own_raw[k : k + 1, SEG * s : SEG * s + SEG] for k in range(2) for s in range(4)], axis=0
    ).astype(bf16)

    raw_all[b] = block_ref[...]
    scl_all[b] = scl_ref[...]

    pl.semaphore_wait(barrier, len(sources) + len(rows) + len(blocks))

    targets = [(r, p, 0) for _, p in blocks]
    targets += [(lax.rem(r + RX - 2 * t - i, RX), t, i) for t in range(TB) for i in (1, 2)]
    sends = []
    for n, (to_r, to_b, i) in enumerate(targets):
        place = i * TB + b
        for src, dst, ss, rs in (
            (block_ref, raw_all, raw_send, raw_recv),
            (scl_ref, scl_all, scl_send, scl_recv),
        ):
            sends.append(remote(src, dst.at[place], ss.at[n], rs.at[place], (to_r, to_b)))
            sends[-1].start()
    for copy in loads[2:8]:
        copy.wait()
    owner = jnp.concatenate(
        [to_column(own_ref[c : c + 1, :].astype(f32), 16) for c in range(2)], axis=0
    )
    code = jnp.concatenate(
        [to_column(em_ref[c : c + 1, :].astype(f32), 16) + (1.0 + 4.0 * c) for c in range(2)],
        axis=0,
    )
    p_row = iota((32, 32), 0)
    p_col = iota((32, 32), 1)
    owner_row = jnp.sum(jnp.where(p_row == p_col, owner, 0.0), axis=0, keepdims=True)
    same = (owner_row == owner) & (p_col < p_row)
    rank = jnp.sum(jnp.where(same, 1.0, 0.0), axis=1, keepdims=True)
    lane = iota((32, 128), 1)
    slot = lax.rem(lane, 64).astype(f32)
    placed = (rank * 32.0 + owner) == slot
    first = lane < 64
    codes = jnp.sum(jnp.where(placed & first, code, 0.0), axis=0, keepdims=True)
    lane1 = iota((1, 128), 1)
    for k in range(3):
        for e in range(4):
            codes = jnp.where(lane1 == 64 + 4 * k + e, start_ref[k : k + 1, e : e + 1], codes)
    for e in range(4):
        codes = jnp.where(lane1 == 76 + e, steps_ref[0:1, e : e + 1].astype(f32), codes)
    pay_ref[1] = codes
    own_code = pltpu.make_async_copy(pay_ref.at[1], table.at[b, 1, r], own_sem.at[5])
    own_code.start()
    for n, peer in enumerate(rows):
        sends.append(
            remote(pay_ref.at[1], table.at[b, 1, r], code_send.at[n], code_recv.at[r], peer)
        )
        sends[-1].start()


    places = [p for _, p in blocks] + [i * TB + t for i in (1, 2) for t in range(TB)]
    for place in places:
        remote(
            block_ref, raw_all.at[place], raw_send.at[0], raw_recv.at[place], blocks[0]
        ).wait_recv()
        remote(
            scl_ref, scl_all.at[place], scl_send.at[0], scl_recv.at[place], blocks[0]
        ).wait_recv()
    for copy in loads[8:]:
        copy.wait()

    raw = raw_all[...].astype(f32).reshape(3 * TB * 8, SEG).astype(bf16)
    spec = jnp.dot(raw, fhi_ref[...], preferred_element_type=f32)
    spec = spec + jnp.dot(raw, flo_ref[...], preferred_element_type=f32)
    cos_part = spec[:, :FFT].reshape(3 * TB, 8, FFT)
    sin_part = spec[:, FFT:].reshape(3 * TB, 8, FFT)
    sub = iota((1, 8, 1), 1)
    sign = jnp.where(sub < 4, 1.0, -1.0).astype(f32)
    pick = iota((1, 8, 4), 2) == lax.rem(iota((1, 8, 4), 1), 4)
    scale = jnp.sum(jnp.where(pick, scl_all[...], 0.0), axis=2, keepdims=True)
    pieces = (cos_part + sign * pltpu.roll(sin_part, 4, 1)) * scale
    for i in range(3):
        re_ref[i, 32:40, :] = jnp.zeros((8, FFT), f32)
        im_ref[i, 32:40, :] = jnp.zeros((8, FFT), f32)
        for t in range(TB):
            re_ref[i, 4 * t : 4 * t + 4, :] = pieces[i * TB + t, 0:4, :]
            im_ref[i, 4 * t : 4 * t + 4, :] = pieces[i * TB + t, 4:8, :]
    near_re = re_ref[0, 0:32, :]
    near_im = im_ref[0, 0:32, :]
    alt = jnp.where(lax.rem(iota((1, FFT), 1), 2) == 0, 1.0, -1.0).astype(f32)
    for c in range(2):
        for j in range(4):
            far_re = re_ref[c + 1, j : j + 32, :] + alt * re_ref[c + 1, j + 1 : j + 33, :]
            far_im = im_ref[c + 1, j : j + 32, :] + alt * im_ref[c + 1, j + 1 : j + 33, :]
            row = (c * 4 + j) * 32
            rr_ref[row : row + 32, :] = near_re * far_re + near_im * far_im
            rr_ref[256 + row : 288 + row, :] = near_im * far_re - near_re * far_im
    own_code.wait()
    for q, _ in rows:
        remote(
            pay_ref.at[1], table.at[b, 1, q], code_send.at[0], code_recv.at[q], rows[0]
        ).wait_recv()
    for n, peer in enumerate(blocks):
        sends.append(
            remote(table.at[b, 1], table.at[b, 1], cfwd_send.at[n], cfwd_recv.at[b], peer)
        )
        sends[-1].start()
    cross = rr_ref[...]
    high = cross.astype(bf16)
    low = (cross - high.astype(f32)).astype(bf16)
    lagged = jnp.dot(high, bhi_ref[...], preferred_element_type=f32)
    lagged = lagged + jnp.dot(low, bhi_ref[...], preferred_element_type=f32)
    lagged = lagged + jnp.dot(high, blo_ref[...], preferred_element_type=f32)
    lag_re = lagged[0:256, 0:256] + lagged[256:512, 256:512]
    lag_im = lagged[256:512, 0:256] - lagged[0:256, 256:512]

    lag_rows = lag_ref[pl.ds(2 * b, 2), :].astype(f32)
    dop_rows = dop_ref[pl.ds(2 * b, 2), :].astype(f32)
    tau_cols, nu_cols, surfs = [], [], []
    for c in range(2):
        top = jnp.concatenate(
            [lag_re[(c * 4 + j) * 32 : (c * 4 + j + 1) * 32] for j in range(4)], axis=1
        )
        low_half = jnp.concatenate(
            [lag_im[(c * 4 + j) * 32 : (c * 4 + j + 1) * 32] for j in range(4)], axis=1
        )
        stacked = jnp.concatenate([top, low_half], axis=0)
        surf = jnp.dot(mix_ref[...], stacked, precision=highest, preferred_element_type=f32)
        surfs.append(surf)
        power = surf * surf
        lag0 = to_column(lag_rows[c : c + 1, :], 16)
        dop0 = to_column(dop_rows[c : c + 1, :], 16)
        offset = (iota((16, 2 * DOPPLER_BINS), 1) // 2).astype(f32) - dop0
        offset = jnp.where(offset < 0.0, offset + DOPPLER_BINS, offset)
        inside = jnp.where(offset < WD, 1.0, 0.0).astype(f32)
        weights = jnp.concatenate([inside, inside * offset], axis=0)
        sums = jnp.dot(weights, power, precision=highest, preferred_element_type=f32)
        step = iota((16, LAG_COUNT), 1).astype(f32) - lag0
        within = (step >= 0.0) & (step < WL)
        plain = jnp.where(within, sums[0:16], 0.0)
        norm = 1.0 / (WL * WD)
        total = jnp.sum(plain, axis=1, keepdims=True) * norm + 1e-06
        lag_mean = jnp.sum(plain * step, axis=1, keepdims=True) * norm / total
        dop_mean = (
            jnp.sum(jnp.where(within, sums[16:32], 0.0), axis=1, keepdims=True) * norm / total
        )
        tau_cols.append((lag0 + lag_mean) * (16.0 / LAG_COUNT))
        nu_cols.append((dop0 + dop_mean) * (4.0 / DOPPLER_BINS))
    tau = jnp.concatenate(tau_cols, axis=0)
    nu = jnp.concatenate(nu_cols, axis=0)
    pay_ref[0] = jnp.sum(
        jnp.where(placed, jnp.where(first, tau, nu), 0.0), axis=0, keepdims=True
    )

    own_pay = pltpu.make_async_copy(pay_ref.at[0], table.at[b, 0, r], own_sem.at[0])
    own_pay.start()
    for n, peer in enumerate(rows):
        sends.append(
            remote(pay_ref.at[0], table.at[b, 0, r], pay_send.at[n], pay_recv.at[r], peer)
        )
        sends[-1].start()
    for t in range(TB):
        surf_ref[t] = jnp.concatenate(
            [surfs[0][8 * t : 8 * t + 8], surfs[1][8 * t : 8 * t + 8]], axis=0
        ).astype(bf16)
    own_surf = pltpu.make_async_copy(surf_ref.at[b], amb.at[b], own_sem.at[1])
    own_surf.start()
    for n, peer in enumerate(blocks):
        sends.append(
            remote(surf_ref.at[peer[1]], amb.at[b], surf_send.at[n], surf_recv.at[b], peer)
        )
        sends[-1].start()
    own_pay.wait()
    plane = r // 4
    spot = lax.rem(r, 4)
    for count, dz in enumerate((0, 1, 7, 2, 6, 3, 5, 4)):
        there = lax.rem(plane + dz, 8)
        for dx in range(4):
            if dz == 0 and dx == 0:
                continue
            q = there * 4 + lax.rem(spot + dx, 4)
            remote(
                pay_ref.at[0], table.at[b, 0, q], pay_send.at[0], pay_recv.at[q], rows[0]
            ).wait_recv()
        chunk = table.at[b, 0, pl.ds(there * 4, 4)]
        for n, peer in enumerate(blocks):
            sends.append(
                remote(chunk, chunk, fwd_send.at[n, count], fwd_recv.at[b, there], peer)
            )
            sends[-1].start()
    for _, t in blocks:
        remote(
            table.at[t, 1], table.at[t, 1], cfwd_send.at[0], cfwd_recv.at[t], blocks[0]
        ).wait_recv()
        for z in range(8):
            chunk = table.at[t, 0, pl.ds(z * 4, 4)]
            remote(chunk, chunk, fwd_send.at[0, 0], fwd_recv.at[t, z], blocks[0]).wait_recv()
        remote(
            surf_ref.at[t], amb.at[t], surf_send.at[0], surf_recv.at[t], blocks[0]
        ).wait_recv()
    own_surf.wait()
    rpos_copy.wait()
    for copy in sends:
        copy.wait_send()


def front(raw, scl, lag, dop, own, em, start, steps, consts, rpos):
    any_spec = pl.BlockSpec(memory_space=pl.ANY)
    dma = pltpu.SemaphoreType.DMA
    operands = (raw, scl, lag, dop, own, em, start, steps, *consts)
    n = 3 * TB - 1
    return pl.pallas_call(
        front_kernel,
        out_shape=(
            pltpu.VMEM((TB, 16, LAG_COUNT), bf16),
            pltpu.VMEM((TB, 2, RX, 1, 128), f32),
            pltpu.VMEM(rpos.shape, f32),
        ),
        in_specs=[any_spec] * (len(operands) + 1),
        out_specs=(any_spec, any_spec, any_spec),
        scratch_shapes=[pltpu.VMEM(x.shape, x.dtype) for x in operands]
        + [
            pltpu.VMEM((8, SEG), bf16),
            pltpu.VMEM((3 * TB, 8, SEG), bf16),
            pltpu.VMEM((3 * TB,) + scl.shape, f32),
            pltpu.VMEM((3, 40, FFT), f32),
            pltpu.VMEM((3, 40, FFT), f32),
            pltpu.VMEM((512, FFT), f32),
            pltpu.VMEM((TB, 16, LAG_COUNT), bf16),
            pltpu.VMEM((2, 1, 128), f32),
            dma((len(operands),)),
            dma((n,)), dma((3 * TB,)), dma((n,)), dma((3 * TB,)),
            dma((RX - 1,)), dma((RX,)), dma((TB - 1,)), dma((TB,)),
            dma((RX - 1,)), dma((RX,)), dma((TB - 1, 8)), dma((TB, 8)),
            dma((TB - 1,)), dma((TB,)), dma((6,)),
        ],
        compiler_params=pltpu.CompilerParams(collective_id=0, has_side_effects=True),
        name="front",
    )(*operands, rpos)


def solve_three(normals, rhs, damp_term):
    entry_xx = normals[0] + damp_term
    entry_xy = normals[1]
    entry_xz = normals[2]
    entry_yy = normals[3] + damp_term
    entry_yz = normals[4]
    entry_zz = normals[5] + damp_term
    minor_xx = entry_yy * entry_zz - entry_yz * entry_yz
    minor_xy = entry_xz * entry_yz - entry_xy * entry_zz
    minor_xz = entry_xy * entry_yz - entry_xz * entry_yy
    minor_yy = entry_xx * entry_zz - entry_xz * entry_xz
    minor_yz = entry_xy * entry_xz - entry_xx * entry_yz
    minor_zz = entry_xx * entry_yy - entry_xy * entry_xy
    inverse = 1.0 / (entry_xx * minor_xx + entry_xy * minor_xy + entry_xz * minor_xz)
    step_x = minor_xx * rhs[0] + minor_xy * rhs[1] + minor_xz * rhs[2]
    step_y = minor_xy * rhs[0] + minor_yy * rhs[1] + minor_yz * rhs[2]
    step_z = minor_xz * rhs[0] + minor_yz * rhs[1] + minor_zz * rhs[2]
    return [step_x * inverse, step_y * inverse, step_z * inverse]


def per_receiver(x, shift):
    return pltpu.roll(x, (RX - shift) % RX, 0)


def solve_kernel(
    table_ref, rpos_ref, amb_in, pos_ref, vel_ref, bias_ref, amb_out,
    stage_ref, stage_sem, tau_ref, nu_ref, mask_ref, late_ref, fst_ref, snd_ref, spread_ref, jac_ref,
):
    for t in range(TB):
        value = amb_in[t].astype(f32)
        for c in range(2):
            for d in range(4):
                row = 8 * c + 2 * d
                stage_ref[d, 2 * t + c] = value[row : row + 2, :]
    stage_out = pltpu.make_async_copy(stage_ref, amb_out, stage_sem.at[0])
    stage_out.start()
    lane = iota((RX, 128), 1)
    low = lane < 64
    own_lane = iota((RX, 128), 0) == lax.rem(lane, RX)
    halves = []
    for k in range(4):
        a0, a1 = table_ref[k, 0], table_ref[k + 4, 0]
        tau_ref[k] = jnp.where(low, a0, pltpu.roll(a1, 64, 1))
        nu_ref[k] = jnp.where(low, pltpu.roll(a0, 64, 1), a1)
        code = jnp.where(low, table_ref[k, 1], pltpu.roll(table_ref[k + 4, 1], 64, 1))
        late = code > 4.5
        late_ref[k] = jnp.where(late, 1.0, 0.0)
        emitter = jnp.where(late, code - 4.0, code)
        for e in range(4):
            mask_ref[e, k] = jnp.where(emitter == e + 1.0, 1.0, 0.0)

    info = table_ref[0, 1]

    def owner_row(col):
        value = jnp.sum(jnp.where(lane == col, info, 0.0), axis=1, keepdims=True)
        return jnp.sum(jnp.where(own_lane, value, 0.0), axis=0, keepdims=True)

    def owner_rows(base):
        return jnp.concatenate([owner_row(base + e) for e in range(4)], axis=0)

    position = [owner_rows(64 + 4 * k) for k in range(3)]
    steps = owner_rows(76)

    def second_of(x, k):
        late = late_ref[k] > 0.5
        near_half = jnp.where(late, per_receiver(x, 2 * k + 2), per_receiver(x, 2 * k + 1))
        far_half = jnp.where(late, per_receiver(x, 2 * k + 10), per_receiver(x, 2 * k + 9))
        return jnp.where(low, near_half, far_half)

    eye = iota((RX, RX), 0) == iota((RX, RX), 1)
    for comp in range(3):
        column = jnp.sum(
            jnp.where(eye, rpos_ref[comp : comp + 1, :], 0.0), axis=1, keepdims=True
        )
        column = jnp.broadcast_to(column, (RX, 128))
        fst_ref[comp] = column
        for k in range(4):
            snd_ref[comp, k] = second_of(column, k)

    def sum_rows(parts):
        rows = jnp.concatenate([jnp.sum(p, axis=0, keepdims=True) for p in parts], axis=0)
        rows = rows + pltpu.roll(rows, 32, 1)
        return rows + pltpu.roll(rows, 64, 1)

    def add_to(acc, key, k, quantity):
        for e in range(4):
            term = mask_ref[e, k] * quantity
            term = term[0:8] + term[8:16] + term[16:24] + term[24:32]
            acc[key][e] = term if k == 0 else acc[key][e] + term

    def at_peaks(rows, k):
        value = mask_ref[0, k] * rows[0:1]
        for e in range(1, 4):
            value = value + mask_ref[e, k] * rows[e : e + 1]
        return value

    def ranges(position, k):
        sq_first = jnp.ones((RX, 128), f32)
        sq_second = sq_first
        firsts, seconds = [], []
        for comp in range(3):
            at = at_peaks(position[comp], k)
            d_first = at - fst_ref[comp]
            d_second = at - snd_ref[comp, k]
            sq_first = sq_first + d_first * d_first
            sq_second = sq_second + d_second * d_second
            firsts.append(d_first)
            seconds.append(d_second)
        inv_first = lax.rsqrt(sq_first)
        inv_second = lax.rsqrt(sq_second)
        spread = sq_second * inv_second - sq_first * inv_first
        spread_ref[k] = spread
        jac = [seconds[i] * inv_second - firsts[i] * inv_first for i in range(3)]
        for i in range(3):
            jac_ref[i, k] = jac[i]
        return spread, jac

    pairs = ((0, 0), (0, 1), (0, 2), (1, 1), (1, 2), (2, 2))
    acc = {key: [None] * 4 for key in range(7)}
    for k in range(4):
        _, jac = ranges(position, k)
        for key, (x, y) in enumerate(pairs):
            add_to(acc, key, k, jac[x] * jac[y])
        add_to(acc, 6, k, jnp.ones((RX, 128), f32))
    normals = [sum_rows(acc[key]) for key in range(6)]
    damp = 2.0 * (sum_rows(acc[6]) + 1.0)
    zero = jnp.zeros((4, 128), f32)

    def gn_step(step, carry):
        position, speed, bias, normals = carry
        moving = step.astype(f32) < steps
        acc = {key: [None] * 4 for key in range(3)}
        for k in range(4):
            delta = second_of(bias, k) - bias
            resid = tau_ref[k] - spread_ref[k] - delta
            for i in range(3):
                add_to(acc, i, k, jac_ref[i, k] * resid)
        moved = solve_three(normals, [sum_rows(acc[i]) for i in range(3)], damp)
        position = [position[i] + jnp.where(moving, moved[i], 0.0) for i in range(3)]
        acc = {key: [None] * 4 for key in range(9)}
        clock = None
        for k in range(4):
            spread, jac = ranges(position, k)
            for key, (x, y) in enumerate(pairs):
                add_to(acc, key, k, jac[x] * jac[y])
            rate = nu_ref[k]
            for i in range(3):
                rate = rate - at_peaks(speed[i], k) * jac[i]
            for i in range(3):
                add_to(acc, 6 + i, k, jac[i] * rate)
            live = mask_ref[0, k] + mask_ref[1, k] + mask_ref[2, k] + mask_ref[3, k]
            delta = second_of(bias, k) - bias
            cres = live * (tau_ref[k] - spread - delta)
            late = late_ref[k] * cres
            early = cres - late
            part = -cres
            for term, keep, shift in (
                (early, low, 2 * k + 1),
                (late, low, 2 * k + 2),
                (early, jnp.logical_not(low), 2 * k + 9),
                (late, jnp.logical_not(low), 2 * k + 10),
            ):
                part = part + pltpu.roll(jnp.where(keep, term, 0.0), shift, 0)
            clock = part if clock is None else clock + part
        normals = [sum_rows(acc[key]) for key in range(6)]
        turned = solve_three(normals, [sum_rows(acc[6 + i]) for i in range(3)], damp)
        speed = [speed[i] + jnp.where(moving, turned[i], 0.0) for i in range(3)]
        total = jnp.sum(clock, axis=1, keepdims=True)
        bias = bias + jnp.broadcast_to(total, (RX, 128)) / (3.0 * 16 * RX)
        return position, speed, bias, normals

    carry = (position, [zero, zero, zero], jnp.zeros((RX, 128), f32), normals)
    position, speed, bias, _ = lax.fori_loop(0, GN_MAX, gn_step, carry)
    r = lax.axis_index("rx")
    lane4 = iota((4, 128), 1)
    sub4 = iota((4, 128), 0)
    for out, value in ((pos_ref, position), (vel_ref, speed)):
        for i in range(3):
            column = jnp.sum(jnp.where(lane4 == r, value[i], 0.0), axis=1, keepdims=True)
            row = jnp.sum(jnp.where(lane4 == sub4, column, 0.0), axis=0, keepdims=True)
            out[i : i + 1, :] = row[:, 0:4]
    bias_row = jnp.sum(jnp.where(iota((RX, 128), 0) == lane, bias, 0.0), axis=0, keepdims=True)
    bias_ref[...] = bias_row[:, 0:RX]
    stage_out.wait()


def solve(table, receiver_pos, amb):
    any_spec = pl.BlockSpec(memory_space=pl.ANY)
    vmem = pl.BlockSpec(memory_space=pltpu.VMEM)
    block = (4, RX, 128)
    return pl.pallas_call(
        solve_kernel,
        out_shape=(
            jax.ShapeDtypeStruct((3, 4), f32),
            jax.ShapeDtypeStruct((3, 4), f32),
            jax.ShapeDtypeStruct((1, RX), f32),
            jax.ShapeDtypeStruct((4, 16, 2, LAG_COUNT), f32),
        ),
        in_specs=[vmem, vmem, vmem],
        out_specs=(vmem, vmem, vmem, any_spec),
        scratch_shapes=[
            pltpu.VMEM((4, 16, 2, LAG_COUNT), f32),
            pltpu.SemaphoreType.DMA((1,)),
            pltpu.VMEM(block, f32),
            pltpu.VMEM(block, f32),
            pltpu.VMEM((4,) + block, f32),
            pltpu.VMEM(block, f32),
            pltpu.VMEM((3, RX, 128), f32),
            pltpu.VMEM((3,) + block, f32),
            pltpu.VMEM(block, f32),
            pltpu.VMEM((3,) + block, f32),
        ],
        compiler_params=pltpu.CompilerParams(vmem_limit_bytes=12 << 20),
        name="solve",
    )(table, receiver_pos, amb)


def local(
    consts, raw_samples, block_scales, lag_window_start, doppler_window_start,
    peak_owner, peak_emitter, gn_steps, receiver_pos, emitter_start,
):
    amb, table, rpos = front(
        raw_samples, block_scales, lag_window_start, doppler_window_start,
        peak_owner.reshape(2, 16), peak_emitter, emitter_start, gn_steps.reshape(1, 4), consts,
        receiver_pos,
    )
    position, speed, bias, amb = solve(
        table.reshape(TB, 2, RX, 128), rpos, amb
    )
    return amb, position, speed, bias.reshape(RX)


def solution(mesh):
    placed = (
        P("rx", None, "tb"),
        P("rx", "tb"),
        P("rx", None),
        P("rx", None),
        P(("rx", "tb"), None, None),
        P(("rx", "tb"), None),
        P("rx"),
        P(),
        P(None, "rx"),
    )
    return jax.shard_map(
        functools.partial(local, tables()),
        mesh=mesh,
        in_specs=placed,
        out_specs=(P("tb", "rx", None, None), P(None, "rx"), P(None, "rx"), P()),
        check_vma=False,
    )
```

```python
import functools
import math

import jax
import jax.numpy as jnp
import numpy as np
from jax import lax
from jax.experimental import pallas as pl
from jax.experimental.pallas import tpu as pltpu
from jax.sharding import PartitionSpec as P

SEG = 256
DOPPLER_BINS = 32
LAG_COUNT = 1024
WL = 16
WD = 4
GN_MAX = 6
RX = 32
TB = 8
FFT = 512
SAMPLES = SEG * DOPPLER_BINS

MESH = pl.DeviceIdType.MESH
f32 = jnp.float32
bf16 = jnp.bfloat16


def split_pair(table):
    high = table.astype(bf16)
    low = (table - high.astype(np.float64)).astype(bf16)
    return high, low


def tables():
    turn = 2.0 * np.pi / FFT
    t_f = np.arange(SEG)[:, None] * np.arange(FFT)[None, :] % FFT * turn
    forward = np.concatenate([np.cos(t_f), np.sin(t_f)], axis=1)
    backward = np.concatenate([np.cos(t_f.T), np.sin(t_f.T)], axis=1)
    d_m = (
        np.arange(DOPPLER_BINS)[:, None] * np.arange(DOPPLER_BINS)[None, :] % DOPPLER_BINS
    ) * (2.0 * np.pi / DOPPLER_BINS)
    mix = np.block([[np.cos(d_m), np.sin(d_m)], [-np.sin(d_m), np.cos(d_m)]])
    mix = mix.reshape(2, DOPPLER_BINS, -1).transpose(1, 0, 2).reshape(2 * DOPPLER_BINS, -1)
    mix = mix / (FFT * math.sqrt(SAMPLES))
    mix_high, mix_low = split_pair(mix)
    deep_mix = np.concatenate([mix_high, mix_low, mix_high], axis=1)
    return split_pair(forward) + split_pair(backward) + (deep_mix,)


def iota(shape, dim):
    return lax.broadcasted_iota(jnp.int32, shape, dim)


def to_column(row, count):
    eye = iota((count, count), 0) == iota((count, count), 1)
    return jnp.sum(jnp.where(eye, row, 0.0), axis=1, keepdims=True)


def peer_lists(r, b):
    rows = [(lax.rem(r + d, RX), b) for d in range(1, RX)]
    blocks = [(r, lax.rem(b + d, TB)) for d in range(1, TB)]
    return rows, blocks


def remote(src, dst, send_sem, recv_sem, peer):
    return pltpu.make_async_remote_copy(
        src_ref=src,
        dst_ref=dst,
        send_sem=send_sem,
        recv_sem=recv_sem,
        device_id={"rx": peer[0], "tb": peer[1]},
        device_id_type=MESH,
    )


def front_kernel(
    raw_in, scl_in, lag_in, dop_in, own_in, em_in, start_in, steps_in,
    fhi_in, flo_in, bhi_in, blo_in, mix_in, rpos_in,
    amb, table, rpos_out,
    raw_ref, scl_ref, lag_ref, dop_ref, own_ref, em_ref, start_ref, steps_ref,
    fhi_ref, flo_ref, bhi_ref, blo_ref, mix_ref,
    block_ref, raw_all, scl_all, re_ref, im_ref, rr_ref, surf_ref, pay_ref,
    load_sem, raw_send, raw_recv, scl_send, scl_recv, code_send, code_recv,
    cfwd_send, cfwd_recv, pay_send, pay_recv, fwd_send, fwd_recv, surf_send, surf_recv, own_sem,
):
    r = lax.axis_index("rx")
    b = lax.axis_index("tb")
    barrier = pltpu.get_barrier_semaphore()
    rows, blocks = peer_lists(r, b)

    def signal(peer):
        pl.semaphore_signal(
            barrier, inc=1, device_id={"rx": peer[0], "tb": peer[1]}, device_id_type=MESH
        )

    sources = [
        (lax.rem(r + 2 * b + i, RX), lax.rem(b + d, TB)) for d in range(1, TB) for i in (1, 2)
    ]
    for peer in sources + rows + blocks:
        signal(peer)

    loads = [
        pltpu.make_async_copy(src, dst, load_sem.at[n])
        for n, (src, dst) in enumerate(
            (
                (raw_in, raw_ref), (scl_in, scl_ref), (own_in, own_ref), (em_in, em_ref),
                (start_in, start_ref), (steps_in, steps_ref), (lag_in, lag_ref),
                (dop_in, dop_ref), (fhi_in, fhi_ref), (flo_in, flo_ref), (bhi_in, bhi_ref),
                (blo_in, blo_ref), (mix_in, mix_ref),
            )
        )
    ]
    for copy in loads:
        copy.start()
    rpos_copy = pltpu.make_async_copy(rpos_in, rpos_out, own_sem.at[2])
    rpos_copy.start()
    for copy in loads[:2]:
        copy.wait()
    own_raw = raw_ref[0].astype(f32)
    block_ref[...] = jnp.concatenate(
        [own_raw[k : k + 1, SEG * s : SEG * s + SEG] for k in range(2) for s in range(4)], axis=0
    ).astype(bf16)

    raw_all[b] = block_ref[...]
    scl_all[b] = scl_ref[...]

    pl.semaphore_wait(barrier, len(sources) + len(rows) + len(blocks))

    targets = [(r, p, 0) for _, p in blocks]
    targets += [(lax.rem(r + RX - 2 * t - i, RX), t, i) for t in range(TB) for i in (1, 2)]
    sends = []
    for n, (to_r, to_b, i) in enumerate(targets):
        place = i * TB + b
        for src, dst, ss, rs in (
            (block_ref, raw_all, raw_send, raw_recv),
            (scl_ref, scl_all, scl_send, scl_recv),
        ):
            sends.append(remote(src, dst.at[place], ss.at[n], rs.at[place], (to_r, to_b)))
            sends[-1].start()
    for copy in loads[2:8]:
        copy.wait()
    owner = jnp.concatenate(
        [to_column(own_ref[c : c + 1, :].astype(f32), 16) for c in range(2)], axis=0
    )
    code = jnp.concatenate(
        [to_column(em_ref[c : c + 1, :].astype(f32), 16) + (1.0 + 4.0 * c) for c in range(2)],
        axis=0,
    )
    p_row = iota((32, 32), 0)
    p_col = iota((32, 32), 1)
    owner_row = jnp.sum(jnp.where(p_row == p_col, owner, 0.0), axis=0, keepdims=True)
    same = (owner_row == owner) & (p_col < p_row)
    rank = jnp.sum(jnp.where(same, 1.0, 0.0), axis=1, keepdims=True)
    lane = iota((32, 128), 1)
    slot = lax.rem(lane, 64).astype(f32)
    placed = (rank * 32.0 + owner) == slot
    first = lane < 64
    codes = jnp.sum(jnp.where(placed & first, code, 0.0), axis=0, keepdims=True)
    lane1 = iota((1, 128), 1)
    for k in range(3):
        for e in range(4):
            codes = jnp.where(lane1 == 64 + 4 * k + e, start_ref[k : k + 1, e : e + 1], codes)
    for e in range(4):
        codes = jnp.where(lane1 == 76 + e, steps_ref[0:1, e : e + 1].astype(f32), codes)
    pay_ref[1] = codes
    own_code = pltpu.make_async_copy(pay_ref.at[1], table.at[b, 1, r], own_sem.at[5])
    own_code.start()
    for n, peer in enumerate(rows):
        sends.append(
            remote(pay_ref.at[1], table.at[b, 1, r], code_send.at[n], code_recv.at[r], peer)
        )
        sends[-1].start()


    places = [p for _, p in blocks] + [i * TB + t for i in (1, 2) for t in range(TB)]
    for place in places:
        remote(
            block_ref, raw_all.at[place], raw_send.at[0], raw_recv.at[place], blocks[0]
        ).wait_recv()
        remote(
            scl_ref, scl_all.at[place], scl_send.at[0], scl_recv.at[place], blocks[0]
        ).wait_recv()
    for copy in loads[8:]:
        copy.wait()

    raw = raw_all[...].astype(f32).reshape(3 * TB * 8, SEG).astype(bf16)
    spec = jnp.dot(raw, fhi_ref[...], preferred_element_type=f32)
    spec = spec + jnp.dot(raw, flo_ref[...], preferred_element_type=f32)
    cos_part = spec[:, :FFT].reshape(3 * TB, 8, FFT)
    sin_part = spec[:, FFT:].reshape(3 * TB, 8, FFT)
    sub = iota((1, 8, 1), 1)
    sign = jnp.where(sub < 4, 1.0, -1.0).astype(f32)
    pick = iota((1, 8, 4), 2) == lax.rem(iota((1, 8, 4), 1), 4)
    scale = jnp.sum(jnp.where(pick, scl_all[...], 0.0), axis=2, keepdims=True)
    pieces = (cos_part + sign * pltpu.roll(sin_part, 4, 1)) * scale
    for i in range(3):
        re_ref[i, 32:40, :] = jnp.zeros((8, FFT), f32)
        im_ref[i, 32:40, :] = jnp.zeros((8, FFT), f32)
        for t in range(TB):
            re_ref[i, 4 * t : 4 * t + 4, :] = pieces[i * TB + t, 0:4, :]
            im_ref[i, 4 * t : 4 * t + 4, :] = pieces[i * TB + t, 4:8, :]
    near_re = re_ref[0, 0:32, :]
    near_im = im_ref[0, 0:32, :]
    alt = jnp.where(lax.rem(iota((1, FFT), 1), 2) == 0, 1.0, -1.0).astype(f32)
    for c in range(2):
        for j in range(4):
            far_re = re_ref[c + 1, j : j + 32, :] + alt * re_ref[c + 1, j + 1 : j + 33, :]
            far_im = im_ref[c + 1, j : j + 32, :] + alt * im_ref[c + 1, j + 1 : j + 33, :]
            row = (c * 4 + j) * 32
            rr_ref[row : row + 32, :] = near_re * far_re + near_im * far_im
            rr_ref[256 + row : 288 + row, :] = near_im * far_re - near_re * far_im
    own_code.wait()
    for q, _ in rows:
        remote(
            pay_ref.at[1], table.at[b, 1, q], code_send.at[0], code_recv.at[q], rows[0]
        ).wait_recv()
    for n, peer in enumerate(blocks):
        sends.append(
            remote(table.at[b, 1], table.at[b, 1], cfwd_send.at[n], cfwd_recv.at[b], peer)
        )
        sends[-1].start()
    cross = rr_ref[...]
    high = cross.astype(bf16)
    low = (cross - high.astype(f32)).astype(bf16)
    lagged = jnp.dot(high, bhi_ref[...], preferred_element_type=f32)
    lagged = lagged + jnp.dot(low, bhi_ref[...], preferred_element_type=f32)
    lagged = lagged + jnp.dot(high, blo_ref[...], preferred_element_type=f32)
    lag_re = lagged[0:256, 0:256] + lagged[256:512, 256:512]
    lag_im = lagged[256:512, 0:256] - lagged[0:256, 256:512]

    lag_rows = lag_ref[pl.ds(2 * b, 2), :].astype(f32)
    dop_rows = dop_ref[pl.ds(2 * b, 2), :].astype(f32)
    tau_cols, nu_cols, surfs = [], [], []
    for c in range(2):
        top = jnp.concatenate(
            [lag_re[(c * 4 + j) * 32 : (c * 4 + j + 1) * 32] for j in range(4)], axis=1
        )
        low_half = jnp.concatenate(
            [lag_im[(c * 4 + j) * 32 : (c * 4 + j + 1) * 32] for j in range(4)], axis=1
        )
        stacked = jnp.concatenate([top, low_half], axis=0)
        high = stacked.astype(bf16)
        low = (stacked - high.astype(f32)).astype(bf16)
        deep = jnp.concatenate([high, high, low], axis=0)
        surf = jnp.dot(mix_ref[...], deep, preferred_element_type=f32)
        surfs.append(surf)
        power = surf * surf
        lag0 = to_column(lag_rows[c : c + 1, :], 16)
        dop0 = to_column(dop_rows[c : c + 1, :], 16)
        offset = (iota((16, 2 * DOPPLER_BINS), 1) // 2).astype(f32) - dop0
        offset = jnp.where(offset < 0.0, offset + DOPPLER_BINS, offset)
        inside = jnp.where(offset < WD, 1.0, 0.0).astype(f32)
        weights = jnp.concatenate([inside, inside * offset], axis=0)
        weights = weights.astype(bf16)
        high = power.astype(bf16)
        low = (power - high.astype(f32)).astype(bf16)
        sums = jnp.dot(
            jnp.concatenate([weights, weights], axis=1),
            jnp.concatenate([high, low], axis=0),
            preferred_element_type=f32,
        )
        step = iota((16, LAG_COUNT), 1).astype(f32) - lag0
        within = (step >= 0.0) & (step < WL)
        plain = jnp.where(within, sums[0:16], 0.0)
        norm = 1.0 / (WL * WD)
        total = jnp.sum(plain, axis=1, keepdims=True) * norm + 1e-06
        lag_mean = jnp.sum(plain * step, axis=1, keepdims=True) * norm / total
        dop_mean = (
            jnp.sum(jnp.where(within, sums[16:32], 0.0), axis=1, keepdims=True) * norm / total
        )
        tau_cols.append((lag0 + lag_mean) * (16.0 / LAG_COUNT))
        nu_cols.append((dop0 + dop_mean) * (4.0 / DOPPLER_BINS))
    tau = jnp.concatenate(tau_cols, axis=0)
    nu = jnp.concatenate(nu_cols, axis=0)
    pay_ref[0] = jnp.sum(
        jnp.where(placed, jnp.where(first, tau, nu), 0.0), axis=0, keepdims=True
    )

    own_pay = pltpu.make_async_copy(pay_ref.at[0], table.at[b, 0, r], own_sem.at[0])
    own_pay.start()
    for n, peer in enumerate(rows):
        sends.append(
            remote(pay_ref.at[0], table.at[b, 0, r], pay_send.at[n], pay_recv.at[r], peer)
        )
        sends[-1].start()
    for t in range(TB):
        surf_ref[t] = jnp.concatenate(
            [surfs[0][8 * t : 8 * t + 8], surfs[1][8 * t : 8 * t + 8]], axis=0
        ).astype(bf16)
    own_surf = pltpu.make_async_copy(surf_ref.at[b], amb.at[b], own_sem.at[1])
    own_surf.start()
    for n, peer in enumerate(blocks):
        sends.append(
            remote(surf_ref.at[peer[1]], amb.at[b], surf_send.at[n], surf_recv.at[b], peer)
        )
        sends[-1].start()
    own_pay.wait()
    for copy in sends[: -len(blocks)]:
        copy.wait_send()
    sends = sends[-len(blocks) :]
    part = r // 8
    spot = lax.rem(r, 8)
    for count, dp in enumerate((0, 1, 3, 2)):
        there = lax.rem(part + dp, 4)
        for dx in range(8):
            if dp == 0 and dx == 0:
                continue
            q = there * 8 + lax.rem(spot + dx, 8)
            remote(
                pay_ref.at[0], table.at[b, 0, q], pay_send.at[0], pay_recv.at[q], rows[0]
            ).wait_recv()
        chunk = table.at[b, 0, pl.ds(there * 8, 8)]
        for n, peer in enumerate(blocks):
            sends.append(
                remote(chunk, chunk, fwd_send.at[n, count], fwd_recv.at[b, there], peer)
            )
            sends[-1].start()
    for _, t in blocks:
        remote(
            table.at[t, 1], table.at[t, 1], cfwd_send.at[0], cfwd_recv.at[t], blocks[0]
        ).wait_recv()
        for z in range(4):
            chunk = table.at[t, 0, pl.ds(z * 8, 8)]
            remote(chunk, chunk, fwd_send.at[0, 0], fwd_recv.at[t, z], blocks[0]).wait_recv()
        remote(
            surf_ref.at[t], amb.at[t], surf_send.at[0], surf_recv.at[t], blocks[0]
        ).wait_recv()
    own_surf.wait()
    rpos_copy.wait()
    for copy in sends:
        copy.wait_send()


def front(raw, scl, lag, dop, own, em, start, steps, consts, rpos):
    any_spec = pl.BlockSpec(memory_space=pl.ANY)
    dma = pltpu.SemaphoreType.DMA
    operands = (raw, scl, lag, dop, own, em, start, steps, *consts)
    n = 3 * TB - 1
    return pl.pallas_call(
        front_kernel,
        out_shape=(
            pltpu.VMEM((TB, 16, LAG_COUNT), bf16),
            pltpu.VMEM((TB, 2, RX, 1, 128), f32),
            pltpu.VMEM(rpos.shape, f32),
        ),
        in_specs=[any_spec] * (len(operands) + 1),
        out_specs=(any_spec, any_spec, any_spec),
        scratch_shapes=[pltpu.VMEM(x.shape, x.dtype) for x in operands]
        + [
            pltpu.VMEM((8, SEG), bf16),
            pltpu.VMEM((3 * TB, 8, SEG), bf16),
            pltpu.VMEM((3 * TB,) + scl.shape, f32),
            pltpu.VMEM((3, 40, FFT), f32),
            pltpu.VMEM((3, 40, FFT), f32),
            pltpu.VMEM((512, FFT), f32),
            pltpu.VMEM((TB, 16, LAG_COUNT), bf16),
            pltpu.VMEM((2, 1, 128), f32),
            dma((len(operands),)),
            dma((n,)), dma((3 * TB,)), dma((n,)), dma((3 * TB,)),
            dma((RX - 1,)), dma((RX,)), dma((TB - 1,)), dma((TB,)),
            dma((RX - 1,)), dma((RX,)), dma((TB - 1, 4)), dma((TB, 4)),
            dma((TB - 1,)), dma((TB,)), dma((6,)),
        ],
        compiler_params=pltpu.CompilerParams(collective_id=0, has_side_effects=True),
        name="front",
    )(*operands, rpos)


def solve_three(normals, rhs, damp_term):
    entry_xx = normals[0] + damp_term
    entry_xy = normals[1]
    entry_xz = normals[2]
    entry_yy = normals[3] + damp_term
    entry_yz = normals[4]
    entry_zz = normals[5] + damp_term
    minor_xx = entry_yy * entry_zz - entry_yz * entry_yz
    minor_xy = entry_xz * entry_yz - entry_xy * entry_zz
    minor_xz = entry_xy * entry_yz - entry_xz * entry_yy
    minor_yy = entry_xx * entry_zz - entry_xz * entry_xz
    minor_yz = entry_xy * entry_xz - entry_xx * entry_yz
    minor_zz = entry_xx * entry_yy - entry_xy * entry_xy
    inverse = 1.0 / (entry_xx * minor_xx + entry_xy * minor_xy + entry_xz * minor_xz)
    step_x = minor_xx * rhs[0] + minor_xy * rhs[1] + minor_xz * rhs[2]
    step_y = minor_xy * rhs[0] + minor_yy * rhs[1] + minor_yz * rhs[2]
    step_z = minor_xz * rhs[0] + minor_yz * rhs[1] + minor_zz * rhs[2]
    return [step_x * inverse, step_y * inverse, step_z * inverse]


def per_receiver(x, shift):
    return pltpu.roll(x, (RX - shift) % RX, 0)


def solve_kernel(
    table_ref, rpos_ref, amb_in, pos_ref, vel_ref, bias_ref, amb_out,
    stage_ref, stage_sem, tau_ref, nu_ref, mask_ref, late_ref, fst_ref, snd_ref, spread_ref, jac_ref,
):
    for t in range(TB):
        value = amb_in[t].astype(f32)
        for c in range(2):
            for d in range(4):
                row = 8 * c + 2 * d
                stage_ref[d, 2 * t + c] = value[row : row + 2, :]
    stage_out = pltpu.make_async_copy(stage_ref, amb_out, stage_sem.at[0])
    stage_out.start()
    lane = iota((RX, 128), 1)
    low = lane < 64
    own_lane = iota((RX, 128), 0) == lax.rem(lane, RX)
    halves = []
    for k in range(4):
        a0, a1 = table_ref[k, 0], table_ref[k + 4, 0]
        tau_ref[k] = jnp.where(low, a0, pltpu.roll(a1, 64, 1))
        nu_ref[k] = jnp.where(low, pltpu.roll(a0, 64, 1), a1)
        code = jnp.where(low, table_ref[k, 1], pltpu.roll(table_ref[k + 4, 1], 64, 1))
        late = code > 4.5
        late_ref[k] = jnp.where(late, 1.0, 0.0)
        emitter = jnp.where(late, code - 4.0, code)
        for e in range(4):
            mask_ref[e, k] = jnp.where(emitter == e + 1.0, 1.0, 0.0)

    info = table_ref[0, 1]

    def owner_row(col):
        value = jnp.sum(jnp.where(lane == col, info, 0.0), axis=1, keepdims=True)
        return jnp.sum(jnp.where(own_lane, value, 0.0), axis=0, keepdims=True)

    def owner_rows(base):
        return jnp.concatenate([owner_row(base + e) for e in range(4)], axis=0)

    position = [owner_rows(64 + 4 * k) for k in range(3)]
    steps = owner_rows(76)

    def second_of(x, k):
        late = late_ref[k] > 0.5
        near_half = jnp.where(late, per_receiver(x, 2 * k + 2), per_receiver(x, 2 * k + 1))
        far_half = jnp.where(late, per_receiver(x, 2 * k + 10), per_receiver(x, 2 * k + 9))
        return jnp.where(low, near_half, far_half)

    eye = iota((RX, RX), 0) == iota((RX, RX), 1)
    for comp in range(3):
        column = jnp.sum(
            jnp.where(eye, rpos_ref[comp : comp + 1, :], 0.0), axis=1, keepdims=True
        )
        column = jnp.broadcast_to(column, (RX, 128))
        fst_ref[comp] = column
        for k in range(4):
            snd_ref[comp, k] = second_of(column, k)

    def sum_rows(parts):
        rows = jnp.concatenate([jnp.sum(p, axis=0, keepdims=True) for p in parts], axis=0)
        rows = rows + pltpu.roll(rows, 32, 1)
        return rows + pltpu.roll(rows, 64, 1)

    def add_to(acc, key, k, quantity):
        for e in range(4):
            term = mask_ref[e, k] * quantity
            term = term[0:8] + term[8:16] + term[16:24] + term[24:32]
            acc[key][e] = term if k == 0 else acc[key][e] + term

    def at_peaks(rows, k):
        value = mask_ref[0, k] * rows[0:1]
        for e in range(1, 4):
            value = value + mask_ref[e, k] * rows[e : e + 1]
        return value

    def ranges(position, k):
        sq_first = jnp.ones((RX, 128), f32)
        sq_second = sq_first
        firsts, seconds = [], []
        for comp in range(3):
            at = at_peaks(position[comp], k)
            d_first = at - fst_ref[comp]
            d_second = at - snd_ref[comp, k]
            sq_first = sq_first + d_first * d_first
            sq_second = sq_second + d_second * d_second
            firsts.append(d_first)
            seconds.append(d_second)
        inv_first = lax.rsqrt(sq_first)
        inv_second = lax.rsqrt(sq_second)
        spread = sq_second * inv_second - sq_first * inv_first
        spread_ref[k] = spread
        jac = [seconds[i] * inv_second - firsts[i] * inv_first for i in range(3)]
        for i in range(3):
            jac_ref[i, k] = jac[i]
        return spread, jac

    pairs = ((0, 0), (0, 1), (0, 2), (1, 1), (1, 2), (2, 2))
    acc = {key: [None] * 4 for key in range(7)}
    for k in range(4):
        _, jac = ranges(position, k)
        for key, (x, y) in enumerate(pairs):
            add_to(acc, key, k, jac[x] * jac[y])
        add_to(acc, 6, k, jnp.ones((RX, 128), f32))
    normals = [sum_rows(acc[key]) for key in range(6)]
    damp = 2.0 * (sum_rows(acc[6]) + 1.0)
    zero = jnp.zeros((4, 128), f32)

    def gn_step(step, carry):
        position, speed, bias, normals = carry
        moving = step.astype(f32) < steps
        acc = {key: [None] * 4 for key in range(3)}
        for k in range(4):
            delta = second_of(bias, k) - bias
            resid = tau_ref[k] - spread_ref[k] - delta
            for i in range(3):
                add_to(acc, i, k, jac_ref[i, k] * resid)
        moved = solve_three(normals, [sum_rows(acc[i]) for i in range(3)], damp)
        position = [position[i] + jnp.where(moving, moved[i], 0.0) for i in range(3)]
        acc = {key: [None] * 4 for key in range(9)}
        clock = None
        for k in range(4):
            spread, jac = ranges(position, k)
            for key, (x, y) in enumerate(pairs):
                add_to(acc, key, k, jac[x] * jac[y])
            rate = nu_ref[k]
            for i in range(3):
                rate = rate - at_peaks(speed[i], k) * jac[i]
            for i in range(3):
                add_to(acc, 6 + i, k, jac[i] * rate)
            live = mask_ref[0, k] + mask_ref[1, k] + mask_ref[2, k] + mask_ref[3, k]
            delta = second_of(bias, k) - bias
            cres = live * (tau_ref[k] - spread - delta)
            late = late_ref[k] * cres
            early = cres - late
            part = -cres
            for term, keep, shift in (
                (early, low, 2 * k + 1),
                (late, low, 2 * k + 2),
                (early, jnp.logical_not(low), 2 * k + 9),
                (late, jnp.logical_not(low), 2 * k + 10),
            ):
                part = part + pltpu.roll(jnp.where(keep, term, 0.0), shift, 0)
            clock = part if clock is None else clock + part
        normals = [sum_rows(acc[key]) for key in range(6)]
        turned = solve_three(normals, [sum_rows(acc[6 + i]) for i in range(3)], damp)
        speed = [speed[i] + jnp.where(moving, turned[i], 0.0) for i in range(3)]
        total = jnp.sum(clock, axis=1, keepdims=True)
        bias = bias + jnp.broadcast_to(total, (RX, 128)) / (3.0 * 16 * RX)
        return position, speed, bias, normals

    carry = (position, [zero, zero, zero], jnp.zeros((RX, 128), f32), normals)
    position, speed, bias, _ = lax.fori_loop(0, GN_MAX, gn_step, carry)
    r = lax.axis_index("rx")
    lane4 = iota((4, 128), 1)
    sub4 = iota((4, 128), 0)
    for out, value in ((pos_ref, position), (vel_ref, speed)):
        for i in range(3):
            column = jnp.sum(jnp.where(lane4 == r, value[i], 0.0), axis=1, keepdims=True)
            row = jnp.sum(jnp.where(lane4 == sub4, column, 0.0), axis=0, keepdims=True)
            out[i : i + 1, :] = row[:, 0:4]
    bias_row = jnp.sum(jnp.where(iota((RX, 128), 0) == lane, bias, 0.0), axis=0, keepdims=True)
    bias_ref[...] = bias_row[:, 0:RX]
    stage_out.wait()


def solve(table, receiver_pos, amb):
    any_spec = pl.BlockSpec(memory_space=pl.ANY)
    vmem = pl.BlockSpec(memory_space=pltpu.VMEM)
    block = (4, RX, 128)
    return pl.pallas_call(
        solve_kernel,
        out_shape=(
            jax.ShapeDtypeStruct((3, 4), f32),
            jax.ShapeDtypeStruct((3, 4), f32),
            jax.ShapeDtypeStruct((1, RX), f32),
            jax.ShapeDtypeStruct((4, 16, 2, LAG_COUNT), f32),
        ),
        in_specs=[vmem, vmem, vmem],
        out_specs=(vmem, vmem, vmem, any_spec),
        scratch_shapes=[
            pltpu.VMEM((4, 16, 2, LAG_COUNT), f32),
            pltpu.SemaphoreType.DMA((1,)),
            pltpu.VMEM(block, f32),
            pltpu.VMEM(block, f32),
            pltpu.VMEM((4,) + block, f32),
            pltpu.VMEM(block, f32),
            pltpu.VMEM((3, RX, 128), f32),
            pltpu.VMEM((3,) + block, f32),
            pltpu.VMEM(block, f32),
            pltpu.VMEM((3,) + block, f32),
        ],
        compiler_params=pltpu.CompilerParams(vmem_limit_bytes=12 << 20),
        name="solve",
    )(table, receiver_pos, amb)


def local(
    consts, raw_samples, block_scales, lag_window_start, doppler_window_start,
    peak_owner, peak_emitter, gn_steps, receiver_pos, emitter_start,
):
    amb, table, rpos = front(
        raw_samples, block_scales, lag_window_start, doppler_window_start,
        peak_owner.reshape(2, 16), peak_emitter, emitter_start, gn_steps.reshape(1, 4), consts,
        receiver_pos,
    )
    position, speed, bias, amb = solve(
        table.reshape(TB, 2, RX, 128), rpos, amb
    )
    return amb, position, speed, bias.reshape(RX)


def solution(mesh):
    placed = (
        P("rx", None, "tb"),
        P("rx", "tb"),
        P("rx", None),
        P("rx", None),
        P(("rx", "tb"), None, None),
        P(("rx", "tb"), None),
        P("rx"),
        P(),
        P(None, "rx"),
    )
    return jax.shard_map(
        functools.partial(local, tables()),
        mesh=mesh,
        in_specs=placed,
        out_specs=(P("tb", "rx", None, None), P(None, "rx"), P(None, "rx"), P()),
        check_vma=False,
    )
```

```python
import functools
import math

import jax
import jax.numpy as jnp
import numpy as np
from jax import lax
from jax.experimental import pallas as pl
from jax.experimental.pallas import tpu as pltpu
from jax.sharding import PartitionSpec as P

SEG = 256
DOPPLER_BINS = 32
LAG_COUNT = 1024
WL = 16
WD = 4
GN_MAX = 6
RX = 32
TB = 8
FFT = 512
SAMPLES = SEG * DOPPLER_BINS

MESH = pl.DeviceIdType.MESH
f32 = jnp.float32
bf16 = jnp.bfloat16


def split_pair(table):
    high = table.astype(bf16)
    low = (table - high.astype(np.float64)).astype(bf16)
    return high, low


def tables():
    turn = 2.0 * np.pi / FFT
    t_f = np.arange(SEG)[:, None] * np.arange(FFT)[None, :] % FFT * turn
    forward = np.concatenate([np.cos(t_f), np.sin(t_f)], axis=1)
    backward = np.concatenate([np.cos(t_f.T), np.sin(t_f.T)], axis=1)
    d_m = (
        np.arange(DOPPLER_BINS)[:, None] * np.arange(DOPPLER_BINS)[None, :] % DOPPLER_BINS
    ) * (2.0 * np.pi / DOPPLER_BINS)
    mix = np.block([[np.cos(d_m), np.sin(d_m)], [-np.sin(d_m), np.cos(d_m)]])
    mix = mix.reshape(2, DOPPLER_BINS, -1).transpose(1, 0, 2).reshape(2 * DOPPLER_BINS, -1)
    mix = mix / (FFT * math.sqrt(SAMPLES))
    mix_high, mix_low = split_pair(mix)
    deep_mix = np.concatenate([mix_high, mix_low, mix_high], axis=1)
    return split_pair(forward) + split_pair(backward) + (deep_mix,)


def iota(shape, dim):
    return lax.broadcasted_iota(jnp.int32, shape, dim)


def to_column(row, count):
    eye = iota((count, count), 0) == iota((count, count), 1)
    return jnp.sum(jnp.where(eye, row, 0.0), axis=1, keepdims=True)


def peer_lists(r, b):
    rows = [(lax.rem(r + d, RX), b) for d in range(1, RX)]
    blocks = [(r, lax.rem(b + d, TB)) for d in range(1, TB)]
    return rows, blocks


def remote(src, dst, send_sem, recv_sem, peer):
    return pltpu.make_async_remote_copy(
        src_ref=src,
        dst_ref=dst,
        send_sem=send_sem,
        recv_sem=recv_sem,
        device_id={"rx": peer[0], "tb": peer[1]},
        device_id_type=MESH,
    )


def front_kernel(
    raw_in, scl_in, lag_in, dop_in, own_in, em_in, start_in, steps_in,
    fhi_in, flo_in, bhi_in, blo_in, mix_in, rpos_in,
    amb, table, prep, small,
    raw_ref, scl_ref, lag_ref, dop_ref, own_ref, em_ref, start_ref, steps_ref,
    fhi_ref, flo_ref, bhi_ref, blo_ref, mix_ref,
    rpos_ref, block_ref, raw_all, scl_all, re_ref, im_ref, rr_ref, surf_ref, pay_ref,
    code_tab, code_ref, prep_ref, small_ref, land_ref, wide_ref,
    load_sem, raw_send, raw_recv, scl_send, scl_recv, code_send, code_recv,
    cfwd_send, cfwd_recv, pay_send, pay_recv, fwd_send, fwd_recv, surf_send, surf_recv, own_sem,
):
    r = lax.axis_index("rx")
    b = lax.axis_index("tb")
    barrier = pltpu.get_barrier_semaphore()
    rows, blocks = peer_lists(r, b)

    def signal(peer):
        pl.semaphore_signal(
            barrier, inc=1, device_id={"rx": peer[0], "tb": peer[1]}, device_id_type=MESH
        )

    sources = [
        (lax.rem(r + 2 * b + i, RX), lax.rem(b + d, TB)) for d in range(1, TB) for i in (1, 2)
    ]
    for peer in sources + rows + blocks:
        signal(peer)

    loads = [
        pltpu.make_async_copy(src, dst, load_sem.at[n])
        for n, (src, dst) in enumerate(
            (
                (raw_in, raw_ref), (scl_in, scl_ref), (own_in, own_ref), (em_in, em_ref),
                (start_in, start_ref), (steps_in, steps_ref), (lag_in, lag_ref),
                (dop_in, dop_ref), (fhi_in, fhi_ref), (flo_in, flo_ref), (bhi_in, bhi_ref),
                (blo_in, blo_ref), (mix_in, mix_ref),
            )
        )
    ]
    for copy in loads:
        copy.start()
    rpos_copy = pltpu.make_async_copy(rpos_in, rpos_ref, own_sem.at[2])
    rpos_copy.start()
    for copy in loads[:2]:
        copy.wait()
    own_raw = raw_ref[0].astype(f32)
    block_ref[...] = jnp.concatenate(
        [own_raw[k : k + 1, SEG * s : SEG * s + SEG] for k in range(2) for s in range(4)], axis=0
    ).astype(bf16)

    raw_all[b] = block_ref[...]
    scl_all[b] = scl_ref[...]

    pl.semaphore_wait(barrier, len(sources) + len(rows) + len(blocks))

    targets = [(r, p, 0) for _, p in blocks]
    targets += [(lax.rem(r + RX - 2 * t - i, RX), t, i) for t in range(TB) for i in (1, 2)]
    sends = []
    for n, (to_r, to_b, i) in enumerate(targets):
        place = i * TB + b
        for src, dst, ss, rs in (
            (block_ref, raw_all, raw_send, raw_recv),
            (scl_ref, scl_all, scl_send, scl_recv),
        ):
            sends.append(remote(src, dst.at[place], ss.at[n], rs.at[place], (to_r, to_b)))
            sends[-1].start()
    for copy in loads[2:8]:
        copy.wait()
    owner = jnp.concatenate(
        [to_column(own_ref[c : c + 1, :].astype(f32), 16) for c in range(2)], axis=0
    )
    code = jnp.concatenate(
        [to_column(em_ref[c : c + 1, :].astype(f32), 16) + (1.0 + 4.0 * c) for c in range(2)],
        axis=0,
    )
    p_row = iota((32, 32), 0)
    p_col = iota((32, 32), 1)
    owner_row = jnp.sum(jnp.where(p_row == p_col, owner, 0.0), axis=0, keepdims=True)
    same = (owner_row == owner) & (p_col < p_row)
    rank = jnp.sum(jnp.where(same, 1.0, 0.0), axis=1, keepdims=True)
    lane = iota((32, 128), 1)
    slot = lax.rem(lane, 64).astype(f32)
    placed = (rank * 32.0 + owner) == slot
    first = lane < 64
    codes = jnp.sum(jnp.where(placed & first, code, 0.0), axis=0, keepdims=True)
    lane1 = iota((1, 128), 1)
    for k in range(3):
        for e in range(4):
            codes = jnp.where(lane1 == 64 + 4 * k + e, start_ref[k : k + 1, e : e + 1], codes)
    for e in range(4):
        codes = jnp.where(lane1 == 76 + e, steps_ref[0:1, e : e + 1].astype(f32), codes)
    pay_ref[1] = codes
    own_code = pltpu.make_async_copy(pay_ref.at[1], code_tab.at[b, r], own_sem.at[5])
    own_code.start()
    for n, peer in enumerate(rows):
        sends.append(
            remote(pay_ref.at[1], code_tab.at[b, r], code_send.at[n], code_recv.at[r], peer)
        )
        sends[-1].start()


    places = [p for _, p in blocks] + [i * TB + t for i in (1, 2) for t in range(TB)]
    for place in places:
        remote(
            block_ref, raw_all.at[place], raw_send.at[0], raw_recv.at[place], blocks[0]
        ).wait_recv()
        remote(
            scl_ref, scl_all.at[place], scl_send.at[0], scl_recv.at[place], blocks[0]
        ).wait_recv()
    for copy in loads[8:]:
        copy.wait()

    raw = raw_all[...].astype(f32).reshape(3 * TB * 8, SEG).astype(bf16)
    spec = jnp.dot(raw, fhi_ref[...], preferred_element_type=f32)
    spec = spec + jnp.dot(raw, flo_ref[...], preferred_element_type=f32)
    cos_part = spec[:, :FFT].reshape(3 * TB, 8, FFT)
    sin_part = spec[:, FFT:].reshape(3 * TB, 8, FFT)
    sub = iota((1, 8, 1), 1)
    sign = jnp.where(sub < 4, 1.0, -1.0).astype(f32)
    pick = iota((1, 8, 4), 2) == lax.rem(iota((1, 8, 4), 1), 4)
    scale = jnp.sum(jnp.where(pick, scl_all[...], 0.0), axis=2, keepdims=True)
    pieces = (cos_part + sign * pltpu.roll(sin_part, 4, 1)) * scale
    for i in range(3):
        re_ref[i, 32:40, :] = jnp.zeros((8, FFT), f32)
        im_ref[i, 32:40, :] = jnp.zeros((8, FFT), f32)
        for t in range(TB):
            re_ref[i, 4 * t : 4 * t + 4, :] = pieces[i * TB + t, 0:4, :]
            im_ref[i, 4 * t : 4 * t + 4, :] = pieces[i * TB + t, 4:8, :]
    near_re = re_ref[0, 0:32, :]
    near_im = im_ref[0, 0:32, :]
    alt = jnp.where(lax.rem(iota((1, FFT), 1), 2) == 0, 1.0, -1.0).astype(f32)
    for c in range(2):
        for j in range(4):
            far_re = re_ref[c + 1, j : j + 32, :] + alt * re_ref[c + 1, j + 1 : j + 33, :]
            far_im = im_ref[c + 1, j : j + 32, :] + alt * im_ref[c + 1, j + 1 : j + 33, :]
            row = (c * 4 + j) * 32
            rr_ref[row : row + 32, :] = near_re * far_re + near_im * far_im
            rr_ref[256 + row : 288 + row, :] = near_im * far_re - near_re * far_im
    own_code.wait()
    for q, _ in rows:
        remote(
            pay_ref.at[1], code_tab.at[b, q], code_send.at[0], code_recv.at[q], rows[0]
        ).wait_recv()
    for n, peer in enumerate(blocks):
        sends.append(
            remote(code_tab.at[b], code_tab.at[b], cfwd_send.at[n], cfwd_recv.at[b], peer)
        )
        sends[-1].start()
    cross = rr_ref[...]
    high = cross.astype(bf16)
    low = (cross - high.astype(f32)).astype(bf16)
    lagged = jnp.dot(high, bhi_ref[...], preferred_element_type=f32)
    lagged = lagged + jnp.dot(low, bhi_ref[...], preferred_element_type=f32)
    lagged = lagged + jnp.dot(high, blo_ref[...], preferred_element_type=f32)
    lag_re = lagged[0:256, 0:256] + lagged[256:512, 256:512]
    lag_im = lagged[256:512, 0:256] - lagged[0:256, 256:512]

    lag_rows = lag_ref[pl.ds(2 * b, 2), :].astype(f32)
    dop_rows = dop_ref[pl.ds(2 * b, 2), :].astype(f32)
    tau_cols, nu_cols, surfs = [], [], []
    for c in range(2):
        top = jnp.concatenate(
            [lag_re[(c * 4 + j) * 32 : (c * 4 + j + 1) * 32] for j in range(4)], axis=1
        )
        low_half = jnp.concatenate(
            [lag_im[(c * 4 + j) * 32 : (c * 4 + j + 1) * 32] for j in range(4)], axis=1
        )
        stacked = jnp.concatenate([top, low_half], axis=0)
        high = stacked.astype(bf16)
        low = (stacked - high.astype(f32)).astype(bf16)
        deep = jnp.concatenate([high, high, low], axis=0)
        surf = jnp.dot(mix_ref[...], deep, preferred_element_type=f32)
        surfs.append(surf)
        power = surf * surf
        lag0 = to_column(lag_rows[c : c + 1, :], 16)
        dop0 = to_column(dop_rows[c : c + 1, :], 16)
        offset = (iota((16, 2 * DOPPLER_BINS), 1) // 2).astype(f32) - dop0
        offset = jnp.where(offset < 0.0, offset + DOPPLER_BINS, offset)
        inside = jnp.where(offset < WD, 1.0, 0.0).astype(f32)
        weights = jnp.concatenate([inside, inside * offset], axis=0)
        weights = weights.astype(bf16)
        high = power.astype(bf16)
        low = (power - high.astype(f32)).astype(bf16)
        sums = jnp.dot(
            jnp.concatenate([weights, weights], axis=1),
            jnp.concatenate([high, low], axis=0),
            preferred_element_type=f32,
        )
        step = iota((16, LAG_COUNT), 1).astype(f32) - lag0
        within = (step >= 0.0) & (step < WL)
        plain = jnp.where(within, sums[0:16], 0.0)
        norm = 1.0 / (WL * WD)
        total = jnp.sum(plain, axis=1, keepdims=True) * norm + 1e-06
        lag_mean = jnp.sum(plain * step, axis=1, keepdims=True) * norm / total
        dop_mean = (
            jnp.sum(jnp.where(within, sums[16:32], 0.0), axis=1, keepdims=True) * norm / total
        )
        tau_cols.append((lag0 + lag_mean) * (16.0 / LAG_COUNT))
        nu_cols.append((dop0 + dop_mean) * (4.0 / DOPPLER_BINS))
    tau = jnp.concatenate(tau_cols, axis=0)
    nu = jnp.concatenate(nu_cols, axis=0)
    pay_ref[0] = jnp.sum(
        jnp.where(placed, jnp.where(first, tau, nu), 0.0), axis=0, keepdims=True
    )

    own_pay = pltpu.make_async_copy(pay_ref.at[0], table.at[b, r], own_sem.at[0])
    own_pay.start()
    for n, peer in enumerate(rows):
        sends.append(
            remote(pay_ref.at[0], table.at[b, r], pay_send.at[n], pay_recv.at[r], peer)
        )
        sends[-1].start()
    for t in range(TB):
        surf_ref[t] = jnp.concatenate(
            [surfs[0][8 * t : 8 * t + 8], surfs[1][8 * t : 8 * t + 8]], axis=0
        ).astype(bf16)
    own_surf = pltpu.make_async_copy(surf_ref.at[b], land_ref.at[b], own_sem.at[1])
    own_surf.start()
    for n, peer in enumerate(blocks):
        sends.append(
            remote(surf_ref.at[peer[1]], land_ref.at[b], surf_send.at[n], surf_recv.at[b], peer)
        )
        sends[-1].start()
    own_pay.wait()
    for copy in sends[: -len(blocks)]:
        copy.wait_send()
    sends = sends[-len(blocks) :]
    for _, t in blocks:
        remote(
            code_tab.at[t], code_tab.at[t], cfwd_send.at[0], cfwd_recv.at[t], blocks[0]
        ).wait_recv()
    rpos_copy.wait()
    for k in range(TB):
        for q in range(RX):
            code_ref[k, q : q + 1, :] = code_tab[k, q]
    prepare(code_ref, rpos_ref, prep_ref, small_ref)
    outs = [
        pltpu.make_async_copy(prep_ref, prep, own_sem.at[2]),
        pltpu.make_async_copy(small_ref, small, own_sem.at[3]),
        pltpu.make_async_copy(wide_ref, amb, own_sem.at[4]),
    ]
    outs[0].start()
    outs[1].start()
    part = r // 8
    spot = lax.rem(r, 8)
    for count, dp in enumerate((0, 1, 3, 2)):
        there = lax.rem(part + dp, 4)
        for dx in range(8):
            if dp == 0 and dx == 0:
                continue
            q = there * 8 + lax.rem(spot + dx, 8)
            remote(
                pay_ref.at[0], table.at[b, q], pay_send.at[0], pay_recv.at[q], rows[0]
            ).wait_recv()
        chunk = table.at[b, pl.ds(there * 8, 8)]
        for n, peer in enumerate(blocks):
            sends.append(
                remote(chunk, chunk, fwd_send.at[n, count], fwd_recv.at[b, there], peer)
            )
            sends[-1].start()
    own_surf.wait()
    for _, t in blocks:
        remote(
            surf_ref.at[t], land_ref.at[t], surf_send.at[0], surf_recv.at[t], blocks[0]
        ).wait_recv()
    for t in range(TB):
        value = land_ref[t].astype(f32)
        for c in range(2):
            for d in range(4):
                row = 8 * c + 2 * d
                wide_ref[d, 2 * t + c] = value[row : row + 2, :]
    outs[2].start()
    for _, t in blocks:
        for z in range(4):
            chunk = table.at[t, pl.ds(z * 8, 8)]
            remote(chunk, chunk, fwd_send.at[0, 0], fwd_recv.at[t, z], blocks[0]).wait_recv()
    for copy in outs:
        copy.wait()
    for copy in sends:
        copy.wait_send()


def front(raw, scl, lag, dop, own, em, start, steps, consts, rpos):
    any_spec = pl.BlockSpec(memory_space=pl.ANY)
    dma = pltpu.SemaphoreType.DMA
    operands = (raw, scl, lag, dop, own, em, start, steps, *consts)
    n = 3 * TB - 1
    return pl.pallas_call(
        front_kernel,
        out_shape=(
            pltpu.VMEM((4, 16, 2, LAG_COUNT), f32),
            pltpu.VMEM((TB, RX, 1, 128), f32),
            pltpu.VMEM((51, RX, 128), f32),
            pltpu.VMEM((11, 8, 128), f32),
        ),
        in_specs=[any_spec] * (len(operands) + 1),
        out_specs=(any_spec,) * 4,
        scratch_shapes=[pltpu.VMEM(x.shape, x.dtype) for x in operands]
        + [
            pltpu.VMEM(rpos.shape, f32),
            pltpu.VMEM((8, SEG), bf16),
            pltpu.VMEM((3 * TB, 8, SEG), bf16),
            pltpu.VMEM((3 * TB,) + scl.shape, f32),
            pltpu.VMEM((3, 40, FFT), f32),
            pltpu.VMEM((3, 40, FFT), f32),
            pltpu.VMEM((512, FFT), f32),
            pltpu.VMEM((TB, 16, LAG_COUNT), bf16),
            pltpu.VMEM((2, 1, 128), f32),
            pltpu.VMEM((TB, RX, 1, 128), f32),
            pltpu.VMEM((TB, RX, 128), f32),
            pltpu.VMEM((51, RX, 128), f32),
            pltpu.VMEM((11, 8, 128), f32),
            pltpu.VMEM((TB, 16, LAG_COUNT), bf16),
            pltpu.VMEM((4, 16, 2, LAG_COUNT), f32),
            dma((len(operands),)),
            dma((n,)), dma((3 * TB,)), dma((n,)), dma((3 * TB,)),
            dma((RX - 1,)), dma((RX,)), dma((TB - 1,)), dma((TB,)),
            dma((RX - 1,)), dma((RX,)), dma((TB - 1, 4)), dma((TB, 4)),
            dma((TB - 1,)), dma((TB,)), dma((6,)),
        ],
        compiler_params=pltpu.CompilerParams(collective_id=0, has_side_effects=True),
        name="front",
    )(*operands, rpos)


def solve_three(normals, rhs, damp_term):
    entry_xx = normals[0] + damp_term
    entry_xy = normals[1]
    entry_xz = normals[2]
    entry_yy = normals[3] + damp_term
    entry_yz = normals[4]
    entry_zz = normals[5] + damp_term
    minor_xx = entry_yy * entry_zz - entry_yz * entry_yz
    minor_xy = entry_xz * entry_yz - entry_xy * entry_zz
    minor_xz = entry_xy * entry_yz - entry_xz * entry_yy
    minor_yy = entry_xx * entry_zz - entry_xz * entry_xz
    minor_yz = entry_xy * entry_xz - entry_xx * entry_yz
    minor_zz = entry_xx * entry_yy - entry_xy * entry_xy
    inverse = 1.0 / (entry_xx * minor_xx + entry_xy * minor_xy + entry_xz * minor_xz)
    step_x = minor_xx * rhs[0] + minor_xy * rhs[1] + minor_xz * rhs[2]
    step_y = minor_xy * rhs[0] + minor_yy * rhs[1] + minor_yz * rhs[2]
    step_z = minor_xz * rhs[0] + minor_yz * rhs[1] + minor_zz * rhs[2]
    return [step_x * inverse, step_y * inverse, step_z * inverse]


def per_receiver(x, shift):
    return pltpu.roll(x, (RX - shift) % RX, 0)


ROW_OF = (0, 4, 2, 6)
OWNER_AT = (0, 0, 2, 2, 1, 1, 3, 3)
PAIRS = ((0, 0), (0, 1), (0, 2), (1, 1), (1, 2), (2, 2))
MASK, LATE, FIRST, SECOND, SPREAD, JAC = 0, 16, 20, 23, 35, 39
START, STEPS, DAMP, NORMAL = 0, 3, 4, 5


def fold(parts):
    sub = iota((8, 128), 0)
    upper = sub < 4
    early = lax.rem(sub, 4) < 2

    def halves(x, y):
        return jnp.where(upper, x, y) + pltpu.roll(jnp.where(upper, y, x), 4, 0)

    one = halves(parts[0], parts[1])
    two = halves(parts[2], parts[3])
    rows = jnp.where(early, one + pltpu.roll(one, 6, 0), two + pltpu.roll(two, 2, 0))
    rows = rows + pltpu.roll(rows, 7, 0)
    rows = rows + pltpu.roll(rows, 32, 1)
    return rows + pltpu.roll(rows, 64, 1)


def add_to(prep_ref, acc, key, k, quantity):
    for e in range(4):
        term = prep_ref[MASK + 4 * e + k] * quantity
        term = (term[0:8] + term[8:16]) + (term[16:24] + term[24:32])
        acc[key][e] = term if k == 0 else acc[key][e] + term


def at_peaks(prep_ref, rows, k):
    value = prep_ref[MASK + k] * rows[0:1]
    for e in range(1, 4):
        value = value + prep_ref[MASK + 4 * e + k] * rows[ROW_OF[e] : ROW_OF[e] + 1]
    return value


def second_of(x, late, k):
    low = iota((RX, 128), 1) < 64
    near_half = jnp.where(late, per_receiver(x, 2 * k + 2), per_receiver(x, 2 * k + 1))
    far_half = jnp.where(late, per_receiver(x, 2 * k + 10), per_receiver(x, 2 * k + 9))
    return jnp.where(low, near_half, far_half)


def ranges(prep_ref, position, k):
    sq_first = jnp.ones((RX, 128), f32)
    sq_second = sq_first
    firsts, seconds = [], []
    for comp in range(3):
        at = at_peaks(prep_ref, position[comp], k)
        d_first = at - prep_ref[FIRST + comp]
        d_second = at - prep_ref[SECOND + 4 * comp + k]
        sq_first = sq_first + d_first * d_first
        sq_second = sq_second + d_second * d_second
        firsts.append(d_first)
        seconds.append(d_second)
    inv_first = lax.rsqrt(sq_first)
    inv_second = lax.rsqrt(sq_second)
    spread = sq_second * inv_second - sq_first * inv_first
    return spread, [seconds[i] * inv_second - firsts[i] * inv_first for i in range(3)]


def prepare(code_ref, rpos_ref, prep_ref, small_ref):
    lane = iota((RX, 128), 1)
    low = lane < 64
    own_lane = iota((RX, 128), 0) == lax.rem(lane, RX)
    for k in range(4):
        code = jnp.where(low, code_ref[k], pltpu.roll(code_ref[k + 4], 64, 1))
        late = code > 4.5
        prep_ref[LATE + k] = jnp.where(late, 1.0, 0.0)
        emitter = jnp.where(late, code - 4.0, code)
        for e in range(4):
            prep_ref[MASK + 4 * e + k] = jnp.where(emitter == e + 1.0, 1.0, 0.0)
    info = code_ref[0]

    def owner_row(col):
        value = jnp.sum(jnp.where(lane == col, info, 0.0), axis=1, keepdims=True)
        return jnp.sum(jnp.where(own_lane, value, 0.0), axis=0, keepdims=True)

    def owner_rows(base):
        made = [owner_row(base + e) for e in range(4)]
        return jnp.concatenate([made[e] for e in OWNER_AT], axis=0)

    position = [owner_rows(64 + 4 * k) for k in range(3)]
    for k in range(3):
        small_ref[START + k] = position[k]
    small_ref[STEPS] = owner_rows(76)
    eye = iota((RX, RX), 0) == iota((RX, RX), 1)
    for comp in range(3):
        column = jnp.sum(
            jnp.where(eye, rpos_ref[comp : comp + 1, :], 0.0), axis=1, keepdims=True
        )
        column = jnp.broadcast_to(column, (RX, 128))
        prep_ref[FIRST + comp] = column
        for k in range(4):
            prep_ref[SECOND + 4 * comp + k] = second_of(column, prep_ref[LATE + k] > 0.5, k)
    acc = {key: [None] * 4 for key in range(7)}
    for k in range(4):
        spread, jac = ranges(prep_ref, position, k)
        prep_ref[SPREAD + k] = spread
        for i in range(3):
            prep_ref[JAC + 4 * i + k] = jac[i]
        for key, (x, y) in enumerate(PAIRS):
            add_to(prep_ref, acc, key, k, jac[x] * jac[y])
        add_to(prep_ref, acc, 6, k, jnp.ones((RX, 128), f32))
    for key in range(6):
        small_ref[NORMAL + key] = fold(acc[key])
    small_ref[DAMP] = 2.0 * (fold(acc[6]) + 1.0)


def solve_kernel(
    table_ref, prep_ref, small_ref, amb_in, pos_ref, vel_ref, bias_ref, amb_out,
    out_sem, tau_ref, nu_ref, spread_ref, jac_ref,
):
    amb_copy = pltpu.make_async_copy(amb_in, amb_out, out_sem.at[0])
    amb_copy.start()
    lane = iota((RX, 128), 1)
    low = lane < 64
    for k in range(4):
        a0, a1 = table_ref[k], table_ref[k + 4]
        tau_ref[k] = jnp.where(low, a0, pltpu.roll(a1, 64, 1))
        nu_ref[k] = jnp.where(low, pltpu.roll(a0, 64, 1), a1)
        spread_ref[k] = prep_ref[SPREAD + k]
        for i in range(3):
            jac_ref[i, k] = prep_ref[JAC + 4 * i + k]
    position = [small_ref[START + k] for k in range(3)]
    steps = small_ref[STEPS]
    damp = small_ref[DAMP]
    normals = [small_ref[NORMAL + key] for key in range(6)]
    zero = jnp.zeros((8, 128), f32)

    def gn_step(step, carry):
        position, speed, bias, normals = carry
        moving = step.astype(f32) < steps
        acc = {key: [None] * 4 for key in range(3)}
        for k in range(4):
            delta = second_of(bias, prep_ref[LATE + k] > 0.5, k) - bias
            resid = tau_ref[k] - spread_ref[k] - delta
            for i in range(3):
                add_to(prep_ref, acc, i, k, jac_ref[i, k] * resid)
        moved = solve_three(normals, [fold(acc[i]) for i in range(3)], damp)
        position = [position[i] + jnp.where(moving, moved[i], 0.0) for i in range(3)]
        acc = {key: [None] * 4 for key in range(9)}
        clock = None
        for k in range(4):
            spread, jac = ranges(prep_ref, position, k)
            spread_ref[k] = spread
            for i in range(3):
                jac_ref[i, k] = jac[i]
            for key, (x, y) in enumerate(PAIRS):
                add_to(prep_ref, acc, key, k, jac[x] * jac[y])
            rate = nu_ref[k]
            for i in range(3):
                rate = rate - at_peaks(prep_ref, speed[i], k) * jac[i]
            for i in range(3):
                add_to(prep_ref, acc, 6 + i, k, jac[i] * rate)
            late_k = prep_ref[LATE + k]
            live = (prep_ref[MASK + k] + prep_ref[MASK + 4 + k]) + (
                prep_ref[MASK + 8 + k] + prep_ref[MASK + 12 + k]
            )
            delta = second_of(bias, late_k > 0.5, k) - bias
            cres = live * (tau_ref[k] - spread - delta)
            late = late_k * cres
            early = cres - late
            part = -cres
            for term, keep, shift in (
                (early, low, 2 * k + 1),
                (late, low, 2 * k + 2),
                (early, jnp.logical_not(low), 2 * k + 9),
                (late, jnp.logical_not(low), 2 * k + 10),
            ):
                part = part + pltpu.roll(jnp.where(keep, term, 0.0), shift, 0)
            clock = part if clock is None else clock + part
        normals = [fold(acc[key]) for key in range(6)]
        turned = solve_three(normals, [fold(acc[6 + i]) for i in range(3)], damp)
        speed = [speed[i] + jnp.where(moving, turned[i], 0.0) for i in range(3)]
        total = jnp.sum(clock, axis=1, keepdims=True)
        bias = bias + jnp.broadcast_to(total, (RX, 128)) / (3.0 * 16 * RX)
        return position, speed, bias, normals

    carry = (position, [zero, zero, zero], jnp.zeros((RX, 128), f32), normals)
    position, speed, bias, _ = lax.fori_loop(0, GN_MAX, gn_step, carry)
    r = lax.axis_index("rx")
    lane8 = iota((8, 128), 1)
    sub8 = iota((8, 128), 0)
    spot = lax.rem(sub8, 4) + jnp.where(sub8 >= 4, 1, 0)
    used = (lax.rem(sub8, 2) == 0) & (lane8 == spot)
    for out, value in ((pos_ref, position), (vel_ref, speed)):
        for i in range(3):
            column = jnp.sum(jnp.where(lane8 == r, value[i], 0.0), axis=1, keepdims=True)
            row = jnp.sum(jnp.where(used, column, 0.0), axis=0, keepdims=True)
            out[i : i + 1, :] = row[:, 0:4]
    bias_row = jnp.sum(jnp.where(iota((RX, 128), 0) == lane, bias, 0.0), axis=0, keepdims=True)
    bias_ref[...] = bias_row[:, 0:RX]
    amb_copy.wait()


def solve(table, prep, small, amb):
    any_spec = pl.BlockSpec(memory_space=pl.ANY)
    vmem = pl.BlockSpec(memory_space=pltpu.VMEM)
    block = (4, RX, 128)
    return pl.pallas_call(
        solve_kernel,
        out_shape=(
            jax.ShapeDtypeStruct((3, 4), f32),
            jax.ShapeDtypeStruct((3, 4), f32),
            jax.ShapeDtypeStruct((1, RX), f32),
            jax.ShapeDtypeStruct((4, 16, 2, LAG_COUNT), f32),
        ),
        in_specs=[vmem, vmem, vmem, any_spec],
        out_specs=(vmem, vmem, vmem, any_spec),
        scratch_shapes=[
            pltpu.SemaphoreType.DMA((1,)),
            pltpu.VMEM(block, f32),
            pltpu.VMEM(block, f32),
            pltpu.VMEM(block, f32),
            pltpu.VMEM((3,) + block, f32),
        ],
        compiler_params=pltpu.CompilerParams(vmem_limit_bytes=12 << 20),
        name="solve",
    )(table, prep, small, amb)


def local(
    consts, raw_samples, block_scales, lag_window_start, doppler_window_start,
    peak_owner, peak_emitter, gn_steps, receiver_pos, emitter_start,
):
    amb, table, prep, small = front(
        raw_samples, block_scales, lag_window_start, doppler_window_start,
        peak_owner.reshape(2, 16), peak_emitter, emitter_start, gn_steps.reshape(1, 4), consts,
        receiver_pos,
    )
    position, speed, bias, amb = solve(
        table.reshape(TB, RX, 128), prep, small, amb
    )
    return amb, position, speed, bias.reshape(RX)


def solution(mesh):
    placed = (
        P("rx", None, "tb"),
        P("rx", "tb"),
        P("rx", None),
        P("rx", None),
        P(("rx", "tb"), None, None),
        P(("rx", "tb"), None),
        P("rx"),
        P(),
        P(None, "rx"),
    )
    return jax.shard_map(
        functools.partial(local, tables()),
        mesh=mesh,
        in_specs=placed,
        out_specs=(P("tb", "rx", None, None), P(None, "rx"), P(None, "rx"), P()),
        check_vma=False,
    )
```

```python
import functools
import math

import jax
import jax.numpy as jnp
import numpy as np
from jax import lax
from jax.experimental import pallas as pl
from jax.experimental.pallas import tpu as pltpu
from jax.sharding import PartitionSpec as P

SEG = 256
DOPPLER_BINS = 32
LAG_COUNT = 1024
WL = 16
WD = 4
GN_MAX = 6
RX = 32
TB = 8
FFT = 512
SAMPLES = SEG * DOPPLER_BINS

MESH = pl.DeviceIdType.MESH
f32 = jnp.float32
bf16 = jnp.bfloat16


def split_pair(table):
    high = table.astype(bf16)
    low = (table - high.astype(np.float64)).astype(bf16)
    return high, low


def tables():
    turn = 2.0 * np.pi / FFT
    t_f = np.arange(SEG)[:, None] * np.arange(FFT)[None, :] % FFT * turn
    forward = np.concatenate([np.cos(t_f), np.sin(t_f)], axis=1)
    backward = np.concatenate([np.cos(t_f.T), np.sin(t_f.T)], axis=1)
    d_m = (
        np.arange(DOPPLER_BINS)[:, None] * np.arange(DOPPLER_BINS)[None, :] % DOPPLER_BINS
    ) * (2.0 * np.pi / DOPPLER_BINS)
    mix = np.block([[np.cos(d_m), np.sin(d_m)], [-np.sin(d_m), np.cos(d_m)]])
    mix = mix.reshape(2, DOPPLER_BINS, -1).transpose(1, 0, 2).reshape(2 * DOPPLER_BINS, -1)
    mix = mix / (FFT * math.sqrt(SAMPLES))
    mix_high, mix_low = split_pair(mix)
    deep_mix = np.concatenate([mix_high, mix_low, mix_high], axis=1)
    return split_pair(forward) + split_pair(backward) + (deep_mix,)


def iota(shape, dim):
    return lax.broadcasted_iota(jnp.int32, shape, dim)


def to_column(row, count):
    eye = iota((count, count), 0) == iota((count, count), 1)
    return jnp.sum(jnp.where(eye, row, 0.0), axis=1, keepdims=True)


def peer_lists(r, b):
    rows = [(lax.rem(r + d, RX), b) for d in range(1, RX)]
    blocks = [(r, lax.rem(b + d, TB)) for d in range(1, TB)]
    return rows, blocks


def remote(src, dst, send_sem, recv_sem, peer):
    return pltpu.make_async_remote_copy(
        src_ref=src,
        dst_ref=dst,
        send_sem=send_sem,
        recv_sem=recv_sem,
        device_id={"rx": peer[0], "tb": peer[1]},
        device_id_type=MESH,
    )


def front_kernel(
    raw_in, scl_in, lag_in, dop_in, own_in, em_in, start_in, steps_in,
    fhi_in, flo_in, bhi_in, blo_in, mix_in, rpos_in,
    amb, table, prep, small,
    raw_ref, scl_ref, lag_ref, dop_ref, own_ref, em_ref, start_ref, steps_ref,
    fhi_ref, flo_ref, bhi_ref, blo_ref, mix_ref,
    rpos_ref, block_ref, raw_all, scl_all, re_ref, im_ref, rr_ref, surf_ref, pay_ref,
    code_tab, code_ref, prep_ref, small_ref, land_ref, wide_ref,
    load_sem, raw_send, raw_recv, scl_send, scl_recv, code_send, code_recv,
    cfwd_send, cfwd_recv, pay_send, pay_recv, fwd_send, fwd_recv, surf_send, surf_recv, own_sem,
):
    r = lax.axis_index("rx")
    b = lax.axis_index("tb")
    barrier = pltpu.get_barrier_semaphore()
    rows, blocks = peer_lists(r, b)

    def signal(peer):
        pl.semaphore_signal(
            barrier, inc=1, device_id={"rx": peer[0], "tb": peer[1]}, device_id_type=MESH
        )

    sources = [
        (lax.rem(r + 2 * b + i, RX), lax.rem(b + d, TB)) for d in range(1, TB) for i in (1, 2)
    ]
    for peer in sources + rows + blocks:
        signal(peer)

    loads = [
        pltpu.make_async_copy(src, dst, load_sem.at[n])
        for n, (src, dst) in enumerate(
            (
                (raw_in, raw_ref), (scl_in, scl_ref), (own_in, own_ref), (em_in, em_ref),
                (start_in, start_ref), (steps_in, steps_ref), (lag_in, lag_ref),
                (dop_in, dop_ref), (fhi_in, fhi_ref), (flo_in, flo_ref), (bhi_in, bhi_ref),
                (blo_in, blo_ref), (mix_in, mix_ref),
            )
        )
    ]
    for copy in loads:
        copy.start()
    rpos_copy = pltpu.make_async_copy(rpos_in, rpos_ref, own_sem.at[2])
    rpos_copy.start()
    for copy in loads[:2]:
        copy.wait()
    own_raw = raw_ref[0].astype(f32)
    block_ref[...] = jnp.concatenate(
        [own_raw[k : k + 1, SEG * s : SEG * s + SEG] for k in range(2) for s in range(4)], axis=0
    ).astype(bf16)

    raw_all[b] = block_ref[...]
    scl_all[b] = scl_ref[...]

    pl.semaphore_wait(barrier, len(sources) + len(rows) + len(blocks))

    targets = [(r, p, 0) for _, p in blocks]
    targets += [(lax.rem(r + RX - 2 * t - i, RX), t, i) for t in range(TB) for i in (1, 2)]
    sends = []
    for n, (to_r, to_b, i) in enumerate(targets):
        place = i * TB + b
        for src, dst, ss, rs in (
            (block_ref, raw_all, raw_send, raw_recv),
            (scl_ref, scl_all, scl_send, scl_recv),
        ):
            sends.append(remote(src, dst.at[place], ss.at[n], rs.at[place], (to_r, to_b)))
            sends[-1].start()
    for copy in loads[2:8]:
        copy.wait()
    owner = jnp.concatenate(
        [to_column(own_ref[c : c + 1, :].astype(f32), 16) for c in range(2)], axis=0
    )
    code = jnp.concatenate(
        [to_column(em_ref[c : c + 1, :].astype(f32), 16) + (1.0 + 4.0 * c) for c in range(2)],
        axis=0,
    )
    p_row = iota((32, 32), 0)
    p_col = iota((32, 32), 1)
    owner_row = jnp.sum(jnp.where(p_row == p_col, owner, 0.0), axis=0, keepdims=True)
    same = (owner_row == owner) & (p_col < p_row)
    rank = jnp.sum(jnp.where(same, 1.0, 0.0), axis=1, keepdims=True)
    lane = iota((32, 128), 1)
    slot = lax.rem(lane, 64).astype(f32)
    placed = (rank * 32.0 + owner) == slot
    first = lane < 64
    codes = jnp.sum(jnp.where(placed & first, code, 0.0), axis=0, keepdims=True)
    lane1 = iota((1, 128), 1)
    for k in range(3):
        for e in range(4):
            codes = jnp.where(lane1 == 64 + 4 * k + e, start_ref[k : k + 1, e : e + 1], codes)
    for e in range(4):
        codes = jnp.where(lane1 == 76 + e, steps_ref[0:1, e : e + 1].astype(f32), codes)
    pay_ref[1] = codes
    own_code = pltpu.make_async_copy(pay_ref.at[1], code_tab.at[b, r], own_sem.at[5])
    own_code.start()
    for n, peer in enumerate(rows):
        sends.append(
            remote(pay_ref.at[1], code_tab.at[b, r], code_send.at[n], code_recv.at[r], peer)
        )
        sends[-1].start()


    places = [p for _, p in blocks] + [i * TB + t for i in (1, 2) for t in range(TB)]
    for place in places:
        remote(
            block_ref, raw_all.at[place], raw_send.at[0], raw_recv.at[place], blocks[0]
        ).wait_recv()
        remote(
            scl_ref, scl_all.at[place], scl_send.at[0], scl_recv.at[place], blocks[0]
        ).wait_recv()
    for copy in loads[8:]:
        copy.wait()

    raw = raw_all[...].astype(f32).reshape(3 * TB * 8, SEG).astype(bf16)
    spec = jnp.dot(raw, fhi_ref[...], preferred_element_type=f32)
    spec = spec + jnp.dot(raw, flo_ref[...], preferred_element_type=f32)
    cos_part = spec[:, :FFT].reshape(3 * TB, 8, FFT)
    sin_part = spec[:, FFT:].reshape(3 * TB, 8, FFT)
    sub = iota((1, 8, 1), 1)
    sign = jnp.where(sub < 4, 1.0, -1.0).astype(f32)
    pick = iota((1, 8, 4), 2) == lax.rem(iota((1, 8, 4), 1), 4)
    scale = jnp.sum(jnp.where(pick, scl_all[...], 0.0), axis=2, keepdims=True)
    pieces = (cos_part + sign * pltpu.roll(sin_part, 4, 1)) * scale
    for i in range(3):
        re_ref[i, 32:40, :] = jnp.zeros((8, FFT), f32)
        im_ref[i, 32:40, :] = jnp.zeros((8, FFT), f32)
        for t in range(TB):
            re_ref[i, 4 * t : 4 * t + 4, :] = pieces[i * TB + t, 0:4, :]
            im_ref[i, 4 * t : 4 * t + 4, :] = pieces[i * TB + t, 4:8, :]
    near_re = re_ref[0, 0:32, :]
    near_im = im_ref[0, 0:32, :]
    alt = jnp.where(lax.rem(iota((1, FFT), 1), 2) == 0, 1.0, -1.0).astype(f32)
    for c in range(2):
        for j in range(4):
            far_re = re_ref[c + 1, j : j + 32, :] + alt * re_ref[c + 1, j + 1 : j + 33, :]
            far_im = im_ref[c + 1, j : j + 32, :] + alt * im_ref[c + 1, j + 1 : j + 33, :]
            row = (c * 4 + j) * 32
            rr_ref[row : row + 32, :] = near_re * far_re + near_im * far_im
            rr_ref[256 + row : 288 + row, :] = near_im * far_re - near_re * far_im
    own_code.wait()
    for q, _ in rows:
        remote(
            pay_ref.at[1], code_tab.at[b, q], code_send.at[0], code_recv.at[q], rows[0]
        ).wait_recv()
    for n, peer in enumerate(blocks):
        sends.append(
            remote(code_tab.at[b], code_tab.at[b], cfwd_send.at[n], cfwd_recv.at[b], peer)
        )
        sends[-1].start()
    cross = rr_ref[...]
    high = cross.astype(bf16)
    low = (cross - high.astype(f32)).astype(bf16)
    lagged = jnp.dot(high, bhi_ref[...], preferred_element_type=f32)
    lagged = lagged + jnp.dot(low, bhi_ref[...], preferred_element_type=f32)
    lagged = lagged + jnp.dot(high, blo_ref[...], preferred_element_type=f32)
    lag_re = lagged[0:256, 0:256] + lagged[256:512, 256:512]
    lag_im = lagged[256:512, 0:256] - lagged[0:256, 256:512]

    lag_rows = lag_ref[pl.ds(2 * b, 2), :].astype(f32)
    dop_rows = dop_ref[pl.ds(2 * b, 2), :].astype(f32)
    tau_cols, nu_cols, surfs = [], [], []
    for c in range(2):
        top = jnp.concatenate(
            [lag_re[(c * 4 + j) * 32 : (c * 4 + j + 1) * 32] for j in range(4)], axis=1
        )
        low_half = jnp.concatenate(
            [lag_im[(c * 4 + j) * 32 : (c * 4 + j + 1) * 32] for j in range(4)], axis=1
        )
        stacked = jnp.concatenate([top, low_half], axis=0)
        high = stacked.astype(bf16)
        low = (stacked - high.astype(f32)).astype(bf16)
        deep = jnp.concatenate([high, high, low], axis=0)
        surf = jnp.dot(mix_ref[...], deep, preferred_element_type=f32)
        surfs.append(surf)
        power = surf * surf
        lag0 = to_column(lag_rows[c : c + 1, :], 16)
        dop0 = to_column(dop_rows[c : c + 1, :], 16)
        offset = (iota((16, 2 * DOPPLER_BINS), 1) // 2).astype(f32) - dop0
        offset = jnp.where(offset < 0.0, offset + DOPPLER_BINS, offset)
        inside = jnp.where(offset < WD, 1.0, 0.0).astype(f32)
        weights = jnp.concatenate([inside, inside * offset], axis=0)
        weights = weights.astype(bf16)
        high = power.astype(bf16)
        low = (power - high.astype(f32)).astype(bf16)
        sums = jnp.dot(
            jnp.concatenate([weights, weights], axis=1),
            jnp.concatenate([high, low], axis=0),
            preferred_element_type=f32,
        )
        step = iota((16, LAG_COUNT), 1).astype(f32) - lag0
        within = (step >= 0.0) & (step < WL)
        plain = jnp.where(within, sums[0:16], 0.0)
        norm = 1.0 / (WL * WD)
        total = jnp.sum(plain, axis=1, keepdims=True) * norm + 1e-06
        lag_mean = jnp.sum(plain * step, axis=1, keepdims=True) * norm / total
        dop_mean = (
            jnp.sum(jnp.where(within, sums[16:32], 0.0), axis=1, keepdims=True) * norm / total
        )
        tau_cols.append((lag0 + lag_mean) * (16.0 / LAG_COUNT))
        nu_cols.append((dop0 + dop_mean) * (4.0 / DOPPLER_BINS))
    tau = jnp.concatenate(tau_cols, axis=0)
    nu = jnp.concatenate(nu_cols, axis=0)
    pay_ref[0] = jnp.sum(
        jnp.where(placed, jnp.where(first, tau, nu), 0.0), axis=0, keepdims=True
    )

    own_pay = pltpu.make_async_copy(pay_ref.at[0], table.at[b, r], own_sem.at[0])
    own_pay.start()
    for n, peer in enumerate(rows):
        sends.append(
            remote(pay_ref.at[0], table.at[b, r], pay_send.at[n], pay_recv.at[r], peer)
        )
        sends[-1].start()
    for t in range(TB):
        surf_ref[t] = jnp.concatenate(
            [surfs[0][8 * t : 8 * t + 8], surfs[1][8 * t : 8 * t + 8]], axis=0
        ).astype(bf16)
    own_surf = pltpu.make_async_copy(surf_ref.at[b], land_ref.at[b], own_sem.at[1])
    own_surf.start()
    for n, peer in enumerate(blocks):
        sends.append(
            remote(surf_ref.at[peer[1]], land_ref.at[b], surf_send.at[n], surf_recv.at[b], peer)
        )
        sends[-1].start()
    own_pay.wait()
    for copy in sends[: -len(blocks)]:
        copy.wait_send()
    sends = sends[-len(blocks) :]
    for _, t in blocks:
        remote(
            code_tab.at[t], code_tab.at[t], cfwd_send.at[0], cfwd_recv.at[t], blocks[0]
        ).wait_recv()
    rpos_copy.wait()
    for k in range(TB):
        for q in range(RX):
            code_ref[k, q : q + 1, :] = code_tab[k, q]
    prepare(code_ref, rpos_ref, prep_ref, small_ref)
    outs = [
        pltpu.make_async_copy(prep_ref, prep, own_sem.at[2]),
        pltpu.make_async_copy(small_ref, small, own_sem.at[3]),
        pltpu.make_async_copy(wide_ref, amb, own_sem.at[4]),
    ]
    outs[0].start()
    outs[1].start()
    part = r // 8
    spot = lax.rem(r, 8)
    for count, dp in enumerate((0, 1, 3, 2)):
        there = lax.rem(part + dp, 4)
        for dx in range(8):
            if dp == 0 and dx == 0:
                continue
            q = there * 8 + lax.rem(spot + dx, 8)
            remote(
                pay_ref.at[0], table.at[b, q], pay_send.at[0], pay_recv.at[q], rows[0]
            ).wait_recv()
        chunk = table.at[b, pl.ds(there * 8, 8)]
        for n, peer in enumerate(blocks):
            sends.append(
                remote(chunk, chunk, fwd_send.at[n, count], fwd_recv.at[b, there], peer)
            )
            sends[-1].start()
    own_surf.wait()
    for _, t in blocks:
        remote(
            surf_ref.at[t], land_ref.at[t], surf_send.at[0], surf_recv.at[t], blocks[0]
        ).wait_recv()
    for t in range(TB):
        value = land_ref[t].astype(f32)
        for c in range(2):
            for d in range(4):
                row = 8 * c + 2 * d
                wide_ref[d, 2 * t + c] = value[row : row + 2, :]
    outs[2].start()
    for _, t in blocks:
        for z in range(4):
            chunk = table.at[t, pl.ds(z * 8, 8)]
            remote(chunk, chunk, fwd_send.at[0, 0], fwd_recv.at[t, z], blocks[0]).wait_recv()
    for copy in outs:
        copy.wait()
    for copy in sends:
        copy.wait_send()


def front(raw, scl, lag, dop, own, em, start, steps, consts, rpos):
    any_spec = pl.BlockSpec(memory_space=pl.ANY)
    dma = pltpu.SemaphoreType.DMA
    operands = (raw, scl, lag, dop, own, em, start, steps, *consts)
    n = 3 * TB - 1
    return pl.pallas_call(
        front_kernel,
        out_shape=(
            pltpu.VMEM((4, 16, 2, LAG_COUNT), f32),
            pltpu.VMEM((TB, RX, 1, 128), f32),
            pltpu.VMEM((PLANES, RX, 128), f32),
            pltpu.VMEM((11, 8, 128), f32),
        ),
        in_specs=[any_spec] * (len(operands) + 1),
        out_specs=(any_spec,) * 4,
        scratch_shapes=[pltpu.VMEM(x.shape, x.dtype) for x in operands]
        + [
            pltpu.VMEM(rpos.shape, f32),
            pltpu.VMEM((8, SEG), bf16),
            pltpu.VMEM((3 * TB, 8, SEG), bf16),
            pltpu.VMEM((3 * TB,) + scl.shape, f32),
            pltpu.VMEM((3, 40, FFT), f32),
            pltpu.VMEM((3, 40, FFT), f32),
            pltpu.VMEM((512, FFT), f32),
            pltpu.VMEM((TB, 16, LAG_COUNT), bf16),
            pltpu.VMEM((2, 1, 128), f32),
            pltpu.VMEM((TB, RX, 1, 128), f32),
            pltpu.VMEM((TB, RX, 128), f32),
            pltpu.VMEM((PLANES, RX, 128), f32),
            pltpu.VMEM((11, 8, 128), f32),
            pltpu.VMEM((TB, 16, LAG_COUNT), bf16),
            pltpu.VMEM((4, 16, 2, LAG_COUNT), f32),
            dma((len(operands),)),
            dma((n,)), dma((3 * TB,)), dma((n,)), dma((3 * TB,)),
            dma((RX - 1,)), dma((RX,)), dma((TB - 1,)), dma((TB,)),
            dma((RX - 1,)), dma((RX,)), dma((TB - 1, 4)), dma((TB, 4)),
            dma((TB - 1,)), dma((TB,)), dma((6,)),
        ],
        compiler_params=pltpu.CompilerParams(collective_id=0, has_side_effects=True),
        name="front",
    )(*operands, rpos)


def solve_three(normals, rhs, damp_term):
    entry_xx = normals[0] + damp_term
    entry_xy = normals[1]
    entry_xz = normals[2]
    entry_yy = normals[3] + damp_term
    entry_yz = normals[4]
    entry_zz = normals[5] + damp_term
    minor_xx = entry_yy * entry_zz - entry_yz * entry_yz
    minor_xy = entry_xz * entry_yz - entry_xy * entry_zz
    minor_xz = entry_xy * entry_yz - entry_xz * entry_yy
    minor_yy = entry_xx * entry_zz - entry_xz * entry_xz
    minor_yz = entry_xy * entry_xz - entry_xx * entry_yz
    minor_zz = entry_xx * entry_yy - entry_xy * entry_xy
    inverse = 1.0 / (entry_xx * minor_xx + entry_xy * minor_xy + entry_xz * minor_xz)
    step_x = minor_xx * rhs[0] + minor_xy * rhs[1] + minor_xz * rhs[2]
    step_y = minor_xy * rhs[0] + minor_yy * rhs[1] + minor_yz * rhs[2]
    step_z = minor_xz * rhs[0] + minor_yz * rhs[1] + minor_zz * rhs[2]
    return [step_x * inverse, step_y * inverse, step_z * inverse]


def per_receiver(x, shift):
    return pltpu.roll(x, (RX - shift) % RX, 0)


ROW_OF = (0, 4, 2, 6)
OWNER_AT = (0, 0, 2, 2, 1, 1, 3, 3)
PAIRS = ((0, 0), (0, 1), (0, 2), (1, 1), (1, 2), (2, 2))
EMIT, MASK, LIVE, LATE, FIRST, SECOND, SPREAD, JAC, PLANES = 0, 4, 16, 20, 24, 27, 39, 43, 55
START, STEPS, DAMP, NORMAL = 0, 3, 4, 5


def fold(parts):
    total, second, third, fourth = parts
    first = total - second - third - fourth
    sub = iota((8, 128), 0)
    upper = sub < 4
    early = lax.rem(sub, 4) < 2

    def halves(x, y):
        return jnp.where(upper, x, y) + pltpu.roll(jnp.where(upper, y, x), 4, 0)

    one = halves(first, second)
    two = halves(third, fourth)
    rows = jnp.where(early, one + pltpu.roll(one, 6, 0), two + pltpu.roll(two, 2, 0))
    rows = rows + pltpu.roll(rows, 7, 0)
    rows = rows + pltpu.roll(rows, 32, 1)
    return rows + pltpu.roll(rows, 64, 1)


def add_to(acc, key, masks, quantity):
    terms = [quantity] + [mask * quantity for mask in masks]
    old = acc[key]
    acc[key] = terms if old is None else [x + y for x, y in zip(old, terms)]


def spread_rows(rows):
    return [jnp.broadcast_to(rows[at : at + 1], (8, 128)) for at in ROW_OF]


def tile_of(k, h):
    return k, slice(8 * h, 8 * h + 8)


def at_peak(which, rows):
    value = rows[0]
    for is_it, row in zip(which, rows[1:]):
        value = jnp.where(is_it, row, value)
    return value


def tile_ranges(prep_ref, which, position, k, part):
    sq_first = None
    firsts, seconds = [], []
    for comp in range(3):
        at = at_peak(which, position[comp])
        d_first = at - prep_ref[FIRST + comp, part, :]
        d_second = at - prep_ref[SECOND + 4 * comp + k, part, :]
        if sq_first is None:
            sq_first = 1.0 + d_first * d_first
            sq_second = 1.0 + d_second * d_second
        else:
            sq_first = sq_first + d_first * d_first
            sq_second = sq_second + d_second * d_second
        firsts.append(d_first)
        seconds.append(d_second)
    inv_first = lax.rsqrt(sq_first)
    inv_second = lax.rsqrt(sq_second)
    spread = sq_second * inv_second - sq_first * inv_first
    live = prep_ref[LIVE + k, part, :]
    inv_first = inv_first * live
    inv_second = inv_second * live
    return spread, [seconds[i] * inv_second - firsts[i] * inv_first for i in range(3)]


def tile_masks(prep_ref, k, part):
    emit = prep_ref[EMIT + k, part, :]
    which = [emit == float(e) for e in (1, 2, 3)]
    return which, [prep_ref[MASK + 4 * e + k, part, :] for e in range(3)]


def turned_by_slot(x):
    low = iota((RX, 128), 1) < 64
    base = jnp.where(low, x, jnp.concatenate([x[8:], x[:8]], axis=0))
    return [per_receiver(base, shift) for shift in range(1, 9)]


def prepare(code_ref, rpos_ref, prep_ref, small_ref):
    lane = iota((RX, 128), 1)
    low = lane < 64
    own_lane = iota((RX, 128), 0) == lax.rem(lane, RX)
    for k in range(4):
        code = jnp.where(low, code_ref[k], pltpu.roll(code_ref[k + 4], 64, 1))
        late = code > 4.5
        prep_ref[LATE + k] = jnp.where(late, 1.0, 0.0)
        emitter = jnp.where(late, code - 5.0, code - 1.0)
        prep_ref[EMIT + k] = emitter
        prep_ref[LIVE + k] = jnp.where(code > 0.5, 1.0, 0.0)
        for e in range(3):
            prep_ref[MASK + 4 * e + k] = jnp.where(emitter == e + 1.0, 1.0, 0.0)
    info = code_ref[0]

    def owner_row(col):
        value = jnp.sum(jnp.where(lane == col, info, 0.0), axis=1, keepdims=True)
        return jnp.sum(jnp.where(own_lane, value, 0.0), axis=0, keepdims=True)

    def owner_rows(base):
        made = [owner_row(base + e) for e in range(4)]
        return jnp.concatenate([made[e] for e in OWNER_AT], axis=0)

    position = [owner_rows(64 + 4 * k) for k in range(3)]
    for k in range(3):
        small_ref[START + k] = position[k]
    small_ref[STEPS] = owner_rows(76)
    eye = iota((RX, RX), 0) == iota((RX, RX), 1)
    for comp in range(3):
        column = jnp.sum(
            jnp.where(eye, rpos_ref[comp : comp + 1, :], 0.0), axis=1, keepdims=True
        )
        column = jnp.broadcast_to(column, (RX, 128))
        prep_ref[FIRST + comp] = column
        turned = turned_by_slot(column)
        for k in range(4):
            prep_ref[SECOND + 4 * comp + k] = jnp.where(
                prep_ref[LATE + k] > 0.5, turned[2 * k + 1], turned[2 * k]
            )
    acc = {key: None for key in range(7)}
    position = [spread_rows(rows) for rows in position]
    for k, part in [tile_of(k, h) for k in range(4) for h in range(4)]:
        which, masks = tile_masks(prep_ref, k, part)
        spread, jac = tile_ranges(prep_ref, which, position, k, part)
        prep_ref[SPREAD + k, part, :] = spread
        for i in range(3):
            prep_ref[JAC + 4 * i + k, part, :] = jac[i]
        for key, (x, y) in enumerate(PAIRS):
            add_to(acc, key, masks, jac[x] * jac[y])
        add_to(acc, 6, masks, prep_ref[LIVE + k, part, :])
    for key in range(6):
        small_ref[NORMAL + key] = fold(acc[key])
    small_ref[DAMP] = 2.0 * (fold(acc[6]) + 1.0)


def solve_kernel(
    table_ref, prep_ref, small_ref, amb_in, pos_ref, vel_ref, bias_ref, amb_out,
    out_sem, tau_ref, nu_ref, spread_ref, jac_ref, left_ref,
):
    amb_copy = pltpu.make_async_copy(amb_in, amb_out, out_sem.at[0])
    amb_copy.start()
    lane = iota((RX, 128), 1)
    low = lane < 64
    for k in range(4):
        a0, a1 = table_ref[k], table_ref[k + 4]
        tau_ref[k] = jnp.where(low, a0, pltpu.roll(a1, 64, 1))
        nu_ref[k] = jnp.where(low, pltpu.roll(a0, 64, 1), a1)
        spread_ref[k] = prep_ref[SPREAD + k]
        for i in range(3):
            jac_ref[i, k] = prep_ref[JAC + 4 * i + k]
    position = [small_ref[START + k] for k in range(3)]
    normals = [small_ref[NORMAL + key] for key in range(6)]
    zero = jnp.zeros((8, 128), f32)
    tiles = [tile_of(k, h) for k in range(4) for h in range(4)]

    def gn_step(step, carry):
        position, speed, bias, normals = carry
        moving = step.astype(f32) < small_ref[STEPS]
        damp = small_ref[DAMP]
        turned = turned_by_slot(bias)
        acc = {key: None for key in range(3)}
        for k in range(4):
            late = prep_ref[LATE + k] > 0.5
            left_ref[k] = tau_ref[k] + bias - jnp.where(late, turned[2 * k + 1], turned[2 * k])
        for k, part in tiles:
            masks = [prep_ref[MASK + 4 * e + k, part, :] for e in range(3)]
            resid = left_ref[k, part, :] - spread_ref[k, part, :]
            for i in range(3):
                add_to(acc, i, masks, jac_ref[i, k, part, :] * resid)
        moved = solve_three(normals, [fold(acc[i]) for i in range(3)], damp)
        position = [position[i] + jnp.where(moving, moved[i], 0.0) for i in range(3)]
        at_rows = [spread_rows(rows) for rows in position]
        speed_rows = [spread_rows(rows) for rows in speed]
        acc = {key: None for key in range(9)}
        for k, part in tiles:
            which, masks = tile_masks(prep_ref, k, part)
            spread, jac = tile_ranges(prep_ref, which, at_rows, k, part)
            spread_ref[k, part, :] = spread
            for i in range(3):
                jac_ref[i, k, part, :] = jac[i]
            rate = nu_ref[k, part, :]
            for i in range(3):
                rate = rate - at_peak(which, speed_rows[i]) * jac[i]
            for key, (x, y) in enumerate(PAIRS):
                add_to(acc, key, masks, jac[x] * jac[y])
            for i in range(3):
                add_to(acc, 6 + i, masks, jac[i] * rate)
        nested, whole = None, None
        for k in (3, 2, 1, 0):
            gap = left_ref[k] - spread_ref[k]
            every = prep_ref[LIVE + k] * gap
            late = prep_ref[LATE + k] * gap
            term = every - late + pltpu.roll(late, 1, 0)
            nested = term if nested is None else term + pltpu.roll(nested, 2, 0)
            whole = every if whole is None else whole + every
        nested = pltpu.roll(nested, 1, 0)
        shifted = jnp.concatenate([nested[24:], nested[:24]], axis=0)
        total = jnp.sum(jnp.where(low, nested, shifted) - whole, axis=1, keepdims=True)
        normals = [fold(acc[key]) for key in range(6)]
        swung = solve_three(normals, [fold(acc[6 + i]) for i in range(3)], damp)
        speed = [speed[i] + jnp.where(moving, swung[i], 0.0) for i in range(3)]
        bias = bias + jnp.broadcast_to(total, (RX, 128)) / (3.0 * 16 * RX)
        return position, speed, bias, normals

    carry = (position, [zero, zero, zero], jnp.zeros((RX, 128), f32), normals)
    position, speed, bias, _ = lax.fori_loop(0, GN_MAX, gn_step, carry)
    r = lax.axis_index("rx")
    lane8 = iota((8, 128), 1)
    sub8 = iota((8, 128), 0)
    spot = lax.rem(sub8, 4) + jnp.where(sub8 >= 4, 1, 0)
    used = (lax.rem(sub8, 2) == 0) & (lane8 == spot)
    for out, value in ((pos_ref, position), (vel_ref, speed)):
        for i in range(3):
            column = jnp.sum(jnp.where(lane8 == r, value[i], 0.0), axis=1, keepdims=True)
            row = jnp.sum(jnp.where(used, column, 0.0), axis=0, keepdims=True)
            out[i : i + 1, :] = row[:, 0:4]
    bias_row = jnp.sum(jnp.where(iota((RX, 128), 0) == lane, bias, 0.0), axis=0, keepdims=True)
    bias_ref[...] = bias_row[:, 0:RX]
    amb_copy.wait()


def solve(table, prep, small, amb):
    any_spec = pl.BlockSpec(memory_space=pl.ANY)
    vmem = pl.BlockSpec(memory_space=pltpu.VMEM)
    block = (4, RX, 128)
    return pl.pallas_call(
        solve_kernel,
        out_shape=(
            jax.ShapeDtypeStruct((3, 4), f32),
            jax.ShapeDtypeStruct((3, 4), f32),
            jax.ShapeDtypeStruct((1, RX), f32),
            jax.ShapeDtypeStruct((4, 16, 2, LAG_COUNT), f32),
        ),
        in_specs=[vmem, vmem, vmem, any_spec],
        out_specs=(vmem, vmem, vmem, any_spec),
        scratch_shapes=[
            pltpu.SemaphoreType.DMA((1,)),
            pltpu.VMEM(block, f32),
            pltpu.VMEM(block, f32),
            pltpu.VMEM(block, f32),
            pltpu.VMEM((3,) + block, f32),
            pltpu.VMEM(block, f32),
        ],
        compiler_params=pltpu.CompilerParams(vmem_limit_bytes=12 << 20),
        name="solve",
    )(table, prep, small, amb)


def local(
    consts, raw_samples, block_scales, lag_window_start, doppler_window_start,
    peak_owner, peak_emitter, gn_steps, receiver_pos, emitter_start,
):
    amb, table, prep, small = front(
        raw_samples, block_scales, lag_window_start, doppler_window_start,
        peak_owner.reshape(2, 16), peak_emitter, emitter_start, gn_steps.reshape(1, 4), consts,
        receiver_pos,
    )
    position, speed, bias, amb = solve(
        table.reshape(TB, RX, 128), prep, small, amb
    )
    return amb, position, speed, bias.reshape(RX)


def solution(mesh):
    placed = (
        P("rx", None, "tb"),
        P("rx", "tb"),
        P("rx", None),
        P("rx", None),
        P(("rx", "tb"), None, None),
        P(("rx", "tb"), None),
        P("rx"),
        P(),
        P(None, "rx"),
    )
    return jax.shard_map(
        functools.partial(local, tables()),
        mesh=mesh,
        in_specs=placed,
        out_specs=(P("tb", "rx", None, None), P(None, "rx"), P(None, "rx"), P()),
        check_vma=False,
    )
```

```python
import functools
import math

import jax
import jax.numpy as jnp
import numpy as np
from jax import lax
from jax.experimental import pallas as pl
from jax.experimental.pallas import tpu as pltpu
from jax.sharding import PartitionSpec as P

SEG = 256
DOPPLER_BINS = 32
LAG_COUNT = 1024
WL = 16
WD = 4
GN_MAX = 6
RX = 32
TB = 8
FFT = 512
SAMPLES = SEG * DOPPLER_BINS

MESH = pl.DeviceIdType.MESH
f32 = jnp.float32
bf16 = jnp.bfloat16


def split_pair(table):
    high = table.astype(bf16)
    low = (table - high.astype(np.float64)).astype(bf16)
    return high, low


def tables():
    turn = 2.0 * np.pi / FFT
    t_f = np.arange(SEG)[:, None] * np.arange(FFT)[None, :] % FFT * turn
    forward = np.concatenate([np.cos(t_f), np.sin(t_f)], axis=1)
    backward = np.concatenate([np.cos(t_f.T), np.sin(t_f.T)], axis=1)
    d_m = (
        np.arange(DOPPLER_BINS)[:, None] * np.arange(DOPPLER_BINS)[None, :] % DOPPLER_BINS
    ) * (2.0 * np.pi / DOPPLER_BINS)
    mix = np.block([[np.cos(d_m), np.sin(d_m)], [-np.sin(d_m), np.cos(d_m)]])
    mix = mix.reshape(2, DOPPLER_BINS, -1).transpose(1, 0, 2).reshape(2 * DOPPLER_BINS, -1)
    mix = mix / (FFT * math.sqrt(SAMPLES))
    mix_high, mix_low = split_pair(mix)
    deep_mix = np.concatenate([mix_high, mix_low, mix_high], axis=1)
    return split_pair(forward) + split_pair(backward) + (deep_mix,)


def iota(shape, dim):
    return lax.broadcasted_iota(jnp.int32, shape, dim)


def to_column(row, count):
    eye = iota((count, count), 0) == iota((count, count), 1)
    return jnp.sum(jnp.where(eye, row, 0.0), axis=1, keepdims=True)


def peer_lists(r, b):
    rows = [(lax.rem(r + d, RX), b) for d in range(1, RX)]
    blocks = [(r, lax.rem(b + d, TB)) for d in range(1, TB)]
    return rows, blocks


def remote(src, dst, send_sem, recv_sem, peer):
    return pltpu.make_async_remote_copy(
        src_ref=src,
        dst_ref=dst,
        send_sem=send_sem,
        recv_sem=recv_sem,
        device_id={"rx": peer[0], "tb": peer[1]},
        device_id_type=MESH,
    )


def front_kernel(
    raw_in, scl_in, lag_in, dop_in, own_in, em_in, start_in, steps_in,
    fhi_in, flo_in, bhi_in, blo_in, mix_in, rpos_in,
    amb, table, prep, small,
    raw_ref, scl_ref, lag_ref, dop_ref, own_ref, em_ref, start_ref, steps_ref,
    fhi_ref, flo_ref, bhi_ref, blo_ref, mix_ref,
    rpos_ref, pad_ref, block_ref, raw_all, scl_all, re_ref, im_ref, rr_ref, surf_ref, pay_ref,
    code_tab, code_ref, prep_ref, small_ref, land_ref, wide_ref,
    load_sem, raw_send, raw_recv, scl_send, scl_recv, code_send, code_recv,
    cfwd_send, cfwd_recv, pay_send, pay_recv, fwd_send, fwd_recv, surf_send, surf_recv, own_sem,
):
    r = lax.axis_index("rx")
    b = lax.axis_index("tb")
    barrier = pltpu.get_barrier_semaphore()
    rows, blocks = peer_lists(r, b)

    def signal(peer):
        pl.semaphore_signal(
            barrier, inc=1, device_id={"rx": peer[0], "tb": peer[1]}, device_id_type=MESH
        )

    sources = [
        (lax.rem(r + 2 * b + i, RX), lax.rem(b + d, TB)) for d in range(1, TB) for i in (1, 2)
    ]
    for peer in sources + rows + blocks:
        signal(peer)

    loads = [
        pltpu.make_async_copy(src, dst, load_sem.at[n])
        for n, (src, dst) in enumerate(
            (
                (raw_in, raw_ref), (scl_in, scl_ref), (own_in, own_ref), (em_in, em_ref),
                (start_in, start_ref), (steps_in, steps_ref), (lag_in, lag_ref),
                (dop_in, dop_ref), (fhi_in, fhi_ref), (flo_in, flo_ref), (bhi_in, bhi_ref),
                (blo_in, blo_ref), (mix_in, mix_ref),
            )
        )
    ]
    for copy in loads:
        copy.start()
    rpos_copy = pltpu.make_async_copy(rpos_in, rpos_ref, own_sem.at[2])
    rpos_copy.start()
    for copy in loads[:2]:
        copy.wait()
    own_raw = raw_ref[0].astype(f32)
    block_ref[...] = jnp.concatenate(
        [own_raw[k : k + 1, SEG * s : SEG * s + SEG] for k in range(2) for s in range(4)], axis=0
    ).astype(bf16)
    pad_ref[...] = jnp.zeros((1, 128), f32)
    pad_ref[:, 0:4] = scl_ref[...]


    pl.semaphore_wait(barrier, len(sources) + len(rows) + len(blocks))

    targets = [(r, p, 0) for _, p in blocks]
    targets += [(lax.rem(r + RX - 2 * t - i, RX), t, i) for t in range(TB) for i in (1, 2)]
    for to_r, to_b, i in targets:
        place = i * TB + b
        for src, dst, ss, rs in (
            (block_ref, raw_all, raw_send, raw_recv),
            (pad_ref, scl_all, scl_send, scl_recv),
        ):
            remote(src, dst.at[place], ss, rs, (to_r, to_b)).start()
    pltpu.make_async_copy(block_ref, raw_all.at[b], raw_recv).start()
    pltpu.make_async_copy(pad_ref, scl_all.at[b], scl_recv).start()
    for copy in loads[2:8]:
        copy.wait()
    owner = jnp.concatenate(
        [to_column(own_ref[c : c + 1, :].astype(f32), 16) for c in range(2)], axis=0
    )
    code = jnp.concatenate(
        [to_column(em_ref[c : c + 1, :].astype(f32), 16) + (1.0 + 4.0 * c) for c in range(2)],
        axis=0,
    )
    p_row = iota((32, 32), 0)
    p_col = iota((32, 32), 1)
    owner_row = jnp.sum(jnp.where(p_row == p_col, owner, 0.0), axis=0, keepdims=True)
    same = (owner_row == owner) & (p_col < p_row)
    rank = jnp.sum(jnp.where(same, 1.0, 0.0), axis=1, keepdims=True)
    lane = iota((32, 128), 1)
    slot = lax.rem(lane, 64).astype(f32)
    placed = (rank * 32.0 + owner) == slot
    first = lane < 64
    codes = jnp.sum(jnp.where(placed & first, code, 0.0), axis=0, keepdims=True)
    lane1 = iota((1, 128), 1)
    for k in range(3):
        for e in range(4):
            codes = jnp.where(lane1 == 64 + 4 * k + e, start_ref[k : k + 1, e : e + 1], codes)
    for e in range(4):
        codes = jnp.where(lane1 == 76 + e, steps_ref[0:1, e : e + 1].astype(f32), codes)
    pay_ref[1] = codes
    pltpu.make_async_copy(pay_ref.at[1], code_tab.at[b, r], code_recv).start()
    for peer in rows:
        remote(pay_ref.at[1], code_tab.at[b, r], code_send, code_recv, peer).start()
    peer = blocks[0]
    remote(raw_all, raw_all, raw_send, raw_recv, peer).wait_recv()
    remote(scl_all, scl_all, scl_send, scl_recv, peer).wait_recv()
    for copy in loads[8:]:
        copy.wait()

    raw = raw_all[...].astype(f32).reshape(3 * TB * 8, SEG).astype(bf16)
    spec = jnp.dot(raw, fhi_ref[...], preferred_element_type=f32)
    spec = spec + jnp.dot(raw, flo_ref[...], preferred_element_type=f32)
    cos_part = spec[:, :FFT].reshape(3 * TB, 8, FFT)
    sin_part = spec[:, FFT:].reshape(3 * TB, 8, FFT)
    sub = iota((1, 8, 1), 1)
    sign = jnp.where(sub < 4, 1.0, -1.0).astype(f32)
    pick = iota((1, 8, 128), 2) == lax.rem(iota((1, 8, 128), 1), 4)
    scale = jnp.sum(jnp.where(pick, scl_all[...], 0.0), axis=2, keepdims=True)
    pieces = (cos_part + sign * pltpu.roll(sin_part, 4, 1)) * scale
    for i in range(3):
        re_ref[i, 32:40, :] = jnp.zeros((8, FFT), f32)
        im_ref[i, 32:40, :] = jnp.zeros((8, FFT), f32)
        for t in range(TB):
            re_ref[i, 4 * t : 4 * t + 4, :] = pieces[i * TB + t, 0:4, :]
            im_ref[i, 4 * t : 4 * t + 4, :] = pieces[i * TB + t, 4:8, :]
    near_re = re_ref[0, 0:32, :]
    near_im = im_ref[0, 0:32, :]
    alt = jnp.where(lax.rem(iota((1, FFT), 1), 2) == 0, 1.0, -1.0).astype(f32)
    for c in range(2):
        for j in range(4):
            far_re = re_ref[c + 1, j : j + 32, :] + alt * re_ref[c + 1, j + 1 : j + 33, :]
            far_im = im_ref[c + 1, j : j + 32, :] + alt * im_ref[c + 1, j + 1 : j + 33, :]
            row = (c * 4 + j) * 32
            rr_ref[row : row + 32, :] = near_re * far_re + near_im * far_im
            rr_ref[256 + row : 288 + row, :] = near_im * far_re - near_re * far_im
    remote(code_tab.at[b], code_tab.at[b], code_send, code_recv, blocks[0]).wait_recv()
    for peer in blocks:
        remote(code_tab.at[b], code_tab.at[b], cfwd_send, cfwd_recv.at[b], peer).start()
    cross = rr_ref[...]
    high = cross.astype(bf16)
    low = (cross - high.astype(f32)).astype(bf16)
    lagged = jnp.dot(high, bhi_ref[...], preferred_element_type=f32)
    lagged = lagged + jnp.dot(low, bhi_ref[...], preferred_element_type=f32)
    lagged = lagged + jnp.dot(high, blo_ref[...], preferred_element_type=f32)
    lag_re = lagged[0:256, 0:256] + lagged[256:512, 256:512]
    lag_im = lagged[256:512, 0:256] - lagged[0:256, 256:512]

    lag_rows = lag_ref[pl.ds(2 * b, 2), :].astype(f32)
    dop_rows = dop_ref[pl.ds(2 * b, 2), :].astype(f32)
    tau_cols, nu_cols, surfs = [], [], []
    for c in range(2):
        top = jnp.concatenate(
            [lag_re[(c * 4 + j) * 32 : (c * 4 + j + 1) * 32] for j in range(4)], axis=1
        )
        low_half = jnp.concatenate(
            [lag_im[(c * 4 + j) * 32 : (c * 4 + j + 1) * 32] for j in range(4)], axis=1
        )
        stacked = jnp.concatenate([top, low_half], axis=0)
        high = stacked.astype(bf16)
        low = (stacked - high.astype(f32)).astype(bf16)
        deep = jnp.concatenate([high, high, low], axis=0)
        surf = jnp.dot(mix_ref[...], deep, preferred_element_type=f32)
        surfs.append(surf)
        power = surf * surf
        lag0 = to_column(lag_rows[c : c + 1, :], 16)
        dop0 = to_column(dop_rows[c : c + 1, :], 16)
        offset = (iota((16, 2 * DOPPLER_BINS), 1) // 2).astype(f32) - dop0
        offset = jnp.where(offset < 0.0, offset + DOPPLER_BINS, offset)
        inside = jnp.where(offset < WD, 1.0, 0.0).astype(f32)
        weights = jnp.concatenate([inside, inside * offset], axis=0)
        weights = weights.astype(bf16)
        high = power.astype(bf16)
        low = (power - high.astype(f32)).astype(bf16)
        sums = jnp.dot(
            jnp.concatenate([weights, weights], axis=1),
            jnp.concatenate([high, low], axis=0),
            preferred_element_type=f32,
        )
        step = iota((16, LAG_COUNT), 1).astype(f32) - lag0
        within = (step >= 0.0) & (step < WL)
        plain = jnp.where(within, sums[0:16], 0.0)
        norm = 1.0 / (WL * WD)
        total = jnp.sum(plain, axis=1, keepdims=True) * norm + 1e-06
        lag_mean = jnp.sum(plain * step, axis=1, keepdims=True) * norm / total
        dop_mean = (
            jnp.sum(jnp.where(within, sums[16:32], 0.0), axis=1, keepdims=True) * norm / total
        )
        tau_cols.append((lag0 + lag_mean) * (16.0 / LAG_COUNT))
        nu_cols.append((dop0 + dop_mean) * (4.0 / DOPPLER_BINS))
    tau = jnp.concatenate(tau_cols, axis=0)
    nu = jnp.concatenate(nu_cols, axis=0)
    pay_ref[0] = jnp.sum(
        jnp.where(placed, jnp.where(first, tau, nu), 0.0), axis=0, keepdims=True
    )

    part = r // 8
    pltpu.make_async_copy(pay_ref.at[0], table.at[b, r], pay_recv.at[part]).start()
    for peer in rows:
        remote(pay_ref.at[0], table.at[b, r], pay_send, pay_recv.at[part], peer).start()
    for t in range(TB):
        surf_ref[t] = jnp.concatenate(
            [surfs[0][8 * t : 8 * t + 8], surfs[1][8 * t : 8 * t + 8]], axis=0
        ).astype(bf16)
    own_surf = pltpu.make_async_copy(surf_ref.at[b], land_ref.at[b], own_sem.at[1])
    own_surf.start()
    for peer in blocks:
        remote(surf_ref.at[peer[1]], land_ref.at[b], surf_send, surf_recv.at[b], peer).start()
    some = blocks[0]
    near = (raw_all.at[pl.ds(0, 3 * TB - 1)], raw_send), (scl_all.at[pl.ds(0, 3 * TB - 1)], scl_send)
    row_set = code_tab.at[0, pl.ds(0, RX - 1)]
    for ref, sem in near + ((row_set, code_send), (row_set, pay_send)):
        remote(ref, ref, sem, raw_recv, some).wait_send()
    for _, t in blocks:
        remote(code_tab.at[t], code_tab.at[t], cfwd_send, cfwd_recv.at[t], some).wait_recv()
    rpos_copy.wait()
    for k in range(TB):
        for q in range(RX):
            code_ref[k, q : q + 1, :] = code_tab[k, q]
    prepare(code_ref, rpos_ref, prep_ref, small_ref)
    outs = [
        pltpu.make_async_copy(prep_ref, prep, own_sem.at[2]),
        pltpu.make_async_copy(small_ref, small, own_sem.at[3]),
        pltpu.make_async_copy(wide_ref, amb, own_sem.at[4]),
    ]
    outs[0].start()
    outs[1].start()
    for dp in (0, 1, 3, 2):
        there = lax.rem(part + dp, 4)
        chunk = table.at[b, pl.ds(there * 8, 8)]
        remote(chunk, chunk, pay_send, pay_recv.at[there], some).wait_recv()
        for peer in blocks:
            remote(chunk, chunk, fwd_send, fwd_recv.at[b], peer).start()
    own_surf.wait()
    for _, t in blocks:
        remote(surf_ref.at[t], land_ref.at[t], surf_send, surf_recv.at[t], some).wait_recv()
    for t in range(TB):
        value = land_ref[t].astype(f32)
        for c in range(2):
            for d in range(4):
                row = 8 * c + 2 * d
                wide_ref[d, 2 * t + c] = value[row : row + 2, :]
    outs[2].start()
    for ref, sem in ((code_tab, cfwd_send), (surf_ref, surf_send)):
        ref = ref.at[pl.ds(0, TB - 1)]
        remote(ref, ref, sem, raw_recv, some).wait_send()
    for _, t in blocks:
        remote(table.at[t], table.at[t], fwd_send, fwd_recv.at[t], some).wait_recv()
    for copy in outs:
        copy.wait()
    ref = table.at[pl.ds(0, TB - 1)]
    remote(ref, ref, fwd_send, raw_recv, some).wait_send()


def front(raw, scl, lag, dop, own, em, start, steps, consts, rpos):
    any_spec = pl.BlockSpec(memory_space=pl.ANY)
    dma = pltpu.SemaphoreType.DMA
    operands = (raw, scl, lag, dop, own, em, start, steps, *consts)
    return pl.pallas_call(
        front_kernel,
        out_shape=(
            pltpu.VMEM((4, 16, 2, LAG_COUNT), f32),
            pltpu.VMEM((TB, RX, 1, 128), f32),
            pltpu.VMEM((PLANES, RX, 128), f32),
            pltpu.VMEM((11, 8, 128), f32),
        ),
        in_specs=[any_spec] * (len(operands) + 1),
        out_specs=(any_spec,) * 4,
        scratch_shapes=[pltpu.VMEM(x.shape, x.dtype) for x in operands]
        + [
            pltpu.VMEM(rpos.shape, f32),
            pltpu.VMEM((1, 128), f32),
            pltpu.VMEM((8, SEG), bf16),
            pltpu.VMEM((3 * TB, 8, SEG), bf16),
            pltpu.VMEM((3 * TB, 1, 128), f32),
            pltpu.VMEM((3, 40, FFT), f32),
            pltpu.VMEM((3, 40, FFT), f32),
            pltpu.VMEM((512, FFT), f32),
            pltpu.VMEM((TB, 16, LAG_COUNT), bf16),
            pltpu.VMEM((2, 1, 128), f32),
            pltpu.VMEM((TB, RX, 1, 128), f32),
            pltpu.VMEM((TB, RX, 128), f32),
            pltpu.VMEM((PLANES, RX, 128), f32),
            pltpu.VMEM((11, 8, 128), f32),
            pltpu.VMEM((TB, 16, LAG_COUNT), bf16),
            pltpu.VMEM((4, 16, 2, LAG_COUNT), f32),
            dma((len(operands),)),
            dma, dma, dma, dma, dma, dma, dma, dma((TB,)), dma, dma((4,)), dma, dma((TB,)),
            dma, dma((TB,)), dma((6,)),
        ],
        compiler_params=pltpu.CompilerParams(collective_id=0, has_side_effects=True),
        name="front",
    )(*operands, rpos)


def solve_three(normals, rhs, damp_term):
    entry_xx = normals[0] + damp_term
    entry_xy = normals[1]
    entry_xz = normals[2]
    entry_yy = normals[3] + damp_term
    entry_yz = normals[4]
    entry_zz = normals[5] + damp_term
    minor_xx = entry_yy * entry_zz - entry_yz * entry_yz
    minor_xy = entry_xz * entry_yz - entry_xy * entry_zz
    minor_xz = entry_xy * entry_yz - entry_xz * entry_yy
    minor_yy = entry_xx * entry_zz - entry_xz * entry_xz
    minor_yz = entry_xy * entry_xz - entry_xx * entry_yz
    minor_zz = entry_xx * entry_yy - entry_xy * entry_xy
    inverse = 1.0 / (entry_xx * minor_xx + entry_xy * minor_xy + entry_xz * minor_xz)
    step_x = minor_xx * rhs[0] + minor_xy * rhs[1] + minor_xz * rhs[2]
    step_y = minor_xy * rhs[0] + minor_yy * rhs[1] + minor_yz * rhs[2]
    step_z = minor_xz * rhs[0] + minor_yz * rhs[1] + minor_zz * rhs[2]
    return [step_x * inverse, step_y * inverse, step_z * inverse]


def per_receiver(x, shift):
    return pltpu.roll(x, (RX - shift) % RX, 0)


ROW_OF = (0, 4, 2, 6)
OWNER_AT = (0, 0, 2, 2, 1, 1, 3, 3)
PAIRS = ((0, 0), (0, 1), (0, 2), (1, 1), (1, 2), (2, 2))
EMIT, MASK, LIVE, LATE, FIRST, SECOND, SPREAD, JAC, PLANES = 0, 4, 16, 20, 24, 27, 39, 43, 55
START, STEPS, DAMP, NORMAL = 0, 3, 4, 5


def fold(parts):
    total, second, third, fourth = parts
    first = total - second - third - fourth
    sub = iota((8, 128), 0)
    upper = sub < 4
    early = lax.rem(sub, 4) < 2

    def halves(x, y):
        return jnp.where(upper, x, y) + pltpu.roll(jnp.where(upper, y, x), 4, 0)

    one = halves(first, second)
    two = halves(third, fourth)
    rows = jnp.where(early, one + pltpu.roll(one, 6, 0), two + pltpu.roll(two, 2, 0))
    rows = rows + pltpu.roll(rows, 7, 0)
    rows = rows + pltpu.roll(rows, 32, 1)
    return rows + pltpu.roll(rows, 64, 1)


def add_to(acc, key, masks, quantity):
    terms = [quantity] + [mask * quantity for mask in masks]
    old = acc[key]
    acc[key] = terms if old is None else [x + y for x, y in zip(old, terms)]


def spread_rows(rows):
    return [jnp.broadcast_to(rows[at : at + 1], (8, 128)) for at in ROW_OF]


def tile_of(k, h):
    return k, slice(8 * h, 8 * h + 8)


def at_peak(which, rows):
    value = rows[0]
    for is_it, row in zip(which, rows[1:]):
        value = jnp.where(is_it, row, value)
    return value


def tile_ranges(prep_ref, which, position, k, part):
    sq_first = None
    firsts, seconds = [], []
    for comp in range(3):
        at = at_peak(which, position[comp])
        d_first = at - prep_ref[FIRST + comp, part, :]
        d_second = at - prep_ref[SECOND + 4 * comp + k, part, :]
        if sq_first is None:
            sq_first = 1.0 + d_first * d_first
            sq_second = 1.0 + d_second * d_second
        else:
            sq_first = sq_first + d_first * d_first
            sq_second = sq_second + d_second * d_second
        firsts.append(d_first)
        seconds.append(d_second)
    inv_first = lax.rsqrt(sq_first)
    inv_second = lax.rsqrt(sq_second)
    spread = sq_second * inv_second - sq_first * inv_first
    live = prep_ref[LIVE + k, part, :]
    inv_first = inv_first * live
    inv_second = inv_second * live
    return spread, [seconds[i] * inv_second - firsts[i] * inv_first for i in range(3)]


def tile_masks(prep_ref, k, part):
    emit = prep_ref[EMIT + k, part, :]
    which = [emit == float(e) for e in (1, 2, 3)]
    return which, [prep_ref[MASK + 4 * e + k, part, :] for e in range(3)]


def turned_by_slot(x):
    low = iota((RX, 128), 1) < 64
    base = jnp.where(low, x, jnp.concatenate([x[8:], x[:8]], axis=0))
    return [per_receiver(base, shift) for shift in range(1, 9)]


def prepare(code_ref, rpos_ref, prep_ref, small_ref):
    lane = iota((RX, 128), 1)
    low = lane < 64
    own_lane = iota((RX, 128), 0) == lax.rem(lane, RX)
    for k in range(4):
        code = jnp.where(low, code_ref[k], pltpu.roll(code_ref[k + 4], 64, 1))
        late = code > 4.5
        prep_ref[LATE + k] = jnp.where(late, 1.0, 0.0)
        emitter = jnp.where(late, code - 5.0, code - 1.0)
        prep_ref[EMIT + k] = emitter
        prep_ref[LIVE + k] = jnp.where(code > 0.5, 1.0, 0.0)
        for e in range(3):
            prep_ref[MASK + 4 * e + k] = jnp.where(emitter == e + 1.0, 1.0, 0.0)
    info = code_ref[0]

    def owner_row(col):
        value = jnp.sum(jnp.where(lane == col, info, 0.0), axis=1, keepdims=True)
        return jnp.sum(jnp.where(own_lane, value, 0.0), axis=0, keepdims=True)

    def owner_rows(base):
        made = [owner_row(base + e) for e in range(4)]
        return jnp.concatenate([made[e] for e in OWNER_AT], axis=0)

    position = [owner_rows(64 + 4 * k) for k in range(3)]
    for k in range(3):
        small_ref[START + k] = position[k]
    small_ref[STEPS] = owner_rows(76)
    eye = iota((RX, RX), 0) == iota((RX, RX), 1)
    for comp in range(3):
        column = jnp.sum(
            jnp.where(eye, rpos_ref[comp : comp + 1, :], 0.0), axis=1, keepdims=True
        )
        column = jnp.broadcast_to(column, (RX, 128))
        prep_ref[FIRST + comp] = column
        turned = turned_by_slot(column)
        for k in range(4):
            prep_ref[SECOND + 4 * comp + k] = jnp.where(
                prep_ref[LATE + k] > 0.5, turned[2 * k + 1], turned[2 * k]
            )
    acc = {key: None for key in range(7)}
    position = [spread_rows(rows) for rows in position]
    for k, part in [tile_of(k, h) for k in range(4) for h in range(4)]:
        which, masks = tile_masks(prep_ref, k, part)
        spread, jac = tile_ranges(prep_ref, which, position, k, part)
        prep_ref[SPREAD + k, part, :] = spread
        for i in range(3):
            prep_ref[JAC + 4 * i + k, part, :] = jac[i]
        for key, (x, y) in enumerate(PAIRS):
            add_to(acc, key, masks, jac[x] * jac[y])
        add_to(acc, 6, masks, prep_ref[LIVE + k, part, :])
    for key in range(6):
        small_ref[NORMAL + key] = fold(acc[key])
    small_ref[DAMP] = 2.0 * (fold(acc[6]) + 1.0)


def solve_kernel(
    table_ref, prep_ref, small_ref, amb_in, pos_ref, vel_ref, bias_ref, amb_out,
    out_sem, tau_ref, nu_ref, spread_ref, jac_ref, left_ref,
):
    amb_copy = pltpu.make_async_copy(amb_in, amb_out, out_sem.at[0])
    amb_copy.start()
    lane = iota((RX, 128), 1)
    low = lane < 64
    for k in range(4):
        a0, a1 = table_ref[k], table_ref[k + 4]
        tau_ref[k] = jnp.where(low, a0, pltpu.roll(a1, 64, 1))
        nu_ref[k] = jnp.where(low, pltpu.roll(a0, 64, 1), a1)
        spread_ref[k] = prep_ref[SPREAD + k]
        for i in range(3):
            jac_ref[i, k] = prep_ref[JAC + 4 * i + k]
    position = [small_ref[START + k] for k in range(3)]
    normals = [small_ref[NORMAL + key] for key in range(6)]
    zero = jnp.zeros((8, 128), f32)
    tiles = [tile_of(k, h) for k in range(4) for h in range(4)]

    def gn_step(step, carry):
        position, speed, bias, normals = carry
        moving = step.astype(f32) < small_ref[STEPS]
        damp = small_ref[DAMP]
        turned = turned_by_slot(bias)
        acc = {key: None for key in range(3)}
        for k in range(4):
            late = prep_ref[LATE + k] > 0.5
            left_ref[k] = tau_ref[k] + bias - jnp.where(late, turned[2 * k + 1], turned[2 * k])
        for k, part in tiles:
            masks = [prep_ref[MASK + 4 * e + k, part, :] for e in range(3)]
            resid = left_ref[k, part, :] - spread_ref[k, part, :]
            for i in range(3):
                add_to(acc, i, masks, jac_ref[i, k, part, :] * resid)
        moved = solve_three(normals, [fold(acc[i]) for i in range(3)], damp)
        position = [position[i] + jnp.where(moving, moved[i], 0.0) for i in range(3)]
        at_rows = [spread_rows(rows) for rows in position]
        speed_rows = [spread_rows(rows) for rows in speed]
        acc = {key: None for key in range(9)}
        for k, part in tiles:
            which, masks = tile_masks(prep_ref, k, part)
            spread, jac = tile_ranges(prep_ref, which, at_rows, k, part)
            spread_ref[k, part, :] = spread
            for i in range(3):
                jac_ref[i, k, part, :] = jac[i]
            rate = nu_ref[k, part, :]
            for i in range(3):
                rate = rate - at_peak(which, speed_rows[i]) * jac[i]
            for key, (x, y) in enumerate(PAIRS):
                add_to(acc, key, masks, jac[x] * jac[y])
            for i in range(3):
                add_to(acc, 6 + i, masks, jac[i] * rate)
        nested, whole = None, None
        for k in (3, 2, 1, 0):
            gap = left_ref[k] - spread_ref[k]
            every = prep_ref[LIVE + k] * gap
            late = prep_ref[LATE + k] * gap
            term = every - late + pltpu.roll(late, 1, 0)
            nested = term if nested is None else term + pltpu.roll(nested, 2, 0)
            whole = every if whole is None else whole + every
        nested = pltpu.roll(nested, 1, 0)
        shifted = jnp.concatenate([nested[24:], nested[:24]], axis=0)
        total = jnp.sum(jnp.where(low, nested, shifted) - whole, axis=1, keepdims=True)
        normals = [fold(acc[key]) for key in range(6)]
        swung = solve_three(normals, [fold(acc[6 + i]) for i in range(3)], damp)
        speed = [speed[i] + jnp.where(moving, swung[i], 0.0) for i in range(3)]
        bias = bias + jnp.broadcast_to(total, (RX, 128)) / (3.0 * 16 * RX)
        return position, speed, bias, normals

    carry = (position, [zero, zero, zero], jnp.zeros((RX, 128), f32), normals)
    position, speed, bias, _ = lax.fori_loop(0, GN_MAX, gn_step, carry)
    r = lax.axis_index("rx")
    lane8 = iota((8, 128), 1)
    sub8 = iota((8, 128), 0)
    spot = lax.rem(sub8, 4) + jnp.where(sub8 >= 4, 1, 0)
    used = (lax.rem(sub8, 2) == 0) & (lane8 == spot)
    for out, value in ((pos_ref, position), (vel_ref, speed)):
        for i in range(3):
            column = jnp.sum(jnp.where(lane8 == r, value[i], 0.0), axis=1, keepdims=True)
            row = jnp.sum(jnp.where(used, column, 0.0), axis=0, keepdims=True)
            out[i : i + 1, :] = row[:, 0:4]
    bias_row = jnp.sum(jnp.where(iota((RX, 128), 0) == lane, bias, 0.0), axis=0, keepdims=True)
    bias_ref[...] = bias_row[:, 0:RX]
    amb_copy.wait()


def solve(table, prep, small, amb):
    any_spec = pl.BlockSpec(memory_space=pl.ANY)
    vmem = pl.BlockSpec(memory_space=pltpu.VMEM)
    block = (4, RX, 128)
    return pl.pallas_call(
        solve_kernel,
        out_shape=(
            jax.ShapeDtypeStruct((3, 4), f32),
            jax.ShapeDtypeStruct((3, 4), f32),
            jax.ShapeDtypeStruct((1, RX), f32),
            jax.ShapeDtypeStruct((4, 16, 2, LAG_COUNT), f32),
        ),
        in_specs=[vmem, vmem, vmem, any_spec],
        out_specs=(vmem, vmem, vmem, any_spec),
        scratch_shapes=[
            pltpu.SemaphoreType.DMA((1,)),
            pltpu.VMEM(block, f32),
            pltpu.VMEM(block, f32),
            pltpu.VMEM(block, f32),
            pltpu.VMEM((3,) + block, f32),
            pltpu.VMEM(block, f32),
        ],
        compiler_params=pltpu.CompilerParams(vmem_limit_bytes=12 << 20),
        name="solve",
    )(table, prep, small, amb)


def local(
    consts, raw_samples, block_scales, lag_window_start, doppler_window_start,
    peak_owner, peak_emitter, gn_steps, receiver_pos, emitter_start,
):
    amb, table, prep, small = front(
        raw_samples, block_scales, lag_window_start, doppler_window_start,
        peak_owner.reshape(2, 16), peak_emitter, emitter_start, gn_steps.reshape(1, 4), consts,
        receiver_pos,
    )
    position, speed, bias, amb = solve(
        table.reshape(TB, RX, 128), prep, small, amb
    )
    return amb, position, speed, bias.reshape(RX)


def solution(mesh):
    placed = (
        P("rx", None, "tb"),
        P("rx", "tb"),
        P("rx", None),
        P("rx", None),
        P(("rx", "tb"), None, None),
        P(("rx", "tb"), None),
        P("rx"),
        P(),
        P(None, "rx"),
    )
    return jax.shard_map(
        functools.partial(local, tables()),
        mesh=mesh,
        in_specs=placed,
        out_specs=(P("tb", "rx", None, None), P(None, "rx"), P(None, "rx"), P()),
        check_vma=False,
    )
```

```python
import functools
import math

import jax
import jax.numpy as jnp
import numpy as np
from jax import lax
from jax.experimental import pallas as pl
from jax.experimental.pallas import tpu as pltpu
from jax.sharding import PartitionSpec as P

SEG = 256
DOPPLER_BINS = 32
LAG_COUNT = 1024
WL = 16
WD = 4
GN_MAX = 6
RX = 32
TB = 8
FFT = 512
SAMPLES = SEG * DOPPLER_BINS

MESH = pl.DeviceIdType.MESH
f32 = jnp.float32
bf16 = jnp.bfloat16


def split_pair(table):
    high = table.astype(bf16)
    low = (table - high.astype(np.float64)).astype(bf16)
    return high, low


def tables():
    turn = 2.0 * np.pi / FFT
    t_f = np.arange(SEG)[:, None] * np.arange(FFT)[None, :] % FFT * turn
    forward = np.concatenate([np.cos(t_f), np.sin(t_f)], axis=1)
    backward = np.concatenate([np.cos(t_f.T), np.sin(t_f.T)], axis=1)
    d_m = (
        np.arange(DOPPLER_BINS)[:, None] * np.arange(DOPPLER_BINS)[None, :] % DOPPLER_BINS
    ) * (2.0 * np.pi / DOPPLER_BINS)
    mix = np.block([[np.cos(d_m), np.sin(d_m)], [-np.sin(d_m), np.cos(d_m)]])
    mix = mix.reshape(2, DOPPLER_BINS, -1).transpose(1, 0, 2).reshape(2 * DOPPLER_BINS, -1)
    mix = mix / (FFT * math.sqrt(SAMPLES))
    mix_high, mix_low = split_pair(mix)
    deep_mix = np.concatenate([mix_high, mix_low, mix_high], axis=1)
    deep_forward = np.concatenate(split_pair(forward), axis=0)
    back_high, back_low = split_pair(backward)
    deep_backward = np.concatenate([back_high, back_low], axis=0)
    return deep_forward, deep_backward, deep_mix


def iota(shape, dim):
    return lax.broadcasted_iota(jnp.int32, shape, dim)


def to_column(row, count):
    eye = iota((count, count), 0) == iota((count, count), 1)
    return jnp.sum(jnp.where(eye, row, 0.0), axis=1, keepdims=True)


def peer_lists(r, b):
    rows = [(lax.rem(r + d, RX), b) for d in range(1, RX)]
    blocks = [(r, lax.rem(b + d, TB)) for d in range(1, TB)]
    return rows, blocks


def remote(src, dst, send_sem, recv_sem, peer):
    return pltpu.make_async_remote_copy(
        src_ref=src,
        dst_ref=dst,
        send_sem=send_sem,
        recv_sem=recv_sem,
        device_id={"rx": peer[0], "tb": peer[1]},
        device_id_type=MESH,
    )


def front_kernel(
    raw_in, scl_in, lag_in, dop_in, own_in, em_in, start_in, steps_in,
    fwd_in, back_in, mix_in, rpos_in,
    amb, table, prep, small,
    raw_ref, scl_ref, lag_ref, dop_ref, own_ref, em_ref, start_ref, steps_ref,
    fwd_ref, back_ref, mix_ref,
    rpos_ref, pad_ref, block_ref, raw_all, scl_all, re_ref, im_ref, rr_ref, surf_ref, pay_ref,
    code_tab, code_ref, prep_ref, small_ref, land_ref, wide_ref,
    load_sem, raw_send, raw_recv, scl_send, scl_recv, code_send, code_recv,
    cfwd_send, cfwd_recv, pay_send, pay_recv, fwd_send, fwd_recv, surf_send, surf_recv, own_sem,
):
    r = lax.axis_index("rx")
    b = lax.axis_index("tb")
    barrier = pltpu.get_barrier_semaphore()
    rows, blocks = peer_lists(r, b)

    def signal(peer):
        pl.semaphore_signal(
            barrier, inc=1, device_id={"rx": peer[0], "tb": peer[1]}, device_id_type=MESH
        )

    sources = [
        (lax.rem(r + 2 * b + i, RX), lax.rem(b + d, TB)) for d in range(1, TB) for i in (1, 2)
    ]
    for peer in sources + rows + blocks:
        signal(peer)

    loads = [
        pltpu.make_async_copy(src, dst, load_sem.at[n])
        for n, (src, dst) in enumerate(
            (
                (raw_in, raw_ref), (scl_in, scl_ref), (own_in, own_ref), (em_in, em_ref),
                (start_in, start_ref), (steps_in, steps_ref), (lag_in, lag_ref),
                (dop_in, dop_ref), (fwd_in, fwd_ref), (back_in, back_ref), (mix_in, mix_ref),
            )
        )
    ]
    for copy in loads:
        copy.start()
    rpos_copy = pltpu.make_async_copy(rpos_in, rpos_ref, own_sem.at[2])
    rpos_copy.start()
    for copy in loads[:2]:
        copy.wait()
    own_raw = raw_ref[0].astype(f32)
    block_ref[...] = jnp.concatenate(
        [own_raw[k : k + 1, SEG * s : SEG * s + SEG] for k in range(2) for s in range(4)], axis=0
    ).astype(bf16)
    pad_ref[...] = jnp.zeros((1, 128), f32)
    pad_ref[:, 0:4] = scl_ref[...]


    pl.semaphore_wait(barrier, len(sources) + len(rows) + len(blocks))

    targets = [(r, p, 0) for _, p in blocks]
    targets += [(lax.rem(r + RX - 2 * t - i, RX), t, i) for t in range(TB) for i in (1, 2)]
    for to_r, to_b, i in targets:
        place = i * TB + b
        for src, dst, ss, rs in (
            (block_ref, raw_all, raw_send, raw_recv),
            (pad_ref, scl_all, scl_send, scl_recv),
        ):
            remote(src, dst.at[place], ss, rs, (to_r, to_b)).start()
    pltpu.make_async_copy(block_ref, raw_all.at[b], raw_recv).start()
    pltpu.make_async_copy(pad_ref, scl_all.at[b], scl_recv).start()
    for copy in loads[2:8]:
        copy.wait()
    owner = jnp.concatenate(
        [to_column(own_ref[c : c + 1, :].astype(f32), 16) for c in range(2)], axis=0
    )
    code = jnp.concatenate(
        [to_column(em_ref[c : c + 1, :].astype(f32), 16) + (1.0 + 4.0 * c) for c in range(2)],
        axis=0,
    )
    p_row = iota((32, 32), 0)
    p_col = iota((32, 32), 1)
    owner_row = jnp.sum(jnp.where(p_row == p_col, owner, 0.0), axis=0, keepdims=True)
    same = (owner_row == owner) & (p_col < p_row)
    rank = jnp.sum(jnp.where(same, 1.0, 0.0), axis=1, keepdims=True)
    lane = iota((32, 128), 1)
    slot = lax.rem(lane, 64).astype(f32)
    placed = (rank * 32.0 + owner) == slot
    first = lane < 64
    codes = jnp.sum(jnp.where(placed & first, code, 0.0), axis=0, keepdims=True)
    lane1 = iota((1, 128), 1)
    for k in range(3):
        for e in range(4):
            codes = jnp.where(lane1 == 64 + 4 * k + e, start_ref[k : k + 1, e : e + 1], codes)
    for e in range(4):
        codes = jnp.where(lane1 == 76 + e, steps_ref[0:1, e : e + 1].astype(f32), codes)
    pay_ref[1] = codes
    pltpu.make_async_copy(pay_ref.at[1], code_tab.at[b, r], code_recv).start()
    for peer in rows:
        remote(pay_ref.at[1], code_tab.at[b, r], code_send, code_recv, peer).start()
    peer = blocks[0]
    remote(raw_all, raw_all, raw_send, raw_recv, peer).wait_recv()
    remote(scl_all, scl_all, scl_send, scl_recv, peer).wait_recv()
    for copy in loads[8:]:
        copy.wait()

    raw = raw_all[...].astype(f32).reshape(3 * TB * 8, SEG).astype(bf16)
    spec = jnp.dot(raw, fwd_ref[0:256, :], preferred_element_type=f32)
    spec = spec + jnp.dot(raw, fwd_ref[256:512, :], preferred_element_type=f32)
    cos_part = spec[:, :FFT].reshape(3 * TB, 8, FFT)
    sin_part = spec[:, FFT:].reshape(3 * TB, 8, FFT)
    sub = iota((1, 8, 1), 1)
    sign = jnp.where(sub < 4, 1.0, -1.0).astype(f32)
    pick = iota((1, 8, 128), 2) == lax.rem(iota((1, 8, 128), 1), 4)
    scale = jnp.sum(jnp.where(pick, scl_all[...], 0.0), axis=2, keepdims=True)
    pieces = (cos_part + sign * pltpu.roll(sin_part, 4, 1)) * scale
    for i in range(3):
        re_ref[i, 32:40, :] = jnp.zeros((8, FFT), f32)
        im_ref[i, 32:40, :] = jnp.zeros((8, FFT), f32)
        for t in range(TB):
            re_ref[i, 4 * t : 4 * t + 4, :] = pieces[i * TB + t, 0:4, :]
            im_ref[i, 4 * t : 4 * t + 4, :] = pieces[i * TB + t, 4:8, :]
    near_re = re_ref[0, 0:32, :]
    near_im = im_ref[0, 0:32, :]
    alt = jnp.where(lax.rem(iota((1, FFT), 1), 2) == 0, 1.0, -1.0).astype(f32)
    for c in range(2):
        for j in range(4):
            far_re = re_ref[c + 1, j : j + 32, :] + alt * re_ref[c + 1, j + 1 : j + 33, :]
            far_im = im_ref[c + 1, j : j + 32, :] + alt * im_ref[c + 1, j + 1 : j + 33, :]
            row = (c * 4 + j) * 32
            rr_ref[row : row + 32, :] = near_re * far_re + near_im * far_im
            rr_ref[256 + row : 288 + row, :] = near_im * far_re - near_re * far_im
    remote(code_tab.at[b], code_tab.at[b], code_send, code_recv, blocks[0]).wait_recv()
    for peer in blocks:
        remote(code_tab.at[b], code_tab.at[b], cfwd_send, cfwd_recv, peer).start()
    cross = rr_ref[...]
    high = cross.astype(bf16)
    low = (cross - high.astype(f32)).astype(bf16)
    lagged = jnp.dot(high, back_ref[0:512, :], preferred_element_type=f32)
    lagged = lagged + jnp.dot(low, back_ref[0:512, :], preferred_element_type=f32)
    lagged = lagged + jnp.dot(high, back_ref[512:1024, :], preferred_element_type=f32)
    lag_re = lagged[0:256, 0:256] + lagged[256:512, 256:512]
    lag_im = lagged[256:512, 0:256] - lagged[0:256, 256:512]

    lag_rows = lag_ref[pl.ds(2 * b, 2), :].astype(f32)
    dop_rows = dop_ref[pl.ds(2 * b, 2), :].astype(f32)
    tau_cols, nu_cols, surfs = [], [], []
    for c in range(2):
        top = jnp.concatenate(
            [lag_re[(c * 4 + j) * 32 : (c * 4 + j + 1) * 32] for j in range(4)], axis=1
        )
        low_half = jnp.concatenate(
            [lag_im[(c * 4 + j) * 32 : (c * 4 + j + 1) * 32] for j in range(4)], axis=1
        )
        stacked = jnp.concatenate([top, low_half], axis=0)
        high = stacked.astype(bf16)
        low = (stacked - high.astype(f32)).astype(bf16)
        deep = jnp.concatenate([high, high, low], axis=0)
        surf = jnp.dot(mix_ref[...], deep, preferred_element_type=f32)
        surfs.append(surf)
        power = surf * surf
        lag0 = to_column(lag_rows[c : c + 1, :], 16)
        dop0 = to_column(dop_rows[c : c + 1, :], 16)
        offset = (iota((16, 2 * DOPPLER_BINS), 1) // 2).astype(f32) - dop0
        offset = jnp.where(offset < 0.0, offset + DOPPLER_BINS, offset)
        inside = jnp.where(offset < WD, 1.0, 0.0).astype(f32)
        weights = jnp.concatenate([inside, inside * offset], axis=0)
        weights = weights.astype(bf16)
        high = power.astype(bf16)
        low = (power - high.astype(f32)).astype(bf16)
        sums = jnp.dot(
            jnp.concatenate([weights, weights], axis=1),
            jnp.concatenate([high, low], axis=0),
            preferred_element_type=f32,
        )
        step = iota((16, LAG_COUNT), 1).astype(f32) - lag0
        within = (step >= 0.0) & (step < WL)
        plain = jnp.where(within, sums[0:16], 0.0)
        norm = 1.0 / (WL * WD)
        total = jnp.sum(plain, axis=1, keepdims=True) * norm + 1e-06
        lag_mean = jnp.sum(plain * step, axis=1, keepdims=True) * norm / total
        dop_mean = (
            jnp.sum(jnp.where(within, sums[16:32], 0.0), axis=1, keepdims=True) * norm / total
        )
        tau_cols.append((lag0 + lag_mean) * (16.0 / LAG_COUNT))
        nu_cols.append((dop0 + dop_mean) * (4.0 / DOPPLER_BINS))
    tau = jnp.concatenate(tau_cols, axis=0)
    nu = jnp.concatenate(nu_cols, axis=0)
    pay_ref[0] = jnp.sum(
        jnp.where(placed, jnp.where(first, tau, nu), 0.0), axis=0, keepdims=True
    )

    part = r // 8
    pltpu.make_async_copy(pay_ref.at[0], table.at[b, r], pay_recv.at[part]).start()
    for peer in rows:
        remote(pay_ref.at[0], table.at[b, r], pay_send, pay_recv.at[part], peer).start()
    for t in range(TB):
        surf_ref[t] = jnp.concatenate(
            [surfs[0][8 * t : 8 * t + 8], surfs[1][8 * t : 8 * t + 8]], axis=0
        ).astype(bf16)
    pltpu.make_async_copy(surf_ref.at[b], land_ref.at[b], surf_recv).start()
    for peer in blocks:
        remote(surf_ref.at[peer[1]], land_ref.at[b], surf_send, surf_recv, peer).start()
    some = blocks[0]
    near = (raw_all.at[pl.ds(0, 3 * TB - 1)], raw_send), (scl_all.at[pl.ds(0, 3 * TB - 1)], scl_send)
    row_set = code_tab.at[0, pl.ds(0, RX - 1)]
    for ref, sem in near + ((row_set, code_send), (row_set, pay_send)):
        remote(ref, ref, sem, raw_recv, some).wait_send()
    ref = code_tab.at[pl.ds(0, TB - 1)]
    remote(ref, ref, cfwd_send, cfwd_recv, some).wait_recv()
    rpos_copy.wait()
    for k in range(TB):
        for q in range(RX):
            code_ref[k, q : q + 1, :] = code_tab[k, q]
    prepare(code_ref, rpos_ref, prep_ref, small_ref)
    outs = [
        pltpu.make_async_copy(prep_ref, prep, own_sem.at[2]),
        pltpu.make_async_copy(small_ref, small, own_sem.at[3]),
        pltpu.make_async_copy(wide_ref, amb, own_sem.at[4]),
    ]
    outs[0].start()
    outs[1].start()
    for dp in (0, 1, 3, 2):
        there = lax.rem(part + dp, 4)
        chunk = table.at[b, pl.ds(there * 8, 8)]
        remote(chunk, chunk, pay_send, pay_recv.at[there], some).wait_recv()
        for peer in blocks:
            remote(chunk, chunk, fwd_send, fwd_recv, peer).start()
    remote(surf_ref, land_ref, surf_send, surf_recv, some).wait_recv()
    for t in range(TB):
        value = land_ref[t].astype(f32)
        for c in range(2):
            for d in range(4):
                row = 8 * c + 2 * d
                wide_ref[d, 2 * t + c] = value[row : row + 2, :]
    outs[2].start()
    for ref, sem in ((code_tab, cfwd_send), (surf_ref, surf_send)):
        ref = ref.at[pl.ds(0, TB - 1)]
        remote(ref, ref, sem, raw_recv, some).wait_send()
    for copy in outs:
        copy.wait()
    ref = table.at[pl.ds(0, TB - 1)]
    remote(ref, ref, fwd_send, fwd_recv, some).wait()


def front(raw, scl, lag, dop, own, em, start, steps, consts, rpos):
    any_spec = pl.BlockSpec(memory_space=pl.ANY)
    dma = pltpu.SemaphoreType.DMA
    operands = (raw, scl, lag, dop, own, em, start, steps, *consts)
    return pl.pallas_call(
        front_kernel,
        out_shape=(
            pltpu.VMEM((4, 16, 2, LAG_COUNT), f32),
            pltpu.VMEM((TB, RX, 1, 128), f32),
            pltpu.VMEM((PLANES, RX, 128), f32),
            pltpu.VMEM((11, 8, 128), f32),
        ),
        in_specs=[any_spec] * (len(operands) + 1),
        out_specs=(any_spec,) * 4,
        scratch_shapes=[pltpu.VMEM(x.shape, x.dtype) for x in operands]
        + [
            pltpu.VMEM(rpos.shape, f32),
            pltpu.VMEM((1, 128), f32),
            pltpu.VMEM((8, SEG), bf16),
            pltpu.VMEM((3 * TB, 8, SEG), bf16),
            pltpu.VMEM((3 * TB, 1, 128), f32),
            pltpu.VMEM((3, 40, FFT), f32),
            pltpu.VMEM((3, 40, FFT), f32),
            pltpu.VMEM((512, FFT), f32),
            pltpu.VMEM((TB, 16, LAG_COUNT), bf16),
            pltpu.VMEM((2, 1, 128), f32),
            pltpu.VMEM((TB, RX, 1, 128), f32),
            pltpu.VMEM((TB, RX, 128), f32),
            pltpu.VMEM((PLANES, RX, 128), f32),
            pltpu.VMEM((11, 8, 128), f32),
            pltpu.VMEM((TB, 16, LAG_COUNT), bf16),
            pltpu.VMEM((4, 16, 2, LAG_COUNT), f32),
            dma((len(operands),)),
            dma, dma, dma, dma, dma, dma, dma, dma, dma, dma((4,)), dma, dma, dma, dma, dma((5,)),
        ],
        compiler_params=pltpu.CompilerParams(collective_id=0, has_side_effects=True),
        name="front",
    )(*operands, rpos)


def solve_three(normals, rhs, damp_term):
    entry_xx = normals[0] + damp_term
    entry_xy = normals[1]
    entry_xz = normals[2]
    entry_yy = normals[3] + damp_term
    entry_yz = normals[4]
    entry_zz = normals[5] + damp_term
    minor_xx = entry_yy * entry_zz - entry_yz * entry_yz
    minor_xy = entry_xz * entry_yz - entry_xy * entry_zz
    minor_xz = entry_xy * entry_yz - entry_xz * entry_yy
    minor_yy = entry_xx * entry_zz - entry_xz * entry_xz
    minor_yz = entry_xy * entry_xz - entry_xx * entry_yz
    minor_zz = entry_xx * entry_yy - entry_xy * entry_xy
    inverse = 1.0 / (entry_xx * minor_xx + entry_xy * minor_xy + entry_xz * minor_xz)
    step_x = minor_xx * rhs[0] + minor_xy * rhs[1] + minor_xz * rhs[2]
    step_y = minor_xy * rhs[0] + minor_yy * rhs[1] + minor_yz * rhs[2]
    step_z = minor_xz * rhs[0] + minor_yz * rhs[1] + minor_zz * rhs[2]
    return [step_x * inverse, step_y * inverse, step_z * inverse]


def per_receiver(x, shift):
    return pltpu.roll(x, (RX - shift) % RX, 0)


ROW_OF = (0, 4, 2, 6)
OWNER_AT = (0, 0, 2, 2, 1, 1, 3, 3)
FULL = ((0, 1, 2), (1, 3, 4), (2, 4, 5))
PAIRS = ((0, 0), (0, 1), (0, 2), (1, 1), (1, 2), (2, 2))
EMIT, MASK, LIVE, LATE, FIRST, SECOND, SPREAD, JAC, PLANES = 0, 4, 16, 20, 24, 27, 39, 43, 55
START, STEPS, DAMP, NORMAL = 0, 3, 4, 5


def fold(parts):
    total, second, third, fourth = parts
    first = total - second - third - fourth
    sub = iota((8, 128), 0)
    upper = sub < 4
    early = lax.rem(sub, 4) < 2

    def halves(x, y):
        return jnp.where(upper, x, y) + pltpu.roll(jnp.where(upper, y, x), 4, 0)

    one = halves(first, second)
    two = halves(third, fourth)
    rows = jnp.where(early, one + pltpu.roll(one, 6, 0), two + pltpu.roll(two, 2, 0))
    rows = rows + pltpu.roll(rows, 7, 0)
    rows = rows + pltpu.roll(rows, 32, 1)
    return rows + pltpu.roll(rows, 64, 1)


def add_to(acc, key, masks, quantity):
    terms = [quantity] + [mask * quantity for mask in masks]
    old = acc[key]
    acc[key] = terms if old is None else [x + y for x, y in zip(old, terms)]


def spread_rows(rows):
    return [jnp.broadcast_to(rows[at : at + 1], (8, 128)) for at in ROW_OF]


def tile_of(k, h):
    return k, slice(8 * h, 8 * h + 8)


def at_peak(which, rows):
    value = rows[0]
    for is_it, row in zip(which, rows[1:]):
        value = jnp.where(is_it, row, value)
    return value


def tile_ranges(prep_ref, which, position, k, part):
    sq_first = None
    firsts, seconds = [], []
    for comp in range(3):
        at = at_peak(which, position[comp])
        d_first = at - prep_ref[FIRST + comp, part, :]
        d_second = at - prep_ref[SECOND + 4 * comp + k, part, :]
        if sq_first is None:
            sq_first = 1.0 + d_first * d_first
            sq_second = 1.0 + d_second * d_second
        else:
            sq_first = sq_first + d_first * d_first
            sq_second = sq_second + d_second * d_second
        firsts.append(d_first)
        seconds.append(d_second)
    inv_first = lax.rsqrt(sq_first)
    inv_second = lax.rsqrt(sq_second)
    spread = sq_second * inv_second - sq_first * inv_first
    live = prep_ref[LIVE + k, part, :]
    inv_first = inv_first * live
    inv_second = inv_second * live
    return spread, [seconds[i] * inv_second - firsts[i] * inv_first for i in range(3)]


def tile_masks(prep_ref, k, part):
    emit = prep_ref[EMIT + k, part, :]
    which = [emit == float(e) for e in (1, 2, 3)]
    return which, [prep_ref[MASK + 4 * e + k, part, :] for e in range(3)]


def turned_by_slot(x):
    low = iota((RX, 128), 1) < 64
    base = jnp.where(low, x, jnp.concatenate([x[8:], x[:8]], axis=0))
    return [per_receiver(base, shift) for shift in range(1, 9)]


def prepare(code_ref, rpos_ref, prep_ref, small_ref):
    lane = iota((RX, 128), 1)
    low = lane < 64
    own_lane = iota((RX, 128), 0) == lax.rem(lane, RX)
    for k in range(4):
        code = jnp.where(low, code_ref[k], pltpu.roll(code_ref[k + 4], 64, 1))
        late = code > 4.5
        prep_ref[LATE + k] = jnp.where(late, 1.0, 0.0)
        emitter = jnp.where(late, code - 5.0, code - 1.0)
        prep_ref[EMIT + k] = emitter
        prep_ref[LIVE + k] = jnp.where(code > 0.5, 1.0, 0.0)
        for e in range(3):
            prep_ref[MASK + 4 * e + k] = jnp.where(emitter == e + 1.0, 1.0, 0.0)
    info = code_ref[0]

    def owner_row(col):
        value = jnp.sum(jnp.where(lane == col, info, 0.0), axis=1, keepdims=True)
        return jnp.sum(jnp.where(own_lane, value, 0.0), axis=0, keepdims=True)

    def owner_rows(base):
        made = [owner_row(base + e) for e in range(4)]
        return jnp.concatenate([made[e] for e in OWNER_AT], axis=0)

    position = [owner_rows(64 + 4 * k) for k in range(3)]
    for k in range(3):
        small_ref[START + k] = position[k]
    small_ref[STEPS] = owner_rows(76)
    eye = iota((RX, RX), 0) == iota((RX, RX), 1)
    for comp in range(3):
        column = jnp.sum(
            jnp.where(eye, rpos_ref[comp : comp + 1, :], 0.0), axis=1, keepdims=True
        )
        column = jnp.broadcast_to(column, (RX, 128))
        prep_ref[FIRST + comp] = column
        turned = turned_by_slot(column)
        for k in range(4):
            prep_ref[SECOND + 4 * comp + k] = jnp.where(
                prep_ref[LATE + k] > 0.5, turned[2 * k + 1], turned[2 * k]
            )
    acc = {key: None for key in range(7)}
    position = [spread_rows(rows) for rows in position]
    for k, part in [tile_of(k, h) for k in range(4) for h in range(4)]:
        which, masks = tile_masks(prep_ref, k, part)
        spread, jac = tile_ranges(prep_ref, which, position, k, part)
        prep_ref[SPREAD + k, part, :] = spread
        for i in range(3):
            prep_ref[JAC + 4 * i + k, part, :] = jac[i]
        for key, (x, y) in enumerate(PAIRS):
            add_to(acc, key, masks, jac[x] * jac[y])
        add_to(acc, 6, masks, prep_ref[LIVE + k, part, :])
    for key in range(6):
        small_ref[NORMAL + key] = fold(acc[key])
    small_ref[DAMP] = 2.0 * (fold(acc[6]) + 1.0)


def solve_kernel(
    table_ref, prep_ref, small_ref, amb_in, pos_ref, vel_ref, bias_ref, amb_out,
    out_sem, tau_ref, nu_ref, spread_ref, jac_ref, left_ref,
):
    amb_copy = pltpu.make_async_copy(amb_in, amb_out, out_sem.at[0])
    amb_copy.start()
    lane = iota((RX, 128), 1)
    low = lane < 64
    for k in range(4):
        a0, a1 = table_ref[k], table_ref[k + 4]
        tau_ref[k] = jnp.where(low, a0, pltpu.roll(a1, 64, 1))
        nu_ref[k] = jnp.where(low, pltpu.roll(a0, 64, 1), a1)
        spread_ref[k] = prep_ref[SPREAD + k]
        for i in range(3):
            jac_ref[i, k] = prep_ref[JAC + 4 * i + k]
    position = [small_ref[START + k] for k in range(3)]
    normals = [small_ref[NORMAL + key] for key in range(6)]
    zero = jnp.zeros((8, 128), f32)
    tiles = [tile_of(k, h) for k in range(4) for h in range(4)]

    def gn_step(step, carry):
        position, speed, bias, normals = carry
        moving = step.astype(f32) < small_ref[STEPS]
        damp = small_ref[DAMP]
        turned = turned_by_slot(bias)
        acc = {key: None for key in range(3)}
        for k in range(4):
            late = prep_ref[LATE + k] > 0.5
            left_ref[k] = tau_ref[k] + bias - jnp.where(late, turned[2 * k + 1], turned[2 * k])
        for k, part in tiles:
            masks = [prep_ref[MASK + 4 * e + k, part, :] for e in range(3)]
            resid = left_ref[k, part, :] - spread_ref[k, part, :]
            for i in range(3):
                add_to(acc, i, masks, jac_ref[i, k, part, :] * resid)
        moved = solve_three(normals, [fold(acc[i]) for i in range(3)], damp)
        position = [position[i] + jnp.where(moving, moved[i], 0.0) for i in range(3)]
        at_rows = [spread_rows(rows) for rows in position]
        acc = {key: None for key in range(9)}
        for k, part in tiles:
            which, masks = tile_masks(prep_ref, k, part)
            spread, jac = tile_ranges(prep_ref, which, at_rows, k, part)
            spread_ref[k, part, :] = spread
            for i in range(3):
                jac_ref[i, k, part, :] = jac[i]
            rate = nu_ref[k, part, :]
            for key, (x, y) in enumerate(PAIRS):
                add_to(acc, key, masks, jac[x] * jac[y])
            for i in range(3):
                add_to(acc, 6 + i, masks, jac[i] * rate)
        nested, whole = None, None
        for k in (3, 2, 1, 0):
            gap = left_ref[k] - spread_ref[k]
            every = prep_ref[LIVE + k] * gap
            late = prep_ref[LATE + k] * gap
            term = every - late + pltpu.roll(late, 1, 0)
            nested = term if nested is None else term + pltpu.roll(nested, 2, 0)
            whole = every if whole is None else whole + every
        nested = pltpu.roll(nested, 1, 0)
        shifted = jnp.concatenate([nested[24:], nested[:24]], axis=0)
        total = jnp.sum(jnp.where(low, nested, shifted) - whole, axis=1, keepdims=True)
        normals = [fold(acc[key]) for key in range(6)]
        swung = solve_three(
            normals,
            [
                fold(acc[6 + i])
                - (
                    normals[FULL[i][0]] * speed[0]
                    + normals[FULL[i][1]] * speed[1]
                    + normals[FULL[i][2]] * speed[2]
                )
                for i in range(3)
            ],
            damp,
        )
        speed = [speed[i] + jnp.where(moving, swung[i], 0.0) for i in range(3)]
        bias = bias + jnp.broadcast_to(total, (RX, 128)) / (3.0 * 16 * RX)
        return position, speed, bias, normals

    carry = (position, [zero, zero, zero], jnp.zeros((RX, 128), f32), normals)
    position, speed, bias, _ = lax.fori_loop(0, GN_MAX, gn_step, carry)
    r = lax.axis_index("rx")
    lane8 = iota((8, 128), 1)
    sub8 = iota((8, 128), 0)
    spot = lax.rem(sub8, 4) + jnp.where(sub8 >= 4, 1, 0)
    used = (lax.rem(sub8, 2) == 0) & (lane8 == spot)
    for out, value in ((pos_ref, position), (vel_ref, speed)):
        for i in range(3):
            column = jnp.sum(jnp.where(lane8 == r, value[i], 0.0), axis=1, keepdims=True)
            row = jnp.sum(jnp.where(used, column, 0.0), axis=0, keepdims=True)
            out[i : i + 1, :] = row[:, 0:4]
    bias_row = jnp.sum(jnp.where(iota((RX, 128), 0) == lane, bias, 0.0), axis=0, keepdims=True)
    bias_ref[...] = bias_row[:, 0:RX]
    amb_copy.wait()


def solve(table, prep, small, amb):
    any_spec = pl.BlockSpec(memory_space=pl.ANY)
    vmem = pl.BlockSpec(memory_space=pltpu.VMEM)
    block = (4, RX, 128)
    return pl.pallas_call(
        solve_kernel,
        out_shape=(
            jax.ShapeDtypeStruct((3, 4), f32),
            jax.ShapeDtypeStruct((3, 4), f32),
            jax.ShapeDtypeStruct((1, RX), f32),
            jax.ShapeDtypeStruct((4, 16, 2, LAG_COUNT), f32),
        ),
        in_specs=[vmem, vmem, vmem, any_spec],
        out_specs=(vmem, vmem, vmem, any_spec),
        scratch_shapes=[
            pltpu.SemaphoreType.DMA((1,)),
            pltpu.VMEM(block, f32),
            pltpu.VMEM(block, f32),
            pltpu.VMEM(block, f32),
            pltpu.VMEM((3,) + block, f32),
            pltpu.VMEM(block, f32),
        ],
        compiler_params=pltpu.CompilerParams(vmem_limit_bytes=12 << 20),
        name="solve",
    )(table, prep, small, amb)


def local(
    consts, raw_samples, block_scales, lag_window_start, doppler_window_start,
    peak_owner, peak_emitter, gn_steps, receiver_pos, emitter_start,
):
    amb, table, prep, small = front(
        raw_samples, block_scales, lag_window_start, doppler_window_start,
        peak_owner.reshape(2, 16), peak_emitter, emitter_start, gn_steps.reshape(1, 4), consts,
        receiver_pos,
    )
    position, speed, bias, amb = solve(
        table.reshape(TB, RX, 128), prep, small, amb
    )
    return amb, position, speed, bias.reshape(RX)


def solution(mesh):
    placed = (
        P("rx", None, "tb"),
        P("rx", "tb"),
        P("rx", None),
        P("rx", None),
        P(("rx", "tb"), None, None),
        P(("rx", "tb"), None),
        P("rx"),
        P(),
        P(None, "rx"),
    )
    return jax.shard_map(
        functools.partial(local, tables()),
        mesh=mesh,
        in_specs=placed,
        out_specs=(P("tb", "rx", None, None), P(None, "rx"), P(None, "rx"), P()),
        check_vma=False,
    )
```

```python
import functools
import math

import jax
import jax.numpy as jnp
import numpy as np
from jax import lax
from jax.experimental import pallas as pl
from jax.experimental.pallas import tpu as pltpu
from jax.sharding import PartitionSpec as P

SEG = 256
DOPPLER_BINS = 32
LAG_COUNT = 1024
WL = 16
WD = 4
GN_MAX = 6
RX = 32
TB = 8
FFT = 512
SAMPLES = SEG * DOPPLER_BINS

MESH = pl.DeviceIdType.MESH
f32 = jnp.float32
bf16 = jnp.bfloat16


def split_pair(table):
    high = table.astype(bf16)
    low = (table - high.astype(np.float64)).astype(bf16)
    return high, low


def tables():
    turn = 2.0 * np.pi / FFT
    t_f = np.arange(SEG)[:, None] * np.arange(FFT)[None, :] % FFT * turn
    forward = np.concatenate([np.cos(t_f), np.sin(t_f)], axis=1)
    backward = np.concatenate([np.cos(t_f.T), np.sin(t_f.T)], axis=1)
    d_m = (
        np.arange(DOPPLER_BINS)[:, None] * np.arange(DOPPLER_BINS)[None, :] % DOPPLER_BINS
    ) * (2.0 * np.pi / DOPPLER_BINS)
    mix = np.block([[np.cos(d_m), np.sin(d_m)], [-np.sin(d_m), np.cos(d_m)]])
    mix = mix.reshape(2, DOPPLER_BINS, -1).transpose(1, 0, 2).reshape(2 * DOPPLER_BINS, -1)
    mix = mix / (FFT * math.sqrt(SAMPLES))
    mix_high, mix_low = split_pair(mix)
    deep_mix = np.concatenate([mix_high, mix_low, mix_high], axis=1)
    deep_forward = np.concatenate(split_pair(forward), axis=0)
    back_high, back_low = split_pair(backward)
    deep_backward = np.concatenate([back_high, back_low], axis=0)
    return deep_forward, deep_backward, deep_mix


def iota(shape, dim):
    return lax.broadcasted_iota(jnp.int32, shape, dim)


def to_column(row, count):
    eye = iota((count, count), 0) == iota((count, count), 1)
    return jnp.sum(jnp.where(eye, row, 0.0), axis=1, keepdims=True)


def peer_lists(r, b):
    rows = [(lax.rem(r + d, RX), b) for d in range(1, RX)]
    blocks = [(r, lax.rem(b + d, TB)) for d in range(1, TB)]
    return rows, blocks


def remote(src, dst, send_sem, recv_sem, peer):
    return pltpu.make_async_remote_copy(
        src_ref=src,
        dst_ref=dst,
        send_sem=send_sem,
        recv_sem=recv_sem,
        device_id={"rx": peer[0], "tb": peer[1]},
        device_id_type=MESH,
    )


def front_kernel(
    raw_in, scl_in, lag_in, dop_in, own_in, em_in, start_in, steps_in,
    fwd_in, back_in, mix_in, rpos_in,
    amb, table, prep, small,
    raw_ref, scl_ref, lag_ref, dop_ref, own_ref, em_ref, start_ref, steps_ref,
    fwd_ref, back_ref, mix_ref,
    rpos_ref, pad_ref, block_ref, raw_all, scl_all, re_ref, im_ref, rr_ref, surf_ref, pay_ref,
    code_tab, code_ref, prep_ref, small_ref, land_ref, wide_ref,
    load_sem, raw_send, raw_recv, scl_send, scl_recv, code_send, code_recv,
    cfwd_send, cfwd_recv, pay_send, pay_recv, fwd_send, fwd_recv, surf_send, surf_recv, own_sem,
):
    r = lax.axis_index("rx")
    b = lax.axis_index("tb")
    barrier = pltpu.get_barrier_semaphore()
    rows, blocks = peer_lists(r, b)

    def signal(peer):
        pl.semaphore_signal(
            barrier, inc=1, device_id={"rx": peer[0], "tb": peer[1]}, device_id_type=MESH
        )

    sources = [
        (lax.rem(r + 2 * b + i, RX), lax.rem(b + d, TB)) for d in range(1, TB) for i in (1, 2)
    ]
    for peer in sources + rows + blocks:
        signal(peer)

    loads = [
        pltpu.make_async_copy(src, dst, load_sem.at[n])
        for n, (src, dst) in enumerate(
            (
                (raw_in, raw_ref), (scl_in, scl_ref), (own_in, own_ref), (em_in, em_ref),
                (start_in, start_ref), (steps_in, steps_ref), (lag_in, lag_ref),
                (dop_in, dop_ref), (fwd_in, fwd_ref), (back_in, back_ref), (mix_in, mix_ref),
            )
        )
    ]
    for copy in loads:
        copy.start()
    rpos_copy = pltpu.make_async_copy(rpos_in, rpos_ref, own_sem.at[2])
    rpos_copy.start()
    for copy in loads[:2]:
        copy.wait()
    own_raw = raw_ref[0].astype(f32)
    block_ref[...] = jnp.concatenate(
        [own_raw[k : k + 1, SEG * s : SEG * s + SEG] for k in range(2) for s in range(4)], axis=0
    ).astype(bf16)
    pad_ref[...] = jnp.zeros((1, 128), f32)
    pad_ref[:, 0:4] = scl_ref[...]


    pl.semaphore_wait(barrier, len(sources) + len(rows) + len(blocks))

    targets = [(r, p, 0) for _, p in blocks]
    targets += [(lax.rem(r + RX - 2 * t - i, RX), t, i) for t in range(TB) for i in (1, 2)]
    for src, dst, ss, rs in (
        (block_ref, raw_all, raw_send, raw_recv),
        (pad_ref, scl_all, scl_send, scl_recv),
    ):
        for to_r, to_b, i in targets:
            remote(src, dst.at[i * TB + b], ss, rs, (to_r, to_b)).start()
    pltpu.make_async_copy(block_ref, raw_all.at[b], raw_recv).start()
    pltpu.make_async_copy(pad_ref, scl_all.at[b], scl_recv).start()
    for copy in loads[2:8]:
        copy.wait()
    owner = jnp.concatenate(
        [to_column(own_ref[c : c + 1, :].astype(f32), 16) for c in range(2)], axis=0
    )
    code = jnp.concatenate(
        [to_column(em_ref[c : c + 1, :].astype(f32), 16) + (1.0 + 4.0 * c) for c in range(2)],
        axis=0,
    )
    p_row = iota((32, 32), 0)
    p_col = iota((32, 32), 1)
    owner_row = jnp.sum(jnp.where(p_row == p_col, owner, 0.0), axis=0, keepdims=True)
    same = (owner_row == owner) & (p_col < p_row)
    rank = jnp.sum(jnp.where(same, 1.0, 0.0), axis=1, keepdims=True)
    lane = iota((32, 128), 1)
    slot = lax.rem(lane, 64).astype(f32)
    placed = (rank * 32.0 + owner) == slot
    first = lane < 64
    codes = jnp.sum(jnp.where(placed & first, code, 0.0), axis=0, keepdims=True)
    lane1 = iota((1, 128), 1)
    for k in range(3):
        for e in range(4):
            codes = jnp.where(lane1 == 64 + 4 * k + e, start_ref[k : k + 1, e : e + 1], codes)
    for e in range(4):
        codes = jnp.where(lane1 == 76 + e, steps_ref[0:1, e : e + 1].astype(f32), codes)
    pay_ref[1] = codes
    pltpu.make_async_copy(pay_ref.at[1], code_tab.at[b, r], code_recv).start()
    for peer in rows:
        remote(pay_ref.at[1], code_tab.at[b, r], code_send, code_recv, peer).start()
    peer = blocks[0]
    remote(raw_all, raw_all, raw_send, raw_recv, peer).wait_recv()
    for copy in loads[8:]:
        copy.wait()

    raw = raw_all[...].astype(f32).reshape(3 * TB * 8, SEG).astype(bf16)
    spec = jnp.dot(raw, fwd_ref[0:256, :], preferred_element_type=f32)
    spec = spec + jnp.dot(raw, fwd_ref[256:512, :], preferred_element_type=f32)
    cos_part = spec[:, :FFT].reshape(3 * TB, 8, FFT)
    sin_part = spec[:, FFT:].reshape(3 * TB, 8, FFT)
    remote(scl_all, scl_all, scl_send, scl_recv, blocks[0]).wait_recv()
    sub = iota((1, 8, 1), 1)
    sign = jnp.where(sub < 4, 1.0, -1.0).astype(f32)
    pick = iota((1, 8, 128), 2) == lax.rem(iota((1, 8, 128), 1), 4)
    scale = jnp.sum(jnp.where(pick, scl_all[...], 0.0), axis=2, keepdims=True)
    pieces = (cos_part + sign * pltpu.roll(sin_part, 4, 1)) * scale
    for i in range(3):
        re_ref[i, 32:40, :] = jnp.zeros((8, FFT), f32)
        im_ref[i, 32:40, :] = jnp.zeros((8, FFT), f32)
        for t in range(TB):
            re_ref[i, 4 * t : 4 * t + 4, :] = pieces[i * TB + t, 0:4, :]
            im_ref[i, 4 * t : 4 * t + 4, :] = pieces[i * TB + t, 4:8, :]
    near_re = re_ref[0, 0:32, :]
    near_im = im_ref[0, 0:32, :]
    alt = jnp.where(lax.rem(iota((1, FFT), 1), 2) == 0, 1.0, -1.0).astype(f32)
    for c in range(2):
        for j in range(4):
            far_re = re_ref[c + 1, j : j + 32, :] + alt * re_ref[c + 1, j + 1 : j + 33, :]
            far_im = im_ref[c + 1, j : j + 32, :] + alt * im_ref[c + 1, j + 1 : j + 33, :]
            row = (c * 4 + j) * 32
            rr_ref[row : row + 32, :] = near_re * far_re + near_im * far_im
            rr_ref[256 + row : 288 + row, :] = near_im * far_re - near_re * far_im
    remote(code_tab.at[b], code_tab.at[b], code_send, code_recv, blocks[0]).wait_recv()
    for peer in blocks:
        remote(code_tab.at[b], code_tab.at[b], cfwd_send, cfwd_recv, peer).start()
    cross = rr_ref[...]
    high = cross.astype(bf16)
    low = (cross - high.astype(f32)).astype(bf16)
    lagged = jnp.dot(high, back_ref[0:512, :], preferred_element_type=f32)
    lagged = lagged + jnp.dot(low, back_ref[0:512, :], preferred_element_type=f32)
    lagged = lagged + jnp.dot(high, back_ref[512:1024, :], preferred_element_type=f32)
    lag_re = lagged[0:256, 0:256] + lagged[256:512, 256:512]
    lag_im = lagged[256:512, 0:256] - lagged[0:256, 256:512]

    lag_rows = lag_ref[pl.ds(2 * b, 2), :].astype(f32)
    dop_rows = dop_ref[pl.ds(2 * b, 2), :].astype(f32)
    tau_cols, nu_cols, surfs = [], [], []
    for c in range(2):
        top = jnp.concatenate(
            [lag_re[(c * 4 + j) * 32 : (c * 4 + j + 1) * 32] for j in range(4)], axis=1
        )
        low_half = jnp.concatenate(
            [lag_im[(c * 4 + j) * 32 : (c * 4 + j + 1) * 32] for j in range(4)], axis=1
        )
        stacked = jnp.concatenate([top, low_half], axis=0)
        high = stacked.astype(bf16)
        low = (stacked - high.astype(f32)).astype(bf16)
        deep = jnp.concatenate([high, high, low], axis=0)
        surf = jnp.dot(mix_ref[...], deep, preferred_element_type=f32)
        surfs.append(surf)
        power = surf * surf
        lag0 = to_column(lag_rows[c : c + 1, :], 16)
        dop0 = to_column(dop_rows[c : c + 1, :], 16)
        offset = (iota((16, 2 * DOPPLER_BINS), 1) // 2).astype(f32) - dop0
        offset = jnp.where(offset < 0.0, offset + DOPPLER_BINS, offset)
        inside = jnp.where(offset < WD, 1.0, 0.0).astype(f32)
        weights = jnp.concatenate([inside, inside * offset], axis=0)
        weights = weights.astype(bf16)
        high = power.astype(bf16)
        low = (power - high.astype(f32)).astype(bf16)
        sums = jnp.dot(
            jnp.concatenate([weights, weights], axis=1),
            jnp.concatenate([high, low], axis=0),
            preferred_element_type=f32,
        )
        step = iota((16, LAG_COUNT), 1).astype(f32) - lag0
        within = (step >= 0.0) & (step < WL)
        plain = jnp.where(within, sums[0:16], 0.0)
        norm = 1.0 / (WL * WD)
        total = jnp.sum(plain, axis=1, keepdims=True) * norm + 1e-06
        lag_mean = jnp.sum(plain * step, axis=1, keepdims=True) * norm / total
        dop_mean = (
            jnp.sum(jnp.where(within, sums[16:32], 0.0), axis=1, keepdims=True) * norm / total
        )
        tau_cols.append((lag0 + lag_mean) * (16.0 / LAG_COUNT))
        nu_cols.append((dop0 + dop_mean) * (4.0 / DOPPLER_BINS))
    tau = jnp.concatenate(tau_cols, axis=0)
    nu = jnp.concatenate(nu_cols, axis=0)
    pay_ref[0] = jnp.sum(
        jnp.where(placed, jnp.where(first, tau, nu), 0.0), axis=0, keepdims=True
    )

    part = r // 8
    pltpu.make_async_copy(pay_ref.at[0], table.at[b, r], pay_recv.at[part]).start()
    for peer in rows:
        remote(pay_ref.at[0], table.at[b, r], pay_send, pay_recv.at[part], peer).start()
    for t in range(TB):
        surf_ref[t] = jnp.concatenate(
            [surfs[0][8 * t : 8 * t + 8], surfs[1][8 * t : 8 * t + 8]], axis=0
        ).astype(bf16)
    pltpu.make_async_copy(surf_ref.at[b], land_ref.at[b], surf_recv).start()
    for peer in blocks:
        remote(surf_ref.at[peer[1]], land_ref.at[b], surf_send, surf_recv, peer).start()
    some = blocks[0]
    near = (raw_all.at[pl.ds(0, 3 * TB - 1)], raw_send), (scl_all.at[pl.ds(0, 3 * TB - 1)], scl_send)
    row_set = code_tab.at[0, pl.ds(0, RX - 1)]
    for ref, sem in near + ((row_set, code_send), (row_set, pay_send)):
        remote(ref, ref, sem, raw_recv, some).wait_send()
    ref = code_tab.at[pl.ds(0, TB - 1)]
    remote(ref, ref, cfwd_send, cfwd_recv, some).wait_recv()
    rpos_copy.wait()
    for k in range(TB):
        for q in range(RX):
            code_ref[k, q : q + 1, :] = code_tab[k, q]
    prepare(code_ref, rpos_ref, prep_ref, small_ref)
    outs = [
        pltpu.make_async_copy(prep_ref, prep, own_sem.at[2]),
        pltpu.make_async_copy(small_ref, small, own_sem.at[3]),
        pltpu.make_async_copy(wide_ref, amb, own_sem.at[4]),
    ]
    outs[0].start()
    outs[1].start()
    for dp in (0, 1, 3, 2):
        there = lax.rem(part + dp, 4)
        chunk = table.at[b, pl.ds(there * 8, 8)]
        remote(chunk, chunk, pay_send, pay_recv.at[there], some).wait_recv()
        for peer in blocks:
            remote(chunk, chunk, fwd_send, fwd_recv, peer).start()
    remote(surf_ref, land_ref, surf_send, surf_recv, some).wait_recv()
    for t in range(TB):
        value = land_ref[t].astype(f32)
        for c in range(2):
            for d in range(4):
                row = 8 * c + 2 * d
                wide_ref[d, 2 * t + c] = value[row : row + 2, :]
    outs[2].start()
    for ref, sem in ((code_tab, cfwd_send), (surf_ref, surf_send)):
        ref = ref.at[pl.ds(0, TB - 1)]
        remote(ref, ref, sem, raw_recv, some).wait_send()
    for copy in outs:
        copy.wait()
    ref = table.at[pl.ds(0, TB - 1)]
    remote(ref, ref, fwd_send, fwd_recv, some).wait()


def front(raw, scl, lag, dop, own, em, start, steps, consts, rpos):
    any_spec = pl.BlockSpec(memory_space=pl.ANY)
    dma = pltpu.SemaphoreType.DMA
    operands = (raw, scl, lag, dop, own, em, start, steps, *consts)
    return pl.pallas_call(
        front_kernel,
        out_shape=(
            pltpu.VMEM((4, 16, 2, LAG_COUNT), f32),
            pltpu.VMEM((TB, RX, 1, 128), f32),
            pltpu.VMEM((PLANES, RX, 128), f32),
            pltpu.VMEM((11, 8, 128), f32),
        ),
        in_specs=[any_spec] * (len(operands) + 1),
        out_specs=(any_spec,) * 4,
        scratch_shapes=[pltpu.VMEM(x.shape, x.dtype) for x in operands]
        + [
            pltpu.VMEM(rpos.shape, f32),
            pltpu.VMEM((1, 128), f32),
            pltpu.VMEM((8, SEG), bf16),
            pltpu.VMEM((3 * TB, 8, SEG), bf16),
            pltpu.VMEM((3 * TB, 1, 128), f32),
            pltpu.VMEM((3, 40, FFT), f32),
            pltpu.VMEM((3, 40, FFT), f32),
            pltpu.VMEM((512, FFT), f32),
            pltpu.VMEM((TB, 16, LAG_COUNT), bf16),
            pltpu.VMEM((2, 1, 128), f32),
            pltpu.VMEM((TB, RX, 1, 128), f32),
            pltpu.VMEM((TB, RX, 128), f32),
            pltpu.VMEM((PLANES, RX, 128), f32),
            pltpu.VMEM((11, 8, 128), f32),
            pltpu.VMEM((TB, 16, LAG_COUNT), bf16),
            pltpu.VMEM((4, 16, 2, LAG_COUNT), f32),
            dma((len(operands),)),
            dma, dma, dma, dma, dma, dma, dma, dma, dma, dma((4,)), dma, dma, dma, dma, dma((5,)),
        ],
        compiler_params=pltpu.CompilerParams(collective_id=0, has_side_effects=True),
        name="front",
    )(*operands, rpos)


def solve_three(normals, rhs, damp_term):
    entry_xx = normals[0] + damp_term
    entry_xy = normals[1]
    entry_xz = normals[2]
    entry_yy = normals[3] + damp_term
    entry_yz = normals[4]
    entry_zz = normals[5] + damp_term
    minor_xx = entry_yy * entry_zz - entry_yz * entry_yz
    minor_xy = entry_xz * entry_yz - entry_xy * entry_zz
    minor_xz = entry_xy * entry_yz - entry_xz * entry_yy
    minor_yy = entry_xx * entry_zz - entry_xz * entry_xz
    minor_yz = entry_xy * entry_xz - entry_xx * entry_yz
    minor_zz = entry_xx * entry_yy - entry_xy * entry_xy
    inverse = 1.0 / (entry_xx * minor_xx + entry_xy * minor_xy + entry_xz * minor_xz)
    step_x = minor_xx * rhs[0] + minor_xy * rhs[1] + minor_xz * rhs[2]
    step_y = minor_xy * rhs[0] + minor_yy * rhs[1] + minor_yz * rhs[2]
    step_z = minor_xz * rhs[0] + minor_yz * rhs[1] + minor_zz * rhs[2]
    return [step_x * inverse, step_y * inverse, step_z * inverse]


def per_receiver(x, shift):
    return pltpu.roll(x, (RX - shift) % RX, 0)


ROW_OF = (0, 4, 2, 6)
OWNER_AT = (0, 0, 2, 2, 1, 1, 3, 3)
FULL = ((0, 1, 2), (1, 3, 4), (2, 4, 5))
PAIRS = ((0, 0), (0, 1), (0, 2), (1, 1), (1, 2), (2, 2))
EMIT, MASK, LIVE, LATE, FIRST, SECOND, SPREAD, JAC, PLANES = 0, 4, 16, 20, 24, 27, 39, 43, 55
START, STEPS, DAMP, NORMAL = 0, 3, 4, 5


def fold(parts):
    total, second, third, fourth = parts
    first = total - second - third - fourth
    sub = iota((8, 128), 0)
    upper = sub < 4
    early = lax.rem(sub, 4) < 2

    def halves(x, y):
        return jnp.where(upper, x, y) + pltpu.roll(jnp.where(upper, y, x), 4, 0)

    one = halves(first, second)
    two = halves(third, fourth)
    rows = jnp.where(early, one + pltpu.roll(one, 6, 0), two + pltpu.roll(two, 2, 0))
    rows = rows + pltpu.roll(rows, 7, 0)
    rows = rows + pltpu.roll(rows, 32, 1)
    return rows + pltpu.roll(rows, 64, 1)


def add_to(acc, key, masks, quantity):
    terms = [quantity] + [mask * quantity for mask in masks]
    old = acc[key]
    acc[key] = terms if old is None else [x + y for x, y in zip(old, terms)]


def spread_rows(rows):
    return [jnp.broadcast_to(rows[at : at + 1], (8, 128)) for at in ROW_OF]


def tile_of(k, h):
    return k, slice(8 * h, 8 * h + 8)


def at_peak(which, rows):
    value = rows[0]
    for is_it, row in zip(which, rows[1:]):
        value = jnp.where(is_it, row, value)
    return value


def tile_ranges(prep_ref, which, position, k, part):
    sq_first = None
    firsts, seconds = [], []
    for comp in range(3):
        at = at_peak(which, position[comp])
        d_first = at - prep_ref[FIRST + comp, part, :]
        d_second = at - prep_ref[SECOND + 4 * comp + k, part, :]
        if sq_first is None:
            sq_first = 1.0 + d_first * d_first
            sq_second = 1.0 + d_second * d_second
        else:
            sq_first = sq_first + d_first * d_first
            sq_second = sq_second + d_second * d_second
        firsts.append(d_first)
        seconds.append(d_second)
    inv_first = lax.rsqrt(sq_first)
    inv_second = lax.rsqrt(sq_second)
    spread = sq_second * inv_second - sq_first * inv_first
    live = prep_ref[LIVE + k, part, :]
    inv_first = inv_first * live
    inv_second = inv_second * live
    return spread, [seconds[i] * inv_second - firsts[i] * inv_first for i in range(3)]


def tile_masks(prep_ref, k, part):
    emit = prep_ref[EMIT + k, part, :]
    which = [emit == float(e) for e in (1, 2, 3)]
    return which, [prep_ref[MASK + 4 * e + k, part, :] for e in range(3)]


def turned_by_slot(x):
    low = iota((RX, 128), 1) < 64
    base = jnp.where(low, x, jnp.concatenate([x[8:], x[:8]], axis=0))
    return [per_receiver(base, shift) for shift in range(1, 9)]


def prepare(code_ref, rpos_ref, prep_ref, small_ref):
    lane = iota((RX, 128), 1)
    low = lane < 64
    own_lane = iota((RX, 128), 0) == lax.rem(lane, RX)
    for k in range(4):
        code = jnp.where(low, code_ref[k], pltpu.roll(code_ref[k + 4], 64, 1))
        late = code > 4.5
        prep_ref[LATE + k] = jnp.where(late, 1.0, 0.0)
        emitter = jnp.where(late, code - 5.0, code - 1.0)
        prep_ref[EMIT + k] = emitter
        prep_ref[LIVE + k] = jnp.where(code > 0.5, 1.0, 0.0)
        for e in range(3):
            prep_ref[MASK + 4 * e + k] = jnp.where(emitter == e + 1.0, 1.0, 0.0)
    info = code_ref[0]

    def owner_row(col):
        value = jnp.sum(jnp.where(lane == col, info, 0.0), axis=1, keepdims=True)
        return jnp.sum(jnp.where(own_lane, value, 0.0), axis=0, keepdims=True)

    def owner_rows(base):
        made = [owner_row(base + e) for e in range(4)]
        return jnp.concatenate([made[e] for e in OWNER_AT], axis=0)

    position = [owner_rows(64 + 4 * k) for k in range(3)]
    for k in range(3):
        small_ref[START + k] = position[k]
    small_ref[STEPS] = owner_rows(76)
    eye = iota((RX, RX), 0) == iota((RX, RX), 1)
    for comp in range(3):
        column = jnp.sum(
            jnp.where(eye, rpos_ref[comp : comp + 1, :], 0.0), axis=1, keepdims=True
        )
        column = jnp.broadcast_to(column, (RX, 128))
        prep_ref[FIRST + comp] = column
        turned = turned_by_slot(column)
        for k in range(4):
            prep_ref[SECOND + 4 * comp + k] = jnp.where(
                prep_ref[LATE + k] > 0.5, turned[2 * k + 1], turned[2 * k]
            )
    acc = {key: None for key in range(7)}
    position = [spread_rows(rows) for rows in position]
    for k, part in [tile_of(k, h) for k in range(4) for h in range(4)]:
        which, masks = tile_masks(prep_ref, k, part)
        spread, jac = tile_ranges(prep_ref, which, position, k, part)
        prep_ref[SPREAD + k, part, :] = spread
        for i in range(3):
            prep_ref[JAC + 4 * i + k, part, :] = jac[i]
        for key, (x, y) in enumerate(PAIRS):
            add_to(acc, key, masks, jac[x] * jac[y])
        add_to(acc, 6, masks, prep_ref[LIVE + k, part, :])
    for key in range(6):
        small_ref[NORMAL + key] = fold(acc[key])
    small_ref[DAMP] = 2.0 * (fold(acc[6]) + 1.0)


def solve_kernel(
    table_ref, prep_ref, small_ref, amb_in, pos_ref, vel_ref, bias_ref, amb_out,
    out_sem, tau_ref, nu_ref, spread_ref, jac_ref, left_ref,
):
    amb_copy = pltpu.make_async_copy(amb_in, amb_out, out_sem.at[0])
    amb_copy.start()
    lane = iota((RX, 128), 1)
    low = lane < 64
    for k in range(4):
        a0, a1 = table_ref[k], table_ref[k + 4]
        tau_ref[k] = jnp.where(low, a0, pltpu.roll(a1, 64, 1))
        nu_ref[k] = jnp.where(low, pltpu.roll(a0, 64, 1), a1)
        spread_ref[k] = prep_ref[SPREAD + k]
        for i in range(3):
            jac_ref[i, k] = prep_ref[JAC + 4 * i + k]
    position = [small_ref[START + k] for k in range(3)]
    normals = [small_ref[NORMAL + key] for key in range(6)]
    zero = jnp.zeros((8, 128), f32)
    tiles = [tile_of(k, h) for k in range(4) for h in range(4)]

    def gn_step(step, carry):
        position, speed, bias, normals = carry
        moving = step.astype(f32) < small_ref[STEPS]
        damp = small_ref[DAMP]
        turned = turned_by_slot(bias)
        acc = {key: None for key in range(3)}
        for k in range(4):
            late = prep_ref[LATE + k] > 0.5
            left_ref[k] = tau_ref[k] + bias - jnp.where(late, turned[2 * k + 1], turned[2 * k])
        for k, part in tiles:
            masks = [prep_ref[MASK + 4 * e + k, part, :] for e in range(3)]
            resid = left_ref[k, part, :] - spread_ref[k, part, :]
            for i in range(3):
                add_to(acc, i, masks, jac_ref[i, k, part, :] * resid)
        moved = solve_three(normals, [fold(acc[i]) for i in range(3)], damp)
        position = [position[i] + jnp.where(moving, moved[i], 0.0) for i in range(3)]
        at_rows = [spread_rows(rows) for rows in position]
        acc = {key: None for key in range(9)}
        for k, part in tiles:
            which, masks = tile_masks(prep_ref, k, part)
            spread, jac = tile_ranges(prep_ref, which, at_rows, k, part)
            spread_ref[k, part, :] = spread
            for i in range(3):
                jac_ref[i, k, part, :] = jac[i]
            rate = nu_ref[k, part, :]
            for key, (x, y) in enumerate(PAIRS):
                add_to(acc, key, masks, jac[x] * jac[y])
            for i in range(3):
                add_to(acc, 6 + i, masks, jac[i] * rate)
        nested, whole = None, None
        for k in (3, 2, 1, 0):
            gap = left_ref[k] - spread_ref[k]
            every = prep_ref[LIVE + k] * gap
            late = prep_ref[LATE + k] * gap
            term = every - late + pltpu.roll(late, 1, 0)
            nested = term if nested is None else term + pltpu.roll(nested, 2, 0)
            whole = every if whole is None else whole + every
        nested = pltpu.roll(nested, 1, 0)
        shifted = jnp.concatenate([nested[24:], nested[:24]], axis=0)
        total = jnp.sum(jnp.where(low, nested, shifted) - whole, axis=1, keepdims=True)
        normals = [fold(acc[key]) for key in range(6)]
        swung = solve_three(
            normals,
            [
                fold(acc[6 + i])
                - (
                    normals[FULL[i][0]] * speed[0]
                    + normals[FULL[i][1]] * speed[1]
                    + normals[FULL[i][2]] * speed[2]
                )
                for i in range(3)
            ],
            damp,
        )
        speed = [speed[i] + jnp.where(moving, swung[i], 0.0) for i in range(3)]
        bias = bias + jnp.broadcast_to(total, (RX, 128)) / (3.0 * 16 * RX)
        return position, speed, bias, normals

    carry = (position, [zero, zero, zero], jnp.zeros((RX, 128), f32), normals)
    position, speed, bias, _ = lax.fori_loop(0, GN_MAX, gn_step, carry)
    r = lax.axis_index("rx")
    lane8 = iota((8, 128), 1)
    sub8 = iota((8, 128), 0)
    spot = lax.rem(sub8, 4) + jnp.where(sub8 >= 4, 1, 0)
    used = (lax.rem(sub8, 2) == 0) & (lane8 == spot)
    for out, value in ((pos_ref, position), (vel_ref, speed)):
        for i in range(3):
            column = jnp.sum(jnp.where(lane8 == r, value[i], 0.0), axis=1, keepdims=True)
            row = jnp.sum(jnp.where(used, column, 0.0), axis=0, keepdims=True)
            out[i : i + 1, :] = row[:, 0:4]
    bias_row = jnp.sum(jnp.where(iota((RX, 128), 0) == lane, bias, 0.0), axis=0, keepdims=True)
    bias_ref[...] = bias_row[:, 0:RX]
    amb_copy.wait()


def solve(table, prep, small, amb):
    any_spec = pl.BlockSpec(memory_space=pl.ANY)
    vmem = pl.BlockSpec(memory_space=pltpu.VMEM)
    block = (4, RX, 128)
    return pl.pallas_call(
        solve_kernel,
        out_shape=(
            jax.ShapeDtypeStruct((3, 4), f32),
            jax.ShapeDtypeStruct((3, 4), f32),
            jax.ShapeDtypeStruct((1, RX), f32),
            jax.ShapeDtypeStruct((4, 16, 2, LAG_COUNT), f32),
        ),
        in_specs=[vmem, vmem, vmem, any_spec],
        out_specs=(vmem, vmem, vmem, any_spec),
        scratch_shapes=[
            pltpu.SemaphoreType.DMA((1,)),
            pltpu.VMEM(block, f32),
            pltpu.VMEM(block, f32),
            pltpu.VMEM(block, f32),
            pltpu.VMEM((3,) + block, f32),
            pltpu.VMEM(block, f32),
        ],
        compiler_params=pltpu.CompilerParams(vmem_limit_bytes=12 << 20),
        name="solve",
    )(table, prep, small, amb)


def local(
    consts, raw_samples, block_scales, lag_window_start, doppler_window_start,
    peak_owner, peak_emitter, gn_steps, receiver_pos, emitter_start,
):
    amb, table, prep, small = front(
        raw_samples, block_scales, lag_window_start, doppler_window_start,
        peak_owner.reshape(2, 16), peak_emitter, emitter_start, gn_steps.reshape(1, 4), consts,
        receiver_pos,
    )
    position, speed, bias, amb = solve(
        table.reshape(TB, RX, 128), prep, small, amb
    )
    return amb, position, speed, bias.reshape(RX)


def solution(mesh):
    placed = (
        P("rx", None, "tb"),
        P("rx", "tb"),
        P("rx", None),
        P("rx", None),
        P(("rx", "tb"), None, None),
        P(("rx", "tb"), None),
        P("rx"),
        P(),
        P(None, "rx"),
    )
    return jax.shard_map(
        functools.partial(local, tables()),
        mesh=mesh,
        in_specs=placed,
        out_specs=(P("tb", "rx", None, None), P(None, "rx"), P(None, "rx"), P()),
        check_vma=False,
    )
```
